32 devices in a mesh: dp: 8 (over z, x), tensor: 4 (over y, core).
Axes of the slice: x: 2, y: 2, z: 4, core: 2. Of those that a mesh axis runs over, the one named last changes fastest.
Arguments:
- tokens: bfloat16 [24, 512, 768], P('dp', None, 'tensor'), may hold values from -6 to 6
- cotangent: bfloat16 [24, 512, 768], P('dp', None, 'tensor'), may hold values from -6 to 6
- prev_logits: bfloat16 [24, 12, 512, 512], P('dp', 'tensor'), may hold values from -6 to 6
- segment_ids: int32 [24, 512], P('dp'), may hold values from 0 to 5, never falling along the last dimension, each value on 1 to 256 neighbouring positions
- w_qkv: float32 [768, 3, 768], P('dp', None, 'tensor'), may hold values from -0.21875 to 0.21875
- b_qv: float32 [2, 768], P(None, 'tensor'), may hold values from -3 to 3
- w_out: float32 [768, 768], P('tensor', 'dp'), may hold values from -0.625 to 0.625
- w_up: float32 [768, 3072], P('dp', 'tensor'), may hold values from -0.21875 to 0.21875
- b_up: float32 [3072], P('tensor'), may hold values from -3 to 3
- w_down: float32 [3072, 768], P('tensor', 'dp'), may hold values from -0.109375 to 0.109375
- biases: float32 [2, 768], replicated, may hold values from -3 to 3
- gains: float32 [2, 768], replicated, may hold values from 0.25 to 1.75
- shifts: float32 [2, 768], replicated, may hold values from -3 to 3
Outputs:
- activations: bfloat16 [24, 512, 768], P('dp', None, 'tensor')
- raw_logits: bfloat16 [24, 12, 512, 512], P('dp', 'tensor')
- input_grad: bfloat16 [24, 512, 768], P('dp', None, 'tensor')
- logits_grad: bfloat16 [24, 12, 512, 512], P('dp', 'tensor')
- grad_qkv: float32 [768, 3, 768], P(None, None, 'tensor')
- grad_b_qv: float32 [2, 768], P(None, 'tensor')
- grad_out: float32 [768, 768], P('tensor')
- grad_up: float32 [768, 3072], P(None, 'tensor')
- grad_b_up: float32 [3072], P('tensor')
- grad_down: float32 [3072, 768], P('tensor')
- grad_biases: float32 [2, 768], replicated
- grad_gains: float32 [2, 768], replicated
- grad_shifts: float32 [2, 768], replicated
The draws below stay inside these ranges and needn't reach their ends.
Inputs may be any that keep to these rules, and one draw needn't show every extreme that they name: `segment_ids`: in each row the segment number never falls; each segment has 1 to 256 slots and one has exactly that many; a query attends only to keys of its own segment.
All inputs are finite; a program needn't handle non-finite values.
Results may differ from the reference program's by a relative error of at most 0.02.
Values may be sent and summed in bfloat16 or wider, within the bound.
No kernel may reach another device: no remote copies, remote signals or barrier semaphores. Data moves between devices by JAX's collectives and lax.ppermute only.
A program may use at most 192 MiB of HBM per device.

```python
import math
import jax
import jax.numpy as jnp
import numpy as np
from jax import lax

D = 768
HEADS = 12
HEAD = 64
FF = 3072
SLOTS = 512
SEGS = 6
ROWS_DEV = 3
ROWS = 24


def level_of(stream_key, dims, shards, smallest, top_value):
    loudness, own = 1.0, jax.random.fold_in(stream_key, 6)
    for position, parts in shards:
        draws = jnp.exp(jax.random.uniform(jax.random.fold_in(own, position), (parts,), jnp.float32, smallest / len(shards), top_value / len(shards)))
        loudness = loudness * jnp.repeat(draws, dims[position] // parts).reshape([-1 if axis == position else 1 for axis in range(len(dims))])
    return loudness


def profile(number_of, total, limit, lean):
    loads = [(1 << 20) // math.isqrt(standing ** lean) + 1 for standing in range(2, number_of + 1)]
    rest, given = total - limit - (number_of - 1), [1] * (number_of - 1)
    while rest > 0:
        movable = [i for i in range(number_of - 1) if given[i] < limit]
        mass, budget = sum([loads[i] for i in movable]), rest
        for i in movable:
            addition = min(limit - given[i], max(1, budget * loads[i] // mass), rest)
            given[i] = given[i] + addition
            rest = rest - addition
    return np.array([limit] + given)


def ragged_sizes(own_key, amount, total, limit, skew):
    if amount == 2:
        one = jax.random.randint(own_key, (), max(1, total - limit), min(limit, total - 1) + 1)
        return jnp.stack([one, total - one])
    lengths = jnp.asarray(profile(amount, total, limit, skew), jnp.int32)
    couples = (amount - 1) // 2
    giver, sink = lengths[1:1 + 2 * couples:2], lengths[2:2 + 2 * couples:2]
    slack = jnp.minimum(giver - 1, limit - sink)
    moved = jax.random.randint(jax.random.fold_in(own_key, 1), (couples,), 0, 1 << 20) % (slack + 1)
    lengths = lengths.at[1:1 + 2 * couples:2].set(giver - moved).at[2:2 + 2 * couples:2].set(sink + moved)
    return lengths[jax.random.permutation(jax.random.fold_in(own_key, 2), amount)]


def centred(rng, shape, width, bound, shards=(), kind=jnp.bfloat16):
    factor_of = level_of(rng, shape, shards, -0.22, 0.18) if shards else 1.0
    values = jax.random.normal(rng, shape, jnp.float32) * width * factor_of
    return jnp.minimum(jnp.maximum(values, -bound), bound).astype(kind)


def setup_inputs(seed: int = 0) -> dict:
    keys = jax.random.split(jax.random.key(seed), 14)
    tokens = centred(keys[0], (ROWS, SLOTS, D), 1.0, 6.0, ((0, 8), (2, 4)))
    cotangent = centred(keys[1], (ROWS, SLOTS, D), 1.0, 6.0, ((0, 8), (2, 4)))
    prev_logits = centred(keys[2], (ROWS, HEADS, SLOTS, SLOTS), 1.5, 6.0, ((0, 8), (1, 4)))
    segment_ids = jax.vmap(lambda own: jnp.searchsorted(jnp.cumsum(ragged_sizes(own, SEGS, SLOTS, SLOTS // 2, 1)), jnp.arange(SLOTS), side="right"))(jax.random.split(keys[3], ROWS)).reshape((ROWS, SLOTS)).astype(jnp.int32)
    w_qkv = centred(keys[4], (D, 3, D), D ** -0.5, 0.21875, ((0, 8), (2, 4)), jnp.float32)
    b_qv = centred(keys[5], (2, D), 0.5, 3.0, ((1, 4),), jnp.float32)
    w_out = centred(keys[6], (D, D), (D // 8) ** -0.5, 0.625, ((0, 4), (1, 8)), jnp.float32)
    w_up = centred(keys[7], (D, FF), D ** -0.5, 0.21875, ((0, 8), (1, 4)), jnp.float32)
    b_up = centred(keys[8], (FF,), 0.5, 3.0, ((0, 4),), jnp.float32)
    w_down = centred(keys[9], (FF, D), FF ** -0.5, 0.109375, ((0, 4), (1, 8)), jnp.float32)
    biases = centred(keys[10], (2, D), 0.5, 3.0, (), jnp.float32)
    gains = jnp.clip(1.0 + 0.15 * jax.random.normal(keys[11], (2, D), jnp.float32), 0.25, 1.75)
    shifts = centred(keys[12], (2, D), 0.5, 3.0, (), jnp.float32)
    return {"tokens": tokens, "cotangent": cotangent, "prev_logits": prev_logits, "segment_ids": segment_ids, "w_qkv": w_qkv, "b_qv": b_qv, "w_out": w_out, "w_up": w_up, "b_up": b_up, "w_down": w_down, "biases": biases, "gains": gains, "shifts": shifts}


EPS = 1e-06
NEG = -1e+30
HIGHEST_PRECISION = lax.Precision.HIGHEST

@jax.custom_vjp
def low(v):
    return lax.optimization_barrier(v.astype(jnp.bfloat16)).astype(jnp.float32)

@jax.custom_vjp
def low_back(v):
    return v

def low_keep(v):
    return (low(v), None)

def low_pass(kept, grad):
    return (grad,)

def back_keep(v):
    return (v, None)

def back_low(kept, grad):
    return (low(grad),)
low.defvjp(low_keep, low_pass)
low_back.defvjp(back_keep, back_low)

def layer_norm(summed, gain_row, shift_row):
    row_mean = lax.optimization_barrier(jnp.mean(summed, axis=-1, keepdims=True))
    centered = summed - row_mean
    inv_std = lax.rsqrt(lax.optimization_barrier(jnp.mean(centered * centered, axis=-1, keepdims=True)) + EPS)
    return centered * inv_std * gain_row + shift_row

def forward(inputs, previous, allowed, w_qkv, b_qv, w_out, w_up, b_up, w_down, biases, gains, shifts):
    group_rows = inputs.shape[0]
    projected = low_back(jnp.einsum('gsd,dcf->gscf', inputs, low(w_qkv), precision=HIGHEST_PRECISION))
    qkv_bias = jnp.stack([b_qv[0], jnp.zeros_like(b_qv[0]), b_qv[1]])
    qkv_all = low(projected + qkv_bias).reshape(group_rows, SLOTS, 3, HEADS, HEAD)
    inv_root = 1.0 / math.sqrt(HEAD)
    scores = jnp.einsum('gqhe,gkhe->ghqk', qkv_all[:, :, 0], qkv_all[:, :, 1], precision=HIGHEST_PRECISION) * inv_root + previous
    rounded_scores = low_back(scores)
    masked = jnp.where(allowed[:, None], rounded_scores, NEG)
    probability = low(jax.nn.softmax(masked, axis=-1))
    attended = jnp.einsum('ghqk,gkhe->gqhe', probability, qkv_all[:, :, 2], precision=HIGHEST_PRECISION)
    attended = low_back(low(attended)).reshape(group_rows, SLOTS, D)
    branch = low_back(jnp.einsum('gsf,fd->gsd', attended, low(w_out), precision=HIGHEST_PRECISION))
    first_out = layer_norm(inputs + branch + biases[0], gains[0], shifts[0])
    hidden = low_back(jnp.einsum('gsd,df->gsf', low(first_out), low(w_up), precision=HIGHEST_PRECISION)) + b_up
    activated = low(jax.nn.gelu(hidden, approximate=False))
    ffn_out = low_back(jnp.einsum('gsf,fd->gsd', activated, low(w_down), precision=HIGHEST_PRECISION))
    return (layer_norm(first_out + ffn_out + biases[1], gains[1], shifts[1]), scores)

def reference(tokens, cotangent, prev_logits, segment_ids, w_qkv, b_qv, w_out, w_up, b_up, w_down, biases, gains, shifts):
    params = (w_qkv, b_qv, w_out, w_up, b_up, w_down, biases, gains, shifts)
    group_count = tokens.shape[0] // ROWS_DEV

    def split_rows(array):
        return array.reshape((group_count, ROWS_DEV) + array.shape[1:])

    def one_group(carry, group_item):
        inputs, previous, segment, grad_final = group_item
        allowed = segment[:, :, None] == segment[:, None, :]

        def local_forward(inputs_f, previous_f, *weights):
            return forward(inputs_f, previous_f, allowed, *weights)
        output, pull_back, scores = jax.vjp(local_forward, inputs.astype(jnp.float32), previous.astype(jnp.float32), *params, has_aux=True)
        grads = pull_back(grad_final.astype(jnp.float32))
        carry = tuple((summed_grad + new_grad for summed_grad, new_grad in zip(carry, grads[2:])))
        return (carry, (output.astype(jnp.bfloat16), scores.astype(jnp.bfloat16), grads[0].astype(jnp.bfloat16), grads[1].astype(jnp.bfloat16)))
    initial = tuple((jnp.zeros(weight_array.shape, jnp.float32) for weight_array in params))
    totals, stacked = lax.scan(one_group, initial, (split_rows(tokens), split_rows(prev_logits), split_rows(segment_ids), split_rows(cotangent)))
    activations = stacked[0].reshape(tokens.shape)
    raw_logits = stacked[1].reshape(prev_logits.shape)
    input_grad = stacked[2].reshape(tokens.shape)
    logits_grad = stacked[3].reshape(prev_logits.shape)
    return (activations, raw_logits, input_grad, logits_grad, totals[0], totals[1], totals[2], totals[3], totals[4], totals[5], totals[6], totals[7], totals[8])
```

```python
import functools

import jax
import jax.numpy as jnp
from jax import lax
from jax.experimental import pallas as pl
from jax.experimental.pallas import tpu as pltpu
from jax.sharding import PartitionSpec as P

EPS = 1e-06
NEG = -1e30
BF = jnp.bfloat16
F32 = jnp.float32
CHUNKS = ((0, 3),)
VMEM_LIMIT = 48 * 1024 * 1024


def dot(a, b):
    return lax.dot_general(a, b, (((1,), (0,)), ((), ())), preferred_element_type=F32)


def dot_nt(a, b):
    return lax.dot_general(a, b, (((1,), (1,)), ((), ())), preferred_element_type=F32)


def dot_tn(a, b):
    return lax.dot_general(a, b, (((0,), (0,)), ((), ())), preferred_element_type=F32)


def place_of(me, step):
    core, chip = lax.rem(me, 2), me // 2
    core = 1 - core if step % 2 else core
    chip = 1 - chip if step // 2 else chip
    return 2 * chip + core


def ln_stats(summed):
    row_mean = jnp.mean(summed, axis=-1, keepdims=True)
    centered = summed - row_mean
    inv_std = lax.rsqrt(jnp.mean(centered * centered, axis=-1, keepdims=True) + EPS)
    return centered * inv_std, inv_std


def ln_back(grad, normed, inv_std, gain):
    scaled = grad * gain
    inner = (
        scaled
        - jnp.mean(scaled, axis=-1, keepdims=True)
        - normed * jnp.mean(scaled * normed, axis=-1, keepdims=True)
    )
    return inner * inv_std


def attend_kernel(
    first, heads, aliased, me_ref, x0, x1, x2, x3, w_ref, b_ref, prev_ref, seg_ref, *rest
):
    if aliased:
        rest = rest[1:]
    raw_ref, p_ref, qkv_ref, own_ref, oth_ref, xt_ref, xh_ref, o_scr = rest
    me = me_ref[0]
    core = lax.rem(me, 2)
    width, slots = x0.shape[1], x0.shape[2]
    half = slots // 2
    size = width // heads
    for step, piece in enumerate((x0, x1, x2, x3)):
        start = pl.multiple_of(place_of(me, step) * width, width)
        xt_ref[0, pl.ds(start, width), :] = piece[0]
    bias = jnp.transpose(jnp.broadcast_to(b_ref[0:1, :], (128, width)))[:, 0:1]
    bias_v = jnp.transpose(jnp.broadcast_to(b_ref[1:2, :], (128, width)))[:, 0:1]
    packed = dot_tn(w_ref[:, : 3 * width], xt_ref[0])
    qkv_ref[0, 0] = (packed[:width] + bias).astype(BF)
    qkv_ref[0, 1] = packed[width : 2 * width].astype(BF)
    qkv_ref[0, 2] = (packed[2 * width :] + bias_v).astype(BF)
    mine = pl.ds(pl.multiple_of(core * half, half), half)
    other = pl.ds(pl.multiple_of((1 - core) * half, half), half)
    xh_ref[0] = jnp.transpose(xt_ref[0, :, mine])
    row = seg_ref[pl.ds(first + pl.program_id(0), 1), :].astype(F32)
    column = jnp.transpose(jnp.broadcast_to(row, (128, slots)))[:, 0:1]
    scale = 1.0 / (size**0.5)
    for block in range(2):
        rows = slice(block * half, (block + 1) * half)
        allowed = column[rows] == row
        for h in range(heads):
            feats = slice(h * size, (h + 1) * size)
            scores = dot_tn(qkv_ref[0, 0, feats, rows], qkv_ref[0, 1, feats, :]) * scale
            scores = scores + prev_ref[0, h, rows, :].astype(F32)
            raw_ref[0, h, rows, :] = scores.astype(BF)
            masked = jnp.where(allowed, scores, NEG)
            expanded = jnp.exp(masked - jnp.max(masked, axis=-1, keepdims=True))
            prob = expanded * (1.0 / jnp.sum(expanded, axis=-1, keepdims=True))
            prob = prob.astype(BF)
            p_ref[0, h, rows, :] = prob
            o_scr[feats, rows] = dot_nt(qkv_ref[0, 2, feats, :], prob).astype(BF)
    own_ref[0] = o_scr[:, mine]
    oth_ref[0] = o_scr[:, other]


def up_kernel(
    me_ref, o0, o1, o2, o3, wo0, wo1, wo2, wo3, big_a, big_b, xh_ref, bias_ref, gain_ref, shift_ref,
    b_up_a, b_up_b,
    n1_ref, r1_ref, x1_ref, ga_ref, gb_ref, gp_ref, part_ref,
):
    units = b_up_a.shape[1]
    w1a, w1b = big_a.at[:, :units], big_b.at[:, :units]
    w2a, w2b = big_a.at[:, units : 2 * units], big_b.at[:, units : 2 * units]
    total = xh_ref[0].astype(F32) + bias_ref[0:1, :]
    for left, right in ((o0, wo0), (o1, wo1), (o2, wo2), (o3, wo3)):
        total = total + dot_nt(jnp.transpose(left[0]), right[...])
    normed, inv_std = ln_stats(total)
    n1_ref[0] = normed
    r1_ref[0] = jnp.broadcast_to(inv_std, r1_ref.shape[1:])
    x1_ref[0] = (normed * gain_ref[0:1, :] + shift_ref[0:1, :]).astype(BF)
    block = 256
    for index, (w1, b_up, g_ref) in enumerate(((w1a, b_up_a, ga_ref), (w1b, b_up_b, gb_ref))):
        for start in range(0, units, block):
            hidden = dot(x1_ref[0], w1[:, start : start + block]) + b_up[:, start : start + block]
            cdf = 0.5 * (1.0 + lax.erf(hidden * (0.5**0.5)))
            pdf = jnp.exp(-0.5 * hidden * hidden) * 0.3989422804014327
            g_ref[0, :, start : start + block] = (hidden * cdf).astype(BF)
            lanes = slice(index * units + start, index * units + start + block)
            gp_ref[0, :, lanes] = (cdf + hidden * pdf).astype(BF)
    part_ref[0] = (dot_nt(ga_ref[0], w2a[...]) + dot_nt(gb_ref[0], w2b[...])).astype(BF)


def down_kernel(
    me_ref, n1_ref, pa_ref, pb_ref, dy0, dy1, dy2, dy3, bias_ref, gain_ref, shift_ref,
    big_a, big_b, gp_ref,
    act_own_ref, act_oth_ref, ds_ref, dsb_ref, da_ref, db_ref, part_ref, vec_ref, bup_ref,
    scr,
):
    me = me_ref[0]
    width = dy0.shape[1]
    units = gp_ref.shape[2] // 2
    w1a, w1b = big_a.at[:, :units], big_b.at[:, :units]
    w2a, w2b = big_a.at[:, units : 2 * units], big_b.at[:, units : 2 * units]
    branch = pa_ref[0].astype(F32) + pb_ref[0].astype(F32)
    first_out = n1_ref[0] * gain_ref[0:1, :] + shift_ref[0:1, :]
    normed, inv_std = ln_stats(first_out + branch + bias_ref[1:2, :])
    gain = gain_ref[1:2, :]
    scr[...] = jnp.transpose(normed * gain + shift_ref[1:2, :])
    for step, out in ((0, act_own_ref), (1, act_oth_ref)):
        start = pl.multiple_of(place_of(me, step) * width, width)
        out[0] = scr[pl.ds(start, width), :].astype(BF)
    for step, piece in enumerate((dy0, dy1, dy2, dy3)):
        start = pl.multiple_of(place_of(me, step) * width, width)
        scr[pl.ds(start, width), :] = piece[0].astype(F32)
    grad = jnp.transpose(scr[...])
    inner = ln_back(grad, normed, inv_std, gain)
    ds_ref[0] = inner
    vec_ref[0, 0:1, :] = jnp.sum(grad * normed, axis=0, keepdims=True)
    vec_ref[0, 1:2, :] = jnp.sum(grad, axis=0, keepdims=True)
    vec_ref[0, 2:3, :] = jnp.sum(inner, axis=0, keepdims=True)
    dsb_ref[0] = inner.astype(BF)
    block = 256
    for index, (w2, dh_ref) in enumerate(((w2a, da_ref), (w2b, db_ref))):
        for start in range(0, units, block):
            lanes = slice(index * units + start, index * units + start + block)
            grad_hidden = dot(dsb_ref[0], w2[:, start : start + block]) * gp_ref[
                0, :, lanes
            ].astype(F32)
            bup_ref[0, 0:1, lanes] = jnp.sum(grad_hidden, axis=0, keepdims=True)
            dh_ref[0, :, start : start + block] = grad_hidden.astype(BF)
    part_ref[0] = (dot_nt(da_ref[0], w1a[...]) + dot_nt(db_ref[0], w1b[...])).astype(BF)


def mid_kernel(
    me_ref, ds_ref, pa_ref, pb_ref, n1_ref, r1_ref, gain_ref, wo0, wo1,
    dsb_ref, near_ref, do_own_ref, do_oth_ref, vec_ref, scr,
):
    chip = me_ref[0] // 2
    width = do_own_ref.shape[1]
    grad = ds_ref[0] + (pa_ref[0].astype(F32) + pb_ref[0].astype(F32))
    normed = n1_ref[0]
    inner = ln_back(grad, normed, r1_ref[0, :, 0:1], gain_ref[0:1, :])
    vec_ref[0, 0:1, :] = jnp.sum(grad * normed, axis=0, keepdims=True)
    vec_ref[0, 1:2, :] = jnp.sum(grad, axis=0, keepdims=True)
    vec_ref[0, 2:3, :] = jnp.sum(inner, axis=0, keepdims=True)
    dsb = inner.astype(BF)
    dsb_ref[0] = dsb
    scr[...] = inner
    chip_lanes = pl.ds(pl.multiple_of(chip * 2 * width, 128), 2 * width)
    near_ref[0] = jnp.transpose(scr[:, chip_lanes])
    do_own_ref[0] = jnp.transpose(dot(dsb, wo0[...])).astype(BF)
    do_oth_ref[0] = jnp.transpose(dot(dsb, wo1[...])).astype(BF)


def back_kernel(
    heads, aliased, me_ref, p_ref, qkv_ref, do_own_ref, do_oth_ref, w_ref, near_ref, *rest
):
    if aliased:
        rest = rest[1:]
    lg_ref, dqkv_ref, e0, e1, e2, e3, vec_ref, do_scr, dx_scr = rest
    me = me_ref[0]
    core, chip = lax.rem(me, 2), me // 2
    width, slots = qkv_ref.shape[2], qkv_ref.shape[3]
    half = slots // 2
    size = width // heads
    mine = pl.ds(pl.multiple_of(core * half, half), half)
    other = pl.ds(pl.multiple_of((1 - core) * half, half), half)
    do_scr[:, mine] = do_own_ref[0]
    do_scr[:, other] = do_oth_ref[0]
    scale = 1.0 / (size**0.5)
    for h in range(heads):
        feats = slice(h * size, (h + 1) * size)
        query, key, value = (qkv_ref[0, part, feats, :] for part in range(3))
        out_grad = do_scr[feats, :]
        for block in range(2):
            rows = slice(block * half, (block + 1) * half)
            prob = p_ref[0, h, rows, :].astype(F32)
            grad_prob = dot_tn(do_scr[feats, rows], value)
            weighted = grad_prob * prob
            inner = jnp.sum(weighted, axis=-1, keepdims=True)
            lg_ref[0, h, rows, :] = (weighted - prob * inner).astype(BF)
        grad_query = dot_nt(key, lg_ref[0, h]) * scale
        grad_key = dot(query, lg_ref[0, h]) * scale
        grad_value = dot(out_grad, p_ref[0, h])
        vec_ref[0, feats, 0:1] = jnp.sum(grad_query, axis=1, keepdims=True)
        vec_ref[0, feats, 1:2] = jnp.sum(grad_value, axis=1, keepdims=True)
        dqkv_ref[0, pl.ds(h * size, size), :] = grad_query.astype(BF)
        dqkv_ref[0, pl.ds(width + h * size, size), :] = grad_key.astype(BF)
        dqkv_ref[0, pl.ds(2 * width + h * size, size), :] = grad_value.astype(BF)
    dx_scr[...] = dot(w_ref[:, : 3 * width], dqkv_ref[0])
    near = pl.ds(pl.multiple_of(chip * 2 * width, width), 2 * width)
    dx_scr[near, mine] = dx_scr[near, mine] + near_ref[0]
    for step, out in enumerate((e0, e1, e2, e3)):
        start = pl.multiple_of(place_of(me, step) * width, width)
        out[0] = dx_scr[pl.ds(start, width), :].astype(BF)


def ffn_grad_kernel(count, split, me_ref, *rest):
    lefts, rights = rest[:count], rest[count : 2 * count]
    keep_ref, send_ref, scr = rest[2 * count :]
    side = me_ref[1]
    total = None
    for left, right in zip(lefts, rights):
        a = left[...].reshape(-1, left.shape[-1])
        b = right[...].reshape(-1, right.shape[-1])
        product = dot_tn(a, b)
        total = product if total is None else total + product
    part = keep_ref.shape[0]
    scr[...] = total
    keep_ref[...] = scr[pl.ds(pl.multiple_of(side * part, part), part), :].astype(BF)
    send_ref[...] = scr[pl.ds(pl.multiple_of((1 - side) * part, part), part), :].astype(BF)


def qkv_grad_kernel(count, me_ref, *rest):
    groups = [rest[i * count : (i + 1) * count] for i in range(6)]
    keep_ref, send_ref, scr = rest[6 * count :]
    side = me_ref[1]
    total = None
    for x, grad in zip(groups[0], groups[1]):
        for index in range(grad.shape[0]):
            product = dot_nt(grad[index], x[index])
            total = product if total is None else total + product
    used = total.shape[0]
    scr[:used, :] = total
    total = None
    for lefts, rights in ((groups[2], groups[3]), (groups[4], groups[5])):
        for left, right in zip(lefts, rights):
            for index in range(left.shape[0]):
                product = dot(left[index], right[index])
                total = product if total is None else total + product
    scr[used:, :] = total
    part = scr.shape[0] // 2
    keep_ref[...] = scr[pl.ds(pl.multiple_of(side * part, part), part), :].astype(BF)
    send_ref[...] = scr[pl.ds(pl.multiple_of((1 - side) * part, part), part), :].astype(BF)


def fold_kernel(me_ref, keep_ref, got_ref, *outs):
    depth = me_ref[2]
    rows = outs[0].shape[0]
    count = len(outs)
    for step, out in enumerate(outs):
        start = pl.multiple_of(lax.rem(depth + step, count) * rows, rows)
        total = keep_ref[pl.ds(start, rows), :].astype(F32) + got_ref[pl.ds(start, rows), :].astype(F32)
        out[...] = total.astype(BF)


def finish_kernel(steps, pair, me_ref, *rest):
    count = len(steps)
    blocks, outs = rest[:count], rest[count:]
    here = ring_place(me_ref[3], count)
    rows = blocks[0].shape[0]
    for number, back in enumerate(steps):
        there = lax.rem(here + count - back, count)
        index = jnp.where(there < count // 2, there, (count - 1 - there) + count // 2)
        if pair:
            part = rows // 2
            place = pl.ds(pl.multiple_of(index * part, part), part)
            outs[0][place, :] = blocks[number][:part, :].astype(F32)
            outs[1][place, :] = blocks[number][part:, :].astype(F32)
            continue
        block = blocks[number][...].astype(F32)
        before = 0
        for out in outs:
            held = out.shape[0] // rows

            @pl.when((index >= before) & (index < before + held))
            def _():
                out[pl.ds(pl.multiple_of((index - before) * rows, rows), rows), :] = block

            before += held


def ring_place(group, groups):
    return jnp.where(lax.rem(group, 2) == 0, group // 2, groups - 1 - group // 2)


def gather_kernel(cuts, steps, me_ref, *rest):
    count = len(steps)
    blocks, outs, sems = rest[:count], rest[count:-1], rest[-1]
    here = ring_place(me_ref[3], count)
    rows = blocks[0].shape[0]
    copies = []
    for number, back in enumerate(steps):
        there = lax.rem(here + count - back, count)
        group = jnp.where(there < count // 2, 2 * there, 2 * (count - 1 - there) + 1)
        place = pl.ds(pl.multiple_of(group * rows, rows), rows)
        for index, (low, high) in enumerate(cuts):
            copies.append(
                pltpu.make_async_copy(
                    blocks[number].at[:, pl.ds(low, high - low)],
                    outs[index].at[place, :],
                    sems.at[number, index],
                )
            )
    for copy in copies:
        copy.start()
    for copy in copies:
        copy.wait()


def whole(array):
    shape = array.shape
    return pl.BlockSpec(shape, lambda i, s: (0,) * len(shape))


def fixed(array):
    shape = array.shape
    return pl.BlockSpec(shape, lambda i, s: (0,) * len(shape), pipeline_mode=pl.Buffered(1))


def by_row(array, first=0):
    shape = array.shape
    rest = (0,) * (len(shape) - 1)
    return pl.BlockSpec((1,) + shape[1:], lambda i, s: (first + i,) + rest)


def call(kernel, grid, ins, outs, out_specs, scratch, name, micros, alias=None):
    flops = int(micros * 1e8)
    return pl.pallas_call(
        kernel,
        out_shape=outs,
        grid_spec=pltpu.PrefetchScalarGridSpec(
            num_scalar_prefetch=1,
            grid=grid,
            in_specs=[spec for _, spec in ins[1:]],
            out_specs=out_specs,
            scratch_shapes=scratch,
        ),
        input_output_aliases=alias or {},
        compiler_params=pltpu.CompilerParams(vmem_limit_bytes=VMEM_LIMIT),
        cost_estimate=pl.CostEstimate(flops=flops, bytes_accessed=1 << 10, transcendentals=0),
        name=name,
    )(*[a for a, _ in ins])


def body(
    tokens, cotangent, prev_logits, segment_ids, w_qkv, b_qv, w_out, w_up, b_up, w_down,
    biases, gains, shifts,
):
    rows, slots, width = tokens.shape
    full = width * lax.axis_size("tensor")
    groups = lax.axis_size("dp")
    near_dp = groups == 8
    heads = prev_logits.shape[1]
    half = slots // 2
    units = w_up.shape[1]
    me = lax.axis_index("tensor").astype(jnp.int32)
    dp = lax.axis_index("dp").astype(jnp.int32)
    me_ref = jnp.stack([me, lax.rem(dp, 2), dp // 2, dp])
    core = lax.rem(me, 2)
    sds = jax.ShapeDtypeStruct

    def after(value, *others):
        return lax.optimization_barrier((value, others))[0]

    def pp(array, step):
        return lax.ppermute(array, "tensor", [(i, i ^ step) for i in range(4)])

    def pp_x(array):
        return lax.ppermute(array, "dp", [(i, i ^ 1) for i in range(groups)])

    def pp_z(array, step):
        deep = groups // 2
        pairs = [(i, (i // 2 + step) % deep * 2 + i % 2) for i in range(groups)]
        return lax.ppermute(array, "dp", pairs)

    order = list(range(0, groups, 2)) + list(range(groups - 1, 0, -2))
    onward = [(order[i], order[(i + 1) % groups]) for i in range(groups)]
    backward = [(b, a) for a, b in onward]

    ring_steps = [0]
    for step in range(1, groups // 2):
        ring_steps += [step, groups - step]
    ring_steps += [groups // 2]

    def ring_step(ahead, behind):
        return lax.ppermute(ahead, "dp", onward), lax.ppermute(behind, "dp", backward)

    def place_rows(blocks, cuts):
        outs = [sds((full, high - low), BF) for low, high in cuts]
        anywhere = pl.BlockSpec(memory_space=pl.ANY)
        return call(
            functools.partial(gather_kernel, cuts, ring_steps), (1,),
            [(me_ref, None)] + [(b, anywhere) for b in blocks], outs, [anywhere] * len(outs),
            [pltpu.SemaphoreType.DMA((groups, len(cuts)))], "gather", 2,
        )

    tokens = jnp.swapaxes(tokens, 1, 2)
    cotangent = jnp.swapaxes(cotangent, 1, 2)
    shard_in = w_qkv.astype(BF).reshape(w_qkv.shape[0], 3 * width)
    x_y = pp(tokens, 2)
    x_c = pp(tokens, 1)
    shard_in = jnp.concatenate([shard_in, w_out.T.astype(BF)], 1)
    shard_big = jnp.concatenate([w_up.astype(BF), w_down.T.astype(BF)], 1)
    big = []
    if near_dp:
        ring = [ring_step(shard_in, shard_in)]
        ring.append(ring_step(*ring[-1]))
        ring.append(ring_step(*ring[-1]))
        last = lax.ppermute(ring[-1][0], "dp", onward)
        shard_big = after(shard_big, last)
        big.append(ring_step(shard_big, shard_big))
        w_in = place_rows([shard_in, *ring[0], *ring[1], *ring[2], last], ((0, full),))[0]
        if len(CHUNKS) == 1:
            w_in = after(w_in, *big[0])
            big.append(ring_step(*big[0]))
    else:
        w_in = lax.all_gather(shard_in, "dp", axis=0, tiled=True)
        big_a = lax.all_gather(shard_big, "dp", axis=0, tiled=True)
    wo0 = w_in[:, 3 * width :]
    wo2 = pp(wo0, 2)
    wo1, wo3 = pp(wo0, 1), pp(wo2, 1)
    x_d = pp(x_y, 1)
    x_pieces = (tokens, x_c, x_y, x_d)
    cot = after(cotangent, x_y)
    dy_mine = lax.dynamic_slice_in_dim(cot, core * half, half, 2)
    dy_other = lax.dynamic_slice_in_dim(cot, (1 - core) * half, half, 2)
    dy1, dy2, dy3 = pp(dy_other, 1), pp(dy_mine, 2), pp(dy_other, 3)
    b_up_a = b_up.reshape(1, units)
    b_up_b = pp(b_up_a, 1)

    raw = None
    state = []
    for first, count in CHUNKS:
        ins = [(me_ref, None)] + [(p, by_row(p, first)) for p in x_pieces]
        ins += [(w_in, fixed(w_in)), (b_qv, whole(b_qv)), (prev_logits, by_row(prev_logits, first))]
        ins += [(segment_ids, whole(segment_ids))]
        alias = None
        if raw is not None:
            alias = {len(ins): 0}
            ins += [(raw, pl.BlockSpec(memory_space=pl.ANY))]
        outs = [
            sds(prev_logits.shape, BF),
            sds((count,) + prev_logits.shape[1:], BF),
            sds((count, 3, width, slots), BF),
            sds((count, width, half), BF),
            sds((count, width, half), BF),
            sds((count, full, slots), BF),
            sds((count, half, full), BF),
        ]
        specs = [by_row(outs[0], first)] + [by_row(o) for o in outs[1:]]
        raw, prob, qkv, o_own, o_oth, xt, xh = call(
            functools.partial(attend_kernel, first, heads, alias is not None),
            (count,), ins, outs, specs, [pltpu.VMEM((width, slots), BF)], "attend",
            4.3 * count, alias,
        )
        state.append(dict(prob=prob, qkv=qkv, o_own=o_own, o_oth=o_oth, xh=xh, xt=xt))
        if near_dp and len(big) < 3 and len(CHUNKS) > 1:
            w_in = after(w_in, *big[-1])
            big.append(ring_step(*after(big[-1], o_own)))

    for s in state:
        s["o1"], s["o2"], s["o3"] = pp(s["o_oth"], 1), pp(s["o_own"], 2), pp(s["o_oth"], 3)
    here = [wo1, wo3, dy1, dy2, dy3] + [s[k] for s in state for k in ("o1", "o2", "o3")]
    if near_dp:
        while len(big) < 3:
            big.append(ring_step(*after(big[-1], state[-1]["o_own"])))
        last = lax.ppermute(after(big[2][0], *here), "dp", onward)
        big_a = place_rows([shard_big, *big[0], *big[1], *big[2], last], ((0, 2 * units),))[0]
    else:
        big_a = after(big_a, state[-1]["o_own"])
    big_b = pp(big_a, 1)
    for (first, count), s in zip(CHUNKS, state):
        ins = [(me_ref, None)]
        ins += [(s[k], by_row(s[k])) for k in ("o_own", "o1", "o2", "o3")]
        ins += [(w, fixed(w)) for w in (wo0, wo1, wo2, wo3, big_a, big_b)]
        ins += [(s["xh"], by_row(s["xh"]))]
        ins += [(w, whole(w)) for w in (biases, gains, shifts)]
        ins += [(w, fixed(w)) for w in (b_up_a, b_up_b)]
        outs = [
            sds((count, half, full), F32),
            sds((count, half, 128), F32),
            sds((count, half, full), BF),
            sds((count, half, units), BF),
            sds((count, half, units), BF),
            sds((count, half, 2 * units), BF),
            sds((count, half, full), BF),
        ]
        s["n1"], s["r1"], s["x1"], s["ga"], s["gb"], s["gp"], s["part"] = call(
            up_kernel, (count,), ins, outs, [by_row(o) for o in outs], [], "up", 4 * count,
        )
        s["part_y"] = pp(s["part"], 2)
        s["gc"], s["x1_c"] = pp(s["gb"], 1), pp(s["x1"], 1)

    for (first, count), s in zip(CHUNKS, state):
        ins = [(me_ref, None)]
        ins += [(s[k], by_row(s[k])) for k in ("n1", "part", "part_y")]
        ins += [(d, by_row(d, first)) for d in (dy_mine, dy1, dy2, dy3)]
        ins += [(w, whole(w)) for w in (biases, gains, shifts)]
        ins += [(w, fixed(w)) for w in (big_a, big_b)]
        ins += [(s["gp"], by_row(s["gp"]))]
        outs = [
            sds((count, width, half), BF),
            sds((count, width, half), BF),
            sds((count, half, full), F32),
            sds((count, half, full), BF),
            sds((count, half, units), BF),
            sds((count, half, units), BF),
            sds((count, half, full), BF),
            sds((count, 3, full), F32),
            sds((count, 1, 2 * units), F32),
        ]
        (
            s["act_own"], s["act_oth"], s["ds2"], s["ds2b"], s["da"], s["db"], s["part2"], s["vec2"],
            s["bup"],
        ) = call(
            down_kernel, (count,), ins, outs, [by_row(o) for o in outs],
            [pltpu.VMEM((full, half), F32)], "down", 4 * count,
        )
        s["part2_y"] = pp(s["part2"], 2)
        s["ds2b_c"], s["dc"] = pp(s["ds2b"], 1), pp(s["db"], 1)

    def ffn_grad(lefts, rights):
        block = 256
        def part(a):
            return pl.BlockSpec(a.shape[:2] + (block,), lambda i, s: (0, 0, i))
        ins = [(me_ref, None)] + [(a, fixed(a)) for a in lefts] + [(a, part(a)) for a in rights]
        across, down = rights[0].shape[-1], lefts[0].shape[-1]
        outs = [sds((down // 2, across), BF)] * 2
        specs = [pl.BlockSpec((down // 2, block), lambda i, s: (0, i))] * 2
        return call(
            functools.partial(ffn_grad_kernel, len(lefts), True),
            (across // block,), ins, outs, specs, [pltpu.VMEM((down, block), F32)], "ffn_grad", 3,
        )

    def fold(keep, got):
        outs = [sds((keep.shape[0] // 4, keep.shape[1]), BF)] * 4
        return call(
            fold_kernel, (1,), [(me_ref, None), (keep, whole(keep)), (got, whole(got))],
            outs, [whole(o) for o in outs], [], "fold", 1,
        )

    def total_of(parts):
        return functools.reduce(jnp.add, [p.astype(F32) for p in parts]).astype(BF)

    def scatter_z(cut):
        return [cut[0]] + [pp_z(cut[step], step) for step in (1, 2, 3)]

    def finish(blocks, outs, pair=False):
        return call(
            functools.partial(finish_kernel, ring_steps, pair), (1,),
            [(me_ref, None)] + [(b, whole(b)) for b in blocks],
            outs, [whole(o) for o in outs], [], "finish", 2,
        )

    def both(own, other):
        return [s[own] for s in state] + [s[other] for s in state]

    keep_d, send_d = ffn_grad(both("ga", "gc"), both("ds2b", "ds2b_c"))
    keep_u, send_u = ffn_grad(both("x1", "x1_c"), both("da", "dc"))

    def whole_of(keep, send):
        low = jnp.where(lax.rem(dp, 2) == 0, keep, send)
        high = jnp.where(lax.rem(dp, 2) == 0, send, keep)
        return jnp.concatenate([low, high], 0)

    if near_dp:
        got_d = pp_x(send_d)
        cut_d = fold(keep_d, got_d)
        state[0]["part2_y"] = after(state[0]["part2_y"], keep_u, *cut_d)
        z_d = scatter_z(cut_d)
        got_u = pp_x(after(send_u, got_d))
    else:
        grad_down, grad_up = lax.psum((whole_of(keep_d, send_d), whole_of(keep_u, send_u)), "dp")
        grad_down, grad_up = grad_down.astype(F32), grad_up.astype(F32)

    lg = None
    for (first, count), s in zip(CHUNKS, state):
        ins = [(me_ref, None)]
        ins += [(s[k], by_row(s[k])) for k in ("ds2", "part2", "part2_y", "n1", "r1")]
        ins += [(gains, whole(gains)), (wo0, fixed(wo0)), (wo1, fixed(wo1))]
        outs = [
            sds((count, half, full), BF),
            sds((count, 2 * width, half), F32),
            sds((count, width, half), BF),
            sds((count, width, half), BF),
            sds((count, 3, full), F32),
        ]
        s["ds1b"], s["near"], s["do_own"], s["do_oth"], s["vec1"] = call(
            mid_kernel, (count,), ins, outs,
            [by_row(o) for o in outs], [pltpu.VMEM((half, full), F32)], "mid", 2 * count,
        )
        s["do_c"], s["ds1b_c"] = pp(s["do_oth"], 1), pp(s["ds1b"], 1)

    def over_rows(key):
        return functools.reduce(jnp.add, [jnp.sum(s[key], axis=0) for s in state])

    if near_dp:
        cut_u = fold(keep_u, got_u)
        state[0]["do_c"] = after(state[0]["do_c"], *cut_u)
        z_u = scatter_z(cut_u)
        total_d = total_of(z_d)

    for (first, count), s in zip(CHUNKS, state):
        ins = [(me_ref, None)]
        ins += [(s[k], by_row(s[k])) for k in ("prob", "qkv", "do_own", "do_c")]
        ins += [(w_in, fixed(w_in)), (s["near"], by_row(s["near"]))]
        alias = None
        if lg is not None:
            alias = {len(ins): 0}
            ins += [(lg, pl.BlockSpec(memory_space=pl.ANY))]
        outs = [sds(prev_logits.shape, BF), sds((count, 3 * width, slots), BF)]
        outs += [sds((count, width, slots), BF)] * 4
        outs += [sds((count, width, 2), F32)]
        specs = [by_row(outs[0], first)] + [by_row(o) for o in outs[1:]]
        scratch = [pltpu.VMEM((width, slots), BF), pltpu.VMEM((full, slots), F32)]
        lg, s["dqkv"], s["e0"], s["e1"], s["e2"], s["e3"], s["bqv"] = call(
            functools.partial(back_kernel, heads, alias is not None),
            (count,), ins, outs, specs, scratch, "back", 4.3 * count, alias,
        )

    ins = [(me_ref, None)]
    for key in ("xt", "dqkv", "o_own", "ds1b", "o_oth", "ds1b_c"):
        ins += [(s[key], whole(s[key])) for s in state]
    outs = [sds((full // 2, full), BF)] * 2
    keep, send = call(
        functools.partial(qkv_grad_kernel, len(state)), (1,), ins, outs, [whole(o) for o in outs],
        [pltpu.VMEM((full, full), F32)], "qkv_grad", 4,
    )

    outs = [sds((3 * width, full), F32), sds((width, full), F32)]
    if near_dp:
        total_u = total_of(z_u)
        pair = jnp.concatenate([total_d, total_u], 0)
        ring_u = [ring_step(pair, pair)]
        got = pp_x(send)
        ring_u.append(ring_step(*ring_u[-1]))
        z_t = scatter_z(fold(keep, got))
        ring_u.append(ring_step(*ring_u[-1]))
        last_u = lax.ppermute(ring_u[-1][0], "dp", onward)
        total = total_of(z_t)
        ring = [ring_step(total, total)]
        ring.append(ring_step(*ring[-1]))
        ring.append(ring_step(*ring[-1]))
        last = lax.ppermute(ring[-1][0], "dp", onward)
        grad_down, grad_up = finish(
            [pair, *ring_u[0], *ring_u[1], *ring_u[2], last_u],
            [sds((units, full), F32), sds((full, units), F32)], True,
        )
        grad_in, grad_out = finish([total, *ring[0], *ring[1], *ring[2], last], outs)
    else:
        tail = lax.psum(whole_of(keep, send), "dp").astype(F32)
        grad_in, grad_out = tail[: 3 * width], tail[3 * width :]
    vec = jnp.concatenate([over_rows("vec1"), over_rows("vec2")], 0)
    bup = over_rows("bup").reshape(2, units)
    bqv = over_rows("bqv").T
    vec = vec + pp(vec, 1)
    vec = (vec + pp(vec, 2)) * 0.5
    bup = bup[0:1] + pp(bup[1:2], 1)
    small = jnp.concatenate(
        [vec, bup, jnp.pad(bqv.reshape(1, -1), ((0, 0), (0, full - 2 * width)))], 0
    )
    if near_dp:
        small = after(small, total)
    step = 1
    while step < groups:
        small = small + lax.ppermute(small, "dp", [(i, i ^ step) for i in range(groups)])
        step *= 2
    grad_b_up = small[6]
    grad_b_qv = small[7, : 2 * width].reshape(2, width)

    grad_in = jnp.transpose(grad_in.reshape(3, width, full), (2, 0, 1))

    def joined(key):
        return state[0][key] if len(state) == 1 else jnp.concatenate([s[key] for s in state], 0)

    act_own, act_c = joined("act_own"), pp(joined("act_oth"), 1)
    block_out = jnp.concatenate(
        [jnp.where(core == 0, act_own, act_c), jnp.where(core == 0, act_c, act_own)], 2
    )

    def dx_of(s):
        near = s["e2"].astype(F32) + pp(s["e3"], 1).astype(F32)
        far = pp(near.astype(BF), 2).astype(F32)
        return s["e0"].astype(F32) + pp(s["e1"], 1).astype(F32) + far

    parts = [dx_of(s) for s in state]
    grad_x = (parts[0] if len(parts) == 1 else jnp.concatenate(parts, 0)).astype(BF)
    return (
        jnp.swapaxes(block_out, 1, 2),
        raw,
        jnp.swapaxes(grad_x, 1, 2),
        lg,
        grad_in,
        grad_b_qv,
        grad_out,
        grad_up,
        grad_b_up,
        grad_down,
        jnp.stack([small[2], small[5]]),
        jnp.stack([small[0], small[3]]),
        jnp.stack([small[1], small[4]]),
    )


def solution(mesh):
    placed = (
        P("dp", None, "tensor"),
        P("dp", None, "tensor"),
        P("dp", "tensor", None, None),
        P("dp", None),
        P("dp", None, "tensor"),
        P(None, "tensor"),
        P("tensor", "dp"),
        P("dp", "tensor"),
        P("tensor"),
        P("tensor", "dp"),
        P(),
        P(),
        P(),
    )
    return jax.shard_map(
        body,
        mesh=mesh,
        in_specs=placed,
        out_specs=(
            P("dp", None, "tensor"),
            P("dp", "tensor", None, None),
            P("dp", None, "tensor"),
            P("dp", "tensor", None, None),
            P(None, None, "tensor"),
            P(None, "tensor"),
            P("tensor", None),
            P(None, "tensor"),
            P("tensor"),
            P("tensor", None),
            P(),
            P(),
            P(),
        ),
        check_vma=False,
    )
```

```python
import functools

import jax
import jax.numpy as jnp
from jax import lax
from jax.experimental import pallas as pl
from jax.experimental.pallas import tpu as pltpu
from jax.sharding import PartitionSpec as P

EPS = 1e-06
NEG = -1e30
BF = jnp.bfloat16
F32 = jnp.float32
VMEM_LIMIT = 48 * 1024 * 1024


def dot(a, b):
    return lax.dot_general(a, b, (((1,), (0,)), ((), ())), preferred_element_type=F32)


def dot_nt(a, b):
    return lax.dot_general(a, b, (((1,), (1,)), ((), ())), preferred_element_type=F32)


def dot_tn(a, b):
    return lax.dot_general(a, b, (((0,), (0,)), ((), ())), preferred_element_type=F32)


def place_of(me, step):
    core, chip = lax.rem(me, 2), me // 2
    core = 1 - core if step % 2 else core
    chip = 1 - chip if step // 2 else chip
    return 2 * chip + core


def ln_stats(summed):
    row_mean = jnp.mean(summed, axis=-1, keepdims=True)
    centered = summed - row_mean
    inv_std = lax.rsqrt(jnp.mean(centered * centered, axis=-1, keepdims=True) + EPS)
    return centered * inv_std, inv_std


def ln_back(grad, normed, inv_std, gain):
    scaled = grad * gain
    inner = (
        scaled
        - jnp.mean(scaled, axis=-1, keepdims=True)
        - normed * jnp.mean(scaled * normed, axis=-1, keepdims=True)
    )
    return inner * inv_std


def attend_kernel(
    heads, me_ref, x0, x1, x2, x3, w_ref, b_ref, prev_ref, seg_ref,
    raw_ref, p_ref, qkv_ref, own_ref, oth_ref, xt_ref, xh_ref, o_scr,
):
    me = me_ref[0]
    core = lax.rem(me, 2)
    width, slots = x0.shape[1], x0.shape[2]
    half = slots // 2
    size = width // heads
    for step, piece in enumerate((x0, x1, x2, x3)):
        start = pl.multiple_of(place_of(me, step) * width, width)
        xt_ref[0, pl.ds(start, width), :] = piece[0]
    bias = jnp.transpose(jnp.broadcast_to(b_ref[0:1, :], (128, width)))[:, 0:1]
    bias_v = jnp.transpose(jnp.broadcast_to(b_ref[1:2, :], (128, width)))[:, 0:1]
    packed = dot_tn(w_ref[:, : 3 * width], xt_ref[0])
    qkv_ref[0, 0] = (packed[:width] + bias).astype(BF)
    qkv_ref[0, 1] = packed[width : 2 * width].astype(BF)
    qkv_ref[0, 2] = (packed[2 * width :] + bias_v).astype(BF)
    mine = pl.ds(pl.multiple_of(core * half, half), half)
    other = pl.ds(pl.multiple_of((1 - core) * half, half), half)
    xh_ref[0] = jnp.transpose(xt_ref[0, :, mine])
    row = seg_ref[pl.ds(pl.program_id(0), 1), :].astype(F32)
    column = jnp.transpose(jnp.broadcast_to(row, (128, slots)))[:, 0:1]
    scale = 1.0 / (size**0.5)
    for block in range(2):
        rows = slice(block * half, (block + 1) * half)
        allowed = column[rows] == row
        for h in range(heads):
            feats = slice(h * size, (h + 1) * size)
            scores = dot_tn(qkv_ref[0, 0, feats, rows], qkv_ref[0, 1, feats, :]) * scale
            scores = scores + prev_ref[0, h, rows, :].astype(F32)
            raw_ref[0, h, rows, :] = scores.astype(BF)
            masked = jnp.where(allowed, scores, NEG)
            expanded = jnp.exp(masked - jnp.max(masked, axis=-1, keepdims=True))
            prob = expanded * (1.0 / jnp.sum(expanded, axis=-1, keepdims=True))
            prob = prob.astype(BF)
            p_ref[0, h, rows, :] = prob
            o_scr[feats, rows] = dot_nt(qkv_ref[0, 2, feats, :], prob).astype(BF)
    own_ref[0] = o_scr[:, mine]
    oth_ref[0] = o_scr[:, other]


def up_kernel(
    me_ref, o0, o1, o2, o3, wo0, wo1, wo2, wo3, big_a, big_b, xh_ref, bias_ref, gain_ref, shift_ref,
    b_up_a, b_up_b,
    n1_ref, r1_ref, x1_ref, ga_ref, gb_ref, gp_ref, part_ref,
):
    units = b_up_a.shape[1]
    w1a, w1b = big_a.at[:, :units], big_b.at[:, :units]
    w2a, w2b = big_a.at[:, units : 2 * units], big_b.at[:, units : 2 * units]
    total = xh_ref[0].astype(F32) + bias_ref[0:1, :]
    for left, right in ((o0, wo0), (o1, wo1), (o2, wo2), (o3, wo3)):
        total = total + dot_nt(jnp.transpose(left[0]), right[...])
    normed, inv_std = ln_stats(total)
    n1_ref[0] = normed
    r1_ref[0] = jnp.broadcast_to(inv_std, r1_ref.shape[1:])
    x1_ref[0] = (normed * gain_ref[0:1, :] + shift_ref[0:1, :]).astype(BF)
    block = 256
    for index, (w1, b_up, g_ref) in enumerate(((w1a, b_up_a, ga_ref), (w1b, b_up_b, gb_ref))):
        for start in range(0, units, block):
            hidden = dot(x1_ref[0], w1[:, start : start + block]) + b_up[:, start : start + block]
            cdf = 0.5 * (1.0 + lax.erf(hidden * (0.5**0.5)))
            pdf = jnp.exp(-0.5 * hidden * hidden) * 0.3989422804014327
            g_ref[0, :, start : start + block] = (hidden * cdf).astype(BF)
            lanes = slice(index * units + start, index * units + start + block)
            gp_ref[0, :, lanes] = (cdf + hidden * pdf).astype(BF)
    part_ref[0] = (dot_nt(ga_ref[0], w2a[...]) + dot_nt(gb_ref[0], w2b[...])).astype(BF)


def down_kernel(
    me_ref, n1_ref, pa_ref, pb_ref, dy0, dy1, dy2, dy3, bias_ref, gain_ref, shift_ref,
    big_a, big_b, gp_ref,
    act_own_ref, act_oth_ref, ds_ref, dsb_ref, da_ref, db_ref, vec_ref, bup_ref, part_ref,
    scr,
):
    me = me_ref[0]
    width = dy0.shape[1]
    units = gp_ref.shape[2] // 2
    w1a, w1b = big_a.at[:, :units], big_b.at[:, :units]
    w2a, w2b = big_a.at[:, units : 2 * units], big_b.at[:, units : 2 * units]
    branch = pa_ref[0].astype(F32) + pb_ref[0].astype(F32)
    first_out = n1_ref[0] * gain_ref[0:1, :] + shift_ref[0:1, :]
    normed, inv_std = ln_stats(first_out + branch + bias_ref[1:2, :])
    gain = gain_ref[1:2, :]
    scr[...] = jnp.transpose(normed * gain + shift_ref[1:2, :])
    for step, out in ((0, act_own_ref), (1, act_oth_ref)):
        start = pl.multiple_of(place_of(me, step) * width, width)
        out[0] = scr[pl.ds(start, width), :].astype(BF)
    for step, piece in enumerate((dy0, dy1, dy2, dy3)):
        start = pl.multiple_of(place_of(me, step) * width, width)
        scr[pl.ds(start, width), :] = piece[0].astype(F32)
    grad = jnp.transpose(scr[...])
    inner = ln_back(grad, normed, inv_std, gain)
    ds_ref[0] = inner
    vec_ref[0, 0:1, :] = jnp.sum(grad * normed, axis=0, keepdims=True)
    vec_ref[0, 1:2, :] = jnp.sum(grad, axis=0, keepdims=True)
    vec_ref[0, 2:3, :] = jnp.sum(inner, axis=0, keepdims=True)
    dsb_ref[0] = inner.astype(BF)
    block = 256
    for index, (w2, dh_ref) in enumerate(((w2a, da_ref), (w2b, db_ref))):
        for start in range(0, units, block):
            lanes = slice(index * units + start, index * units + start + block)
            grad_hidden = dot(dsb_ref[0], w2[:, start : start + block]) * gp_ref[
                0, :, lanes
            ].astype(F32)
            bup_ref[0, 0:1, lanes] = jnp.sum(grad_hidden, axis=0, keepdims=True)
            dh_ref[0, :, start : start + block] = grad_hidden.astype(BF)
    part_ref[0] = (dot_nt(da_ref[0], w1a[...]) + dot_nt(db_ref[0], w1b[...])).astype(BF)


def mid_kernel(
    me_ref, ds_ref, pa_ref, pb_ref, n1_ref, r1_ref, gain_ref, wo0, wo1,
    dsb_ref, near_ref, vec_ref, do_own_ref, do_oth_ref, scr,
):
    chip = me_ref[0] // 2
    width = do_own_ref.shape[1]
    grad = ds_ref[0] + (pa_ref[0].astype(F32) + pb_ref[0].astype(F32))
    normed = n1_ref[0]
    inner = ln_back(grad, normed, r1_ref[0, :, 0:1], gain_ref[0:1, :])
    vec_ref[0, 0:1, :] = jnp.sum(grad * normed, axis=0, keepdims=True)
    vec_ref[0, 1:2, :] = jnp.sum(grad, axis=0, keepdims=True)
    vec_ref[0, 2:3, :] = jnp.sum(inner, axis=0, keepdims=True)
    dsb = inner.astype(BF)
    dsb_ref[0] = dsb
    scr[...] = inner
    chip_lanes = pl.ds(pl.multiple_of(chip * 2 * width, 128), 2 * width)
    near_ref[0] = jnp.transpose(scr[:, chip_lanes])
    do_own_ref[0] = jnp.transpose(dot(dsb, wo0[...])).astype(BF)
    do_oth_ref[0] = jnp.transpose(dot(dsb, wo1[...])).astype(BF)


def back_kernel(
    heads, me_ref, p_ref, qkv_ref, do_own_ref, do_oth_ref, w_ref, near_ref,
    lg_ref, dqkv_ref, e0, e1, e2, e3, vec_ref, do_scr, dx_scr,
):
    me = me_ref[0]
    core, chip = lax.rem(me, 2), me // 2
    width, slots = qkv_ref.shape[2], qkv_ref.shape[3]
    half = slots // 2
    size = width // heads
    mine = pl.ds(pl.multiple_of(core * half, half), half)
    other = pl.ds(pl.multiple_of((1 - core) * half, half), half)
    do_scr[:, mine] = do_own_ref[0]
    do_scr[:, other] = do_oth_ref[0]
    scale = 1.0 / (size**0.5)
    for h in range(heads):
        feats = slice(h * size, (h + 1) * size)
        query, key, value = (qkv_ref[0, part, feats, :] for part in range(3))
        out_grad = do_scr[feats, :]
        for block in range(2):
            rows = slice(block * half, (block + 1) * half)
            prob = p_ref[0, h, rows, :].astype(F32)
            grad_prob = dot_tn(do_scr[feats, rows], value)
            weighted = grad_prob * prob
            inner = jnp.sum(weighted, axis=-1, keepdims=True)
            lg_ref[0, h, rows, :] = (weighted - prob * inner).astype(BF)
        grad_query = dot_nt(key, lg_ref[0, h]) * scale
        grad_key = dot(query, lg_ref[0, h]) * scale
        grad_value = dot(out_grad, p_ref[0, h])
        vec_ref[0, feats, 0:1] = jnp.sum(grad_query, axis=1, keepdims=True)
        vec_ref[0, feats, 1:2] = jnp.sum(grad_value, axis=1, keepdims=True)
        dqkv_ref[0, pl.ds(h * size, size), :] = grad_query.astype(BF)
        dqkv_ref[0, pl.ds(width + h * size, size), :] = grad_key.astype(BF)
        dqkv_ref[0, pl.ds(2 * width + h * size, size), :] = grad_value.astype(BF)
    dx_scr[...] = dot(w_ref[:, : 3 * width], dqkv_ref[0])
    near = pl.ds(pl.multiple_of(chip * 2 * width, width), 2 * width)
    dx_scr[near, mine] = dx_scr[near, mine] + near_ref[0]
    for step, out in enumerate((e0, e1, e2, e3)):
        start = pl.multiple_of(place_of(me, step) * width, width)
        out[0] = dx_scr[pl.ds(start, width), :].astype(BF)


def ffn_grad_kernel(count, me_ref, *rest):
    lefts, rights = rest[:count], rest[count : 2 * count]
    keep_ref, send_ref, scr = rest[2 * count :]
    side = me_ref[1]
    total = None
    for left, right in zip(lefts, rights):
        a = left[...].reshape(-1, left.shape[-1])
        b = right[...].reshape(-1, right.shape[-1])
        product = dot_tn(a, b)
        total = product if total is None else total + product
    part = keep_ref.shape[0]
    scr[...] = total
    keep_ref[...] = scr[pl.ds(pl.multiple_of(side * part, part), part), :].astype(BF)
    send_ref[...] = scr[pl.ds(pl.multiple_of((1 - side) * part, part), part), :].astype(BF)


def qkv_grad_kernel(count, me_ref, *rest):
    groups = [rest[i * count : (i + 1) * count] for i in range(6)]
    keep_ref, send_ref, scr = rest[6 * count :]
    side = me_ref[1]
    total = None
    for x, grad in zip(groups[0], groups[1]):
        for index in range(grad.shape[0]):
            product = dot_nt(grad[index], x[index])
            total = product if total is None else total + product
    used = total.shape[0]
    scr[:used, :] = total
    total = None
    for lefts, rights in ((groups[2], groups[3]), (groups[4], groups[5])):
        for left, right in zip(lefts, rights):
            for index in range(left.shape[0]):
                product = dot(left[index], right[index])
                total = product if total is None else total + product
    scr[used:, :] = total
    part = scr.shape[0] // 2
    keep_ref[...] = scr[pl.ds(pl.multiple_of(side * part, part), part), :].astype(BF)
    send_ref[...] = scr[pl.ds(pl.multiple_of((1 - side) * part, part), part), :].astype(BF)


def fold_kernel(me_ref, keep_ref, got_ref, *outs):
    depth = me_ref[2]
    rows = outs[0].shape[0]
    count = len(outs)
    for step, out in enumerate(outs):
        start = pl.multiple_of(lax.rem(depth + step, count) * rows, rows)
        total = keep_ref[pl.ds(start, rows), :].astype(F32) + got_ref[pl.ds(start, rows), :].astype(F32)
        out[...] = total.astype(BF)


def finish_kernel(steps, pair, me_ref, *rest):
    count = len(steps)
    blocks, outs = rest[:count], rest[count:]
    here = ring_place(me_ref[3], count)
    rows = blocks[0].shape[0]
    for number, back in enumerate(steps):
        there = lax.rem(here + count - back, count)
        index = jnp.where(there < count // 2, there, (count - 1 - there) + count // 2)
        if pair:
            part = rows // 2
            place = pl.ds(pl.multiple_of(index * part, part), part)
            outs[0][place, :] = blocks[number][:part, :].astype(F32)
            outs[1][place, :] = blocks[number][part:, :].astype(F32)
            continue
        block = blocks[number][...].astype(F32)
        before = 0
        for out in outs:
            held = out.shape[0] // rows

            @pl.when((index >= before) & (index < before + held))
            def _():
                out[pl.ds(pl.multiple_of((index - before) * rows, rows), rows), :] = block

            before += held


def ring_place(group, groups):
    return jnp.where(lax.rem(group, 2) == 0, group // 2, groups - 1 - group // 2)


def gather_kernel(cuts, steps, me_ref, *rest):
    count = len(steps)
    blocks, outs, sems = rest[:count], rest[count:-1], rest[-1]
    here = ring_place(me_ref[3], count)
    rows = blocks[0].shape[0]
    copies = []
    for number, back in enumerate(steps):
        there = lax.rem(here + count - back, count)
        group = jnp.where(there < count // 2, 2 * there, 2 * (count - 1 - there) + 1)
        place = pl.ds(pl.multiple_of(group * rows, rows), rows)
        for index, (low, high) in enumerate(cuts):
            copies.append(
                pltpu.make_async_copy(
                    blocks[number].at[:, pl.ds(low, high - low)],
                    outs[index].at[place, :],
                    sems.at[number, index],
                )
            )
    for copy in copies:
        copy.start()
    for copy in copies:
        copy.wait()


def whole(array):
    shape = array.shape
    return pl.BlockSpec(shape, lambda i, s: (0,) * len(shape))


def held(array):
    return pl.BlockSpec(memory_space=pltpu.VMEM)


def by_row(array, first=0):
    shape = array.shape
    rest = (0,) * (len(shape) - 1)
    return pl.BlockSpec((1,) + shape[1:], lambda i, s: (first + i,) + rest)


def without(low, high, kernel):
    def inner(*refs):
        kernel(*refs[:low], *refs[high:])

    return inner


def call(kernel, grid, ins, outs, out_specs, scratch, name, micros, alias=None):
    flops = int(micros * 1e8)
    return pl.pallas_call(
        kernel,
        out_shape=outs,
        grid_spec=pltpu.PrefetchScalarGridSpec(
            num_scalar_prefetch=1,
            grid=grid,
            in_specs=[spec for _, spec in ins[1:]],
            out_specs=out_specs,
            scratch_shapes=scratch,
        ),
        input_output_aliases=alias or {},
        compiler_params=pltpu.CompilerParams(vmem_limit_bytes=VMEM_LIMIT),
        cost_estimate=pl.CostEstimate(flops=flops, bytes_accessed=1 << 10, transcendentals=0),
        name=name,
    )(*[a for a, _ in ins])


def body(
    tokens, cotangent, prev_logits, segment_ids, w_qkv, b_qv, w_out, w_up, b_up, w_down,
    biases, gains, shifts,
):
    rows, slots, width = tokens.shape
    full = width * lax.axis_size("tensor")
    groups = lax.axis_size("dp")
    near_dp = groups == 8
    heads = prev_logits.shape[1]
    half = slots // 2
    units = w_up.shape[1]
    me = lax.axis_index("tensor").astype(jnp.int32)
    dp = lax.axis_index("dp").astype(jnp.int32)
    me_ref = jnp.stack([me, lax.rem(dp, 2), dp // 2, dp])
    core = lax.rem(me, 2)
    sds = jax.ShapeDtypeStruct

    def after(value, *others):
        return lax.optimization_barrier((value, others))[0]

    together = lax.optimization_barrier

    def pp(array, step):
        return lax.ppermute(array, "tensor", [(i, i ^ step) for i in range(4)])

    def pp_x(array):
        return lax.ppermute(array, "dp", [(i, i ^ 1) for i in range(groups)])

    def pp_z(array, step):
        deep = groups // 2
        pairs = [(i, (i // 2 + step) % deep * 2 + i % 2) for i in range(groups)]
        return lax.ppermute(array, "dp", pairs)

    order = list(range(0, groups, 2)) + list(range(groups - 1, 0, -2))
    onward = [(order[i], order[(i + 1) % groups]) for i in range(groups)]
    backward = [(b, a) for a, b in onward]

    ring_steps = [0]
    for step in range(1, groups // 2):
        ring_steps += [step, groups - step]
    ring_steps += [groups // 2]

    def ring_step(ahead, behind):
        return lax.ppermute(ahead, "dp", onward), lax.ppermute(behind, "dp", backward)

    def place_rows(blocks, cuts):
        outs = [sds((full, high - low), BF) for low, high in cuts]
        anywhere = pl.BlockSpec(memory_space=pl.ANY)
        return call(
            functools.partial(gather_kernel, cuts, ring_steps), (1,),
            [(me_ref, None)] + [(b, anywhere) for b in blocks], outs, [anywhere] * len(outs),
            [pltpu.SemaphoreType.DMA((groups, len(cuts)))], "gather", 2,
        )

    tokens = jnp.swapaxes(tokens, 1, 2)
    cotangent = jnp.swapaxes(cotangent, 1, 2)
    shard_in = w_qkv.astype(BF).reshape(w_qkv.shape[0], 3 * width)
    x_y = pp(tokens, 2)
    x_c = pp(tokens, 1)
    shard_in = jnp.concatenate([shard_in, w_out.T.astype(BF)], 1)
    shard_big = jnp.concatenate([w_up.astype(BF), w_down.T.astype(BF)], 1)
    big = []
    if near_dp:
        ring = [ring_step(shard_in, shard_in)]
        ring.append(ring_step(*together(ring[-1])))
        ring.append(ring_step(*together(ring[-1])))
        last = lax.ppermute(together(ring[-1])[0], "dp", onward)
        shard_big = after(shard_big, last)
        big.append(ring_step(shard_big, shard_big))
        w_in = place_rows([shard_in, *ring[0], *ring[1], *ring[2], last], ((0, full),))[0]
        w_in = after(w_in, *big[0])
        big.append(ring_step(*big[0]))
    else:
        w_in = lax.all_gather(shard_in, "dp", axis=0, tiled=True)
        big_a = lax.all_gather(shard_big, "dp", axis=0, tiled=True)
    wo0 = w_in[:, 3 * width :]
    wo2 = pp(wo0, 2)
    wo1, wo3 = pp(wo0, 1), pp(wo2, 1)
    x_d = pp(x_y, 1)
    x_pieces = (tokens, x_c, x_y, x_d)
    cot = after(cotangent, x_y)
    dy_mine = lax.dynamic_slice_in_dim(cot, core * half, half, 2)
    dy_other = lax.dynamic_slice_in_dim(cot, (1 - core) * half, half, 2)
    dy1, dy2, dy3 = pp(dy_other, 1), pp(dy_mine, 2), pp(dy_other, 3)
    b_up_a = b_up.reshape(1, units)
    b_up_b = pp(b_up_a, 1)

    sds3 = lambda *shape_type: sds((rows,) + shape_type[:-1], shape_type[-1])

    def per_row(kernel, inputs, fulls, parts, scratch, name, micros):
        kept, out_parts = None, []
        for row in range(rows):
            ins = [(me_ref, None)] + inputs(row)
            low = len(ins)
            alias = {}
            body_kernel = kernel
            if kept is not None:
                alias = {low + i: i for i in range(len(fulls))}
                ins += [(k, pl.BlockSpec(memory_space=pl.ANY)) for k in kept]
                body_kernel = without(low, low + len(kept), kernel)
            outs = list(fulls) + list(parts)
            specs = [by_row(o, row) for o in fulls] + [by_row(o) for o in parts]
            result = call(body_kernel, (1,), ins, outs, specs, scratch, name, micros, alias)
            kept = result[: len(fulls)]
            out_parts.append(result[len(fulls) :])
        return kept, list(zip(*out_parts))

    ins = [(me_ref, None)] + [(p, by_row(p)) for p in x_pieces]
    ins += [(w_in, held(w_in)), (b_qv, whole(b_qv)), (prev_logits, by_row(prev_logits))]
    ins += [(segment_ids, whole(segment_ids))]
    outs = [
        sds(prev_logits.shape, BF),
        sds(prev_logits.shape, BF),
        sds3(3, width, slots, BF),
        sds3(width, half, BF),
        sds3(width, half, BF),
        sds3(full, slots, BF),
        sds3(half, full, BF),
    ]
    raw, prob, qkv, o_own, o_oth, xt, xh = call(
        functools.partial(attend_kernel, heads), (rows,), ins, outs, [by_row(o) for o in outs],
        [pltpu.VMEM((width, slots), BF)], "attend", 4.3 * rows,
    )
    o1, o2, o3 = pp(o_oth, 1), pp(o_own, 2), pp(o_oth, 3)
    if near_dp:
        big.append(ring_step(*after(big[-1], o_own)))
        last = lax.ppermute(after(big[2][0], wo1, wo3, dy1, dy2, dy3, o1, o2, o3), "dp", onward)
        big_a = place_rows([shard_big, *big[0], *big[1], *big[2], last], ((0, 2 * units),))[0]
    else:
        big_a = after(big_a, o_own)
    big_b = pp(big_a, 1)

    one = (1, half, full)
    (n1, r1, x1, ga, gb, gp), (part,) = per_row(
        up_kernel,
        lambda row: [(o, by_row(o, row)) for o in (o_own, o1, o2, o3)]
        + [(w, held(w)) for w in (wo0, wo1, wo2, wo3, big_a, big_b)]
        + [(xh, by_row(xh, row))]
        + [(w, whole(w)) for w in (biases, gains, shifts, b_up_a, b_up_b)],
        [
            sds3(half, full, F32), sds3(half, 128, F32), sds3(half, full, BF),
            sds3(half, units, BF), sds3(half, units, BF), sds3(half, 2 * units, BF),
        ],
        [sds(one, BF)], [], "up", 4,
    )
    part_y = [pp(p, 2) for p in part]
    gc, x1_c = pp(gb, 1), pp(x1, 1)

    (act_own, act_oth, ds2, ds2b, da, db, vec2, bup), (part2,) = per_row(
        down_kernel,
        lambda row: [(n1, by_row(n1, row)), (part[row], by_row(part[row])), (part_y[row], by_row(part_y[row]))]
        + [(d, by_row(d, row)) for d in (dy_mine, dy1, dy2, dy3)]
        + [(w, whole(w)) for w in (biases, gains, shifts)]
        + [(w, held(w)) for w in (big_a, big_b)]
        + [(gp, by_row(gp, row))],
        [
            sds3(width, half, BF), sds3(width, half, BF), sds3(half, full, F32),
            sds3(half, full, BF), sds3(half, units, BF), sds3(half, units, BF),
            sds3(3, full, F32), sds3(1, 2 * units, F32),
        ],
        [sds(one, BF)], [pltpu.VMEM((full, half), F32)], "down", 4,
    )
    part2_y = [pp(p, 2) for p in part2]
    ds2b_c, dc = pp(ds2b, 1), pp(db, 1)

    def ffn_grad(lefts, rights):
        block = 256
        def part(a):
            return pl.BlockSpec(a.shape[:2] + (block,), lambda i, s: (0, 0, i))
        ins = [(me_ref, None)] + [(a, whole(a)) for a in lefts] + [(a, part(a)) for a in rights]
        across, down = rights[0].shape[-1], lefts[0].shape[-1]
        outs = [sds((down // 2, across), BF)] * 2
        specs = [pl.BlockSpec((down // 2, block), lambda i, s: (0, i))] * 2
        return call(
            functools.partial(ffn_grad_kernel, len(lefts)),
            (across // block,), ins, outs, specs, [pltpu.VMEM((down, block), F32)], "ffn_grad", 3,
        )

    def fold(keep, got):
        outs = [sds((keep.shape[0] // 4, keep.shape[1]), BF)] * 4
        return call(
            fold_kernel, (1,), [(me_ref, None), (keep, whole(keep)), (got, whole(got))],
            outs, [whole(o) for o in outs], [], "fold", 1,
        )

    def total_of(parts):
        return functools.reduce(jnp.add, [p.astype(F32) for p in parts]).astype(BF)

    def scatter_z(cut):
        return [cut[0]] + [pp_z(cut[step], step) for step in (1, 2, 3)]

    def finish(blocks, outs, pair=False):
        return call(
            functools.partial(finish_kernel, ring_steps, pair), (1,),
            [(me_ref, None)] + [(b, whole(b)) for b in blocks],
            outs, [whole(o) for o in outs], [], "finish", 2,
        )

    def whole_of(keep, send):
        low = jnp.where(lax.rem(dp, 2) == 0, keep, send)
        high = jnp.where(lax.rem(dp, 2) == 0, send, keep)
        return jnp.concatenate([low, high], 0)

    keep_d, send_d = ffn_grad((ga, gc), (ds2b, ds2b_c))
    keep_u, send_u = ffn_grad((x1, x1_c), (da, dc))
    if near_dp:
        got_d = pp_x(send_d)
        part2_y[0] = after(part2_y[0], keep_d, keep_u)
        got_u = pp_x(after(send_u, got_d))
        cut_d = fold(keep_d, got_d)
        part2_y[2] = after(part2_y[2], *cut_d)
        z_d = scatter_z(cut_d)
        cut_u = fold(keep_u, got_u)
        z_u = scatter_z(cut_u)
        total_d = total_of(z_d)
    else:
        grad_down, grad_up = lax.psum((whole_of(keep_d, send_d), whole_of(keep_u, send_u)), "dp")
        grad_down, grad_up = grad_down.astype(F32), grad_up.astype(F32)

    (ds1b, near, vec1), (do_own, do_oth) = per_row(
        mid_kernel,
        lambda row: [(ds2, by_row(ds2, row)), (part2[row], by_row(part2[row])), (part2_y[row], by_row(part2_y[row]))]
        + [(n1, by_row(n1, row)), (r1, by_row(r1, row)), (gains, whole(gains))]
        + [(wo0, held(wo0)), (wo1, held(wo1))],
        [sds3(half, full, BF), sds3(2 * width, half, F32), sds3(3, full, F32)],
        [sds((1, width, half), BF)] * 2, [pltpu.VMEM((half, full), F32)], "mid", 2,
    )
    do_c = [pp(d, 1) for d in do_oth]
    ds1b_c = pp(ds1b, 1)

    if near_dp:
        do_c[2] = after(do_c[2], *cut_u)
    (lg, dqkv, e0, e1, e2, e3, bqv), _ = per_row(
        functools.partial(back_kernel, heads),
        lambda row: [(prob, by_row(prob, row)), (qkv, by_row(qkv, row))]
        + [(do_own[row], by_row(do_own[row])), (do_c[row], by_row(do_c[row]))]
        + [(w_in, held(w_in)), (near, by_row(near, row))],
        [sds(prev_logits.shape, BF), sds3(3 * width, slots, BF)]
        + [sds3(width, slots, BF)] * 4 + [sds3(width, 2, F32)],
        [], [pltpu.VMEM((width, slots), BF), pltpu.VMEM((full, slots), F32)], "back", 4.3,
    )

    ins = [(me_ref, None)] + [(a, whole(a)) for a in (xt, dqkv, o_own, ds1b, o_oth, ds1b_c)]
    outs = [sds((full // 2, full), BF)] * 2
    keep, send = call(
        functools.partial(qkv_grad_kernel, 1), (1,), ins, outs, [whole(o) for o in outs],
        [pltpu.VMEM((full, full), F32)], "qkv_grad", 4,
    )

    outs = [sds((3 * width, full), F32), sds((width, full), F32)]
    if near_dp:
        total_u = total_of(z_u)
        pair = jnp.concatenate([total_d, total_u], 0)
        ring_u = [ring_step(pair, pair)]
        got = pp_x(send)
        ring_u.append(ring_step(*ring_u[-1]))
        z_t = scatter_z(fold(keep, got))
        ring_u.append(ring_step(*ring_u[-1]))
        last_u = lax.ppermute(ring_u[-1][0], "dp", onward)
        total = total_of(z_t)
        ring = [ring_step(total, total)]
        ring.append(ring_step(*ring[-1]))
        ring.append(ring_step(*ring[-1]))
        last = lax.ppermute(ring[-1][0], "dp", onward)
        grad_down, grad_up = finish(
            [pair, *ring_u[0], *ring_u[1], *ring_u[2], last_u],
            [sds((units, full), F32), sds((full, units), F32)], True,
        )
        grad_in, grad_out = finish([total, *ring[0], *ring[1], *ring[2], last], outs)
    else:
        tail = lax.psum(whole_of(keep, send), "dp").astype(F32)
        grad_in, grad_out = tail[: 3 * width], tail[3 * width :]
    vec = jnp.concatenate([jnp.sum(vec1, 0), jnp.sum(vec2, 0)], 0)
    bup = jnp.sum(bup, 0).reshape(2, units)
    bqv = jnp.sum(bqv, 0).T
    vec = vec + pp(vec, 1)
    vec = (vec + pp(vec, 2)) * 0.5
    bup = bup[0:1] + pp(bup[1:2], 1)
    small = jnp.concatenate(
        [vec, bup, jnp.pad(bqv.reshape(1, -1), ((0, 0), (0, full - 2 * width)))], 0
    )
    if near_dp:
        small = after(small, total)
    step = 1
    while step < groups:
        small = small + lax.ppermute(small, "dp", [(i, i ^ step) for i in range(groups)])
        step *= 2
    grad_b_up = small[6]
    grad_b_qv = small[7, : 2 * width].reshape(2, width)

    grad_in = jnp.transpose(grad_in.reshape(3, width, full), (2, 0, 1))

    act_c = pp(act_oth, 1)
    block_out = jnp.concatenate(
        [jnp.where(core == 0, act_own, act_c), jnp.where(core == 0, act_c, act_own)], 2
    )
    near_sum = e2.astype(F32) + pp(e3, 1).astype(F32)
    far = pp(near_sum.astype(BF), 2).astype(F32)
    grad_x = (e0.astype(F32) + pp(e1, 1).astype(F32) + far).astype(BF)
    return (
        jnp.swapaxes(block_out, 1, 2),
        raw,
        jnp.swapaxes(grad_x, 1, 2),
        lg,
        grad_in,
        grad_b_qv,
        grad_out,
        grad_up,
        grad_b_up,
        grad_down,
        jnp.stack([small[2], small[5]]),
        jnp.stack([small[0], small[3]]),
        jnp.stack([small[1], small[4]]),
    )


def solution(mesh):
    placed = (
        P("dp", None, "tensor"),
        P("dp", None, "tensor"),
        P("dp", "tensor", None, None),
        P("dp", None),
        P("dp", None, "tensor"),
        P(None, "tensor"),
        P("tensor", "dp"),
        P("dp", "tensor"),
        P("tensor"),
        P("tensor", "dp"),
        P(),
        P(),
        P(),
    )
    return jax.shard_map(
        body,
        mesh=mesh,
        in_specs=placed,
        out_specs=(
            P("dp", None, "tensor"),
            P("dp", "tensor", None, None),
            P("dp", None, "tensor"),
            P("dp", "tensor", None, None),
            P(None, None, "tensor"),
            P(None, "tensor"),
            P("tensor", None),
            P(None, "tensor"),
            P("tensor"),
            P("tensor", None),
            P(),
            P(),
            P(),
        ),
        check_vma=False,
    )
```

```python
import functools

import jax
import jax.numpy as jnp
from jax import lax
from jax.experimental import pallas as pl
from jax.experimental.pallas import tpu as pltpu
from jax.sharding import PartitionSpec as P

EPS = 1e-06
NEG = -1e30
BF = jnp.bfloat16
F32 = jnp.float32


def dot(a, b):
    return lax.dot_general(a, b, (((1,), (0,)), ((), ())), preferred_element_type=F32)


def dot_nt(a, b):
    return lax.dot_general(a, b, (((1,), (1,)), ((), ())), preferred_element_type=F32)


def dot_tn(a, b):
    return lax.dot_general(a, b, (((0,), (0,)), ((), ())), preferred_element_type=F32)


def place_of(me, step):
    core, chip = lax.rem(me, 2), me // 2
    core = 1 - core if step % 2 else core
    chip = 1 - chip if step // 2 else chip
    return 2 * chip + core


def ln_stats(summed):
    row_mean = jnp.mean(summed, axis=-1, keepdims=True)
    centered = summed - row_mean
    inv_std = lax.rsqrt(jnp.mean(centered * centered, axis=-1, keepdims=True) + EPS)
    return centered * inv_std, inv_std


def ln_back(grad, normed, inv_std, gain):
    scaled = grad * gain
    inner = (
        scaled
        - jnp.mean(scaled, axis=-1, keepdims=True)
        - normed * jnp.mean(scaled * normed, axis=-1, keepdims=True)
    )
    return inner * inv_std


def attend_kernel(
    heads, steps, me_ref, x0, x1, x2, x3, b_ref, prev_ref, seg_ref, *rest
):
    count = len(steps)
    blocks = rest[:count]
    raw_ref, p_ref, qkv_ref, own_ref, oth_ref, xt_ref, xh_ref, w_ref, o_scr = rest[count:]

    @pl.when(pl.program_id(0) == 0)
    def _():
        rows = blocks[0].shape[0]
        for block, back in zip(blocks, steps):
            group = group_at(me_ref, back, count) if count > 1 else 0
            w_ref[pl.ds(pl.multiple_of(group * rows, rows), rows), :] = block[...]

    me = me_ref[0]
    core = lax.rem(me, 2)
    width, slots = x0.shape[1], x0.shape[2]
    half = slots // 2
    size = width // heads
    for step, piece in enumerate((x0, x1, x2, x3)):
        start = pl.multiple_of(place_of(me, step) * width, width)
        xt_ref[0, pl.ds(start, width), :] = piece[0]
    bias = jnp.transpose(jnp.broadcast_to(b_ref[0:1, :], (128, width)))[:, 0:1]
    bias_v = jnp.transpose(jnp.broadcast_to(b_ref[1:2, :], (128, width)))[:, 0:1]
    packed = dot_tn(w_ref[:, : 3 * width], xt_ref[0])
    qkv_ref[0, 0] = (packed[:width] + bias).astype(BF)
    qkv_ref[0, 1] = packed[width : 2 * width].astype(BF)
    qkv_ref[0, 2] = (packed[2 * width :] + bias_v).astype(BF)
    mine = pl.ds(pl.multiple_of(core * half, half), half)
    other = pl.ds(pl.multiple_of((1 - core) * half, half), half)
    xh_ref[0] = jnp.transpose(xt_ref[0, :, mine])
    row = seg_ref[pl.ds(pl.program_id(0), 1), :].astype(F32)
    column = jnp.transpose(jnp.broadcast_to(row, (128, slots)))[:, 0:1]
    scale = 1.0 / (size**0.5)
    for block in range(2):
        rows = slice(block * half, (block + 1) * half)
        allowed = column[rows] == row
        for h in range(heads):
            feats = slice(h * size, (h + 1) * size)
            scores = dot_tn(qkv_ref[0, 0, feats, rows], qkv_ref[0, 1, feats, :]) * scale
            scores = scores + prev_ref[0, h, rows, :].astype(F32)
            raw_ref[0, h, rows, :] = scores.astype(BF)
            masked = jnp.where(allowed, scores, NEG)
            expanded = jnp.exp(masked - jnp.max(masked, axis=-1, keepdims=True))
            prob = expanded * (1.0 / jnp.sum(expanded, axis=-1, keepdims=True))
            prob = prob.astype(BF)
            p_ref[0, h, rows, :] = prob
            o_scr[feats, rows] = dot_nt(qkv_ref[0, 2, feats, :], prob).astype(BF)
    own_ref[0] = o_scr[:, mine]
    oth_ref[0] = o_scr[:, other]


def up_kernel(
    me_ref, o0, o1, o2, o3, wo0, wo1, wo2, wo3, big_a, big_b, xh_ref, bias_ref, gain_ref, shift_ref,
    b_up_a, b_up_b,
    n1_ref, r1_ref, x1_ref, ga_ref, gb_ref, gpa_ref, gpb_ref, part_ref,
):
    units = b_up_a.shape[1]
    w1a, w1b = big_a.at[:, :units], big_b.at[:, :units]
    w2a, w2b = big_a.at[:, units : 2 * units], big_b.at[:, units : 2 * units]
    total = xh_ref[0].astype(F32) + bias_ref[0:1, :]
    for left, right in ((o0, wo0), (o1, wo1), (o2, wo2), (o3, wo3)):
        total = total + dot_nt(jnp.transpose(left[0]), right[...])
    normed, inv_std = ln_stats(total)
    n1_ref[0] = normed
    r1_ref[0] = jnp.broadcast_to(inv_std, r1_ref.shape[1:])
    x1_ref[0] = (normed * gain_ref[0:1, :] + shift_ref[0:1, :]).astype(BF)
    block = 256

    def one_block(step, carry):
        lanes = pl.ds(pl.multiple_of(step * block, block), block)
        sides = ((w1a, b_up_a, ga_ref, gpa_ref), (w1b, b_up_b, gb_ref, gpb_ref))
        for w1, b_up, g_ref, gp_ref in sides:
            hidden = dot(x1_ref[0], w1[:, lanes]) + b_up[:, lanes]
            cdf = 0.5 * (1.0 + lax.erf(hidden * (0.5**0.5)))
            pdf = jnp.exp(-0.5 * hidden * hidden) * 0.3989422804014327
            g_ref[0, :, lanes] = (hidden * cdf).astype(BF)
            gp_ref[0, :, lanes] = (cdf + hidden * pdf).astype(BF)
        return carry

    lax.fori_loop(0, units // block, one_block, 0)
    part_ref[0] = (dot_nt(ga_ref[0], w2a[...]) + dot_nt(gb_ref[0], w2b[...])).astype(BF)


def down_kernel(
    me_ref, n1_ref, pa_ref, pb_ref, dy0, dy1, dy2, dy3, bias_ref, gain_ref, shift_ref,
    big_a, big_b, gpa_ref, gpb_ref,
    act_own_ref, act_oth_ref, ds_ref, dsb_ref, da_ref, db_ref, vec_ref, bup_a_ref, bup_b_ref, part_ref,
    scr,
):
    me = me_ref[0]
    width = dy0.shape[1]
    units = gpa_ref.shape[2]
    w1a, w1b = big_a.at[:, :units], big_b.at[:, :units]
    w2a, w2b = big_a.at[:, units : 2 * units], big_b.at[:, units : 2 * units]
    branch = pa_ref[0].astype(F32) + pb_ref[0].astype(F32)
    first_out = n1_ref[0] * gain_ref[0:1, :] + shift_ref[0:1, :]
    normed, inv_std = ln_stats(first_out + branch + bias_ref[1:2, :])
    gain = gain_ref[1:2, :]
    scr[...] = jnp.transpose(normed * gain + shift_ref[1:2, :])
    for step, out in ((0, act_own_ref), (1, act_oth_ref)):
        start = pl.multiple_of(place_of(me, step) * width, width)
        out[0] = scr[pl.ds(start, width), :].astype(BF)
    for step, piece in enumerate((dy0, dy1, dy2, dy3)):
        start = pl.multiple_of(place_of(me, step) * width, width)
        scr[pl.ds(start, width), :] = piece[0].astype(F32)
    grad = jnp.transpose(scr[...])
    inner = ln_back(grad, normed, inv_std, gain)
    ds_ref[0] = inner
    vec_ref[0, 0:1, :] = jnp.sum(grad * normed, axis=0, keepdims=True)
    vec_ref[0, 1:2, :] = jnp.sum(grad, axis=0, keepdims=True)
    vec_ref[0, 2:3, :] = jnp.sum(inner, axis=0, keepdims=True)
    dsb_ref[0] = inner.astype(BF)
    block = 256

    def one_block(step, carry):
        lanes = pl.ds(pl.multiple_of(step * block, block), block)
        sides = ((w2a, da_ref, gpa_ref, bup_a_ref), (w2b, db_ref, gpb_ref, bup_b_ref))
        for w2, dh_ref, gp_ref, bup_ref in sides:
            grad_hidden = dot(dsb_ref[0], w2[:, lanes]) * gp_ref[0, :, lanes].astype(F32)
            bup_ref[0, 0:1, lanes] = jnp.sum(grad_hidden, axis=0, keepdims=True)
            dh_ref[0, :, lanes] = grad_hidden.astype(BF)
        return carry

    lax.fori_loop(0, units // block, one_block, 0)
    part_ref[0] = (dot_nt(da_ref[0], w1a[...]) + dot_nt(db_ref[0], w1b[...])).astype(BF)


def mid_kernel(
    me_ref, ds_ref, pa_ref, pb_ref, n1_ref, r1_ref, gain_ref, wo0, wo1,
    dsb_ref, vec_ref, do_own_ref, do_oth_ref, near_ref, scr,
):
    chip = me_ref[0] // 2
    width = do_own_ref.shape[1]
    grad = ds_ref[0] + (pa_ref[0].astype(F32) + pb_ref[0].astype(F32))
    normed = n1_ref[0]
    inner = ln_back(grad, normed, r1_ref[0, :, 0:1], gain_ref[0:1, :])
    vec_ref[0, 0:1, :] = jnp.sum(grad * normed, axis=0, keepdims=True)
    vec_ref[0, 1:2, :] = jnp.sum(grad, axis=0, keepdims=True)
    vec_ref[0, 2:3, :] = jnp.sum(inner, axis=0, keepdims=True)
    dsb = inner.astype(BF)
    dsb_ref[0] = dsb
    scr[...] = inner
    chip_lanes = pl.ds(pl.multiple_of(chip * 2 * width, 128), 2 * width)
    near_ref[0] = jnp.transpose(scr[:, chip_lanes])
    do_own_ref[0] = jnp.transpose(dot(dsb, wo0[...])).astype(BF)
    do_oth_ref[0] = jnp.transpose(dot(dsb, wo1[...])).astype(BF)


def back_kernel(
    heads, me_ref, p_ref, qkv_ref, do_own_ref, do_oth_ref, w_ref, near_ref,
    lg_ref, dqkv_ref, e0, e1, e2, e3, vec_ref, do_scr, dx_scr, sum_scr,
):
    me = me_ref[0]
    core, chip = lax.rem(me, 2), me // 2
    width, slots = qkv_ref.shape[2], qkv_ref.shape[3]
    half = slots // 2
    size = width // heads
    mine = pl.ds(pl.multiple_of(core * half, half), half)
    other = pl.ds(pl.multiple_of((1 - core) * half, half), half)
    do_scr[:, mine] = do_own_ref[0]
    do_scr[:, other] = do_oth_ref[0]
    scale = 1.0 / (size**0.5)
    def one_head(h, carry):
        feats = pl.ds(pl.multiple_of(h * size, size), size)
        query, key, value = (qkv_ref[0, part, feats, :] for part in range(3))
        out_grad = do_scr[feats, :]
        for block in range(2):
            rows = slice(block * half, (block + 1) * half)
            prob = p_ref[0, h, rows, :].astype(F32)
            grad_prob = dot_tn(do_scr[feats, rows], value)
            weighted = grad_prob * prob
            inner = jnp.sum(weighted, axis=-1, keepdims=True)
            lg_ref[0, h, rows, :] = (weighted - prob * inner).astype(BF)
        grad_query = dot_nt(key, lg_ref[0, h]) * scale
        grad_key = dot(query, lg_ref[0, h]) * scale
        grad_value = dot(out_grad, p_ref[0, h])
        for number, grad in ((0, grad_query), (1, grad_value)):
            line = jnp.sum(grad, axis=1, keepdims=True)
            sum_scr[number, feats, :] = jnp.broadcast_to(line, (size, 128))
        dqkv_ref[0, feats, :] = grad_query.astype(BF)
        dqkv_ref[0, pl.ds(pl.multiple_of(width + h * size, size), size), :] = grad_key.astype(BF)
        dqkv_ref[0, pl.ds(pl.multiple_of(2 * width + h * size, size), size), :] = grad_value.astype(BF)
        return carry

    lax.fori_loop(0, heads, one_head, 0)
    for number in range(2):
        vec_ref[0, number : number + 1, :] = jnp.transpose(sum_scr[number])[0:1, :]
    dx_scr[...] = dot(w_ref[:, : 3 * width], dqkv_ref[0])
    near = pl.ds(pl.multiple_of(chip * 2 * width, width), 2 * width)
    dx_scr[near, mine] = dx_scr[near, mine] + near_ref[0]
    for step, out in enumerate((e0, e1, e2, e3)):
        start = pl.multiple_of(place_of(me, step) * width, width)
        out[0] = dx_scr[pl.ds(start, width), :].astype(BF)


def ffn_grad_kernel(count, bit, me_ref, *rest):
    lefts, rights = rest[:count], rest[count : 2 * count]
    keep_ref, send_ref, scr = rest[2 * count :]
    side = me_ref[2 + bit]
    total = None
    for left, right in zip(lefts, rights):
        a = left[...].reshape(-1, left.shape[-1])
        b = right[...].reshape(-1, right.shape[-1])
        product = dot_tn(a, b)
        total = product if total is None else total + product
    part = keep_ref.shape[0]
    scr[...] = total
    keep_ref[...] = scr[pl.ds(pl.multiple_of(side * part, part), part), :].astype(BF)
    send_ref[...] = scr[pl.ds(pl.multiple_of((1 - side) * part, part), part), :].astype(BF)


def qkv_grad_kernel(count, me_ref, *rest):
    groups = [rest[i * count : (i + 1) * count] for i in range(6)]
    small_ref, came_ref, *bqv, keep_ref, send_ref, scr = rest[6 * count :]
    side = me_ref[2]
    width = bqv[0].shape[2]
    line = lax.broadcasted_iota(jnp.int32, small_ref.shape, 0)
    small = small_ref[...]
    scr[:8, :] = jnp.where(line < 6, (small + came_ref[...]) * 0.5, small)
    total = functools.reduce(jnp.add, [b[0] for b in bqv])
    scr[7:8, :width] = total[0:1, :]
    scr[7:8, width : 2 * width] = total[1:2, :]
    halves = as_halves(scr[:8, :])
    total = None
    for x, grad in zip(groups[0], groups[1]):
        for index in range(grad.shape[0]):
            product = dot_nt(grad[index], x[index])
            total = product if total is None else total + product
    used = total.shape[0]
    scr[:used, :] = total
    total = None
    for lefts, rights in ((groups[2], groups[3]), (groups[4], groups[5])):
        for left, right in zip(lefts, rights):
            for index in range(left.shape[0]):
                product = dot(left[index], right[index])
                total = product if total is None else total + product
    scr[used:, :] = total
    part = scr.shape[0] // 2
    for out, half in ((keep_ref, side), (send_ref, 1 - side)):
        place = pl.ds(pl.multiple_of(half * part, part), part)
        out[:part, :] = scr[place, :].astype(BF)
        out[part:, :] = halves


def halve_kernel(bit, tail, me_ref, *rest):
    count = (len(rest) - 2) // 2
    keep_ref, send_ref = rest[-2:]
    side = me_ref[2 + bit]
    rows = (rest[0].shape[0] - tail) // 2
    for number in range(count):
        kept, came = rest[2 * number], rest[2 * number + 1]
        for out, half in ((keep_ref, side), (send_ref, 1 - side)):
            place = pl.ds(pl.multiple_of(half * rows, rows), rows)
            total = kept[place, :].astype(F32) + came[place, :].astype(F32)
            out[number * rows : (number + 1) * rows, :] = total.astype(BF)
    if tail:
        both = as_halves(from_halves(kept[2 * rows :, :]) + from_halves(came[2 * rows :, :]))
        keep_ref[rows:, :] = both
        send_ref[rows:, :] = both


def last_kernel(me_ref, kept, came, out_ref, small_ref):
    rows = out_ref.shape[0]
    out_ref[...] = (kept[:rows, :].astype(F32) + came[:rows, :].astype(F32)).astype(BF)
    small_ref[...] = from_halves(kept[rows:, :]) + from_halves(came[rows:, :])


def finish_kernel(steps, pair, me_ref, *rest):
    count = len(steps)
    blocks, outs = rest[:count], rest[count:]
    rows = blocks[0].shape[0]
    for number, back in enumerate(steps):
        group = group_at(me_ref, back, count)
        bits = lax.rem(group, 2), lax.rem(group // 2, 2), group // 4
        index = bits[0] * 4 + bits[1] * 2 + bits[2]
        if pair:
            part = rows // 2
            other = bits[1] * 4 + bits[0] * 2 + bits[2]
            for out, place, low in ((outs[0], index, 0), (outs[1], other, part)):
                place = pl.ds(pl.multiple_of(place * part, part), part)
                out[place, :] = blocks[number][low : low + part, :].astype(F32)
            continue
        block = blocks[number][...].astype(F32)
        before = 0
        for out in outs:
            held = out.shape[0] // rows

            @pl.when((index >= before) & (index < before + held))
            def _():
                out[pl.ds(pl.multiple_of((index - before) * rows, rows), rows), :] = block

            before += held


def ring_place(group, groups):
    return jnp.where(lax.rem(group, 2) == 0, group // 2, groups - 1 - group // 2)


def group_at(me_ref, back, count):
    there = lax.rem(ring_place(me_ref[1], count) + count - back, count)
    return jnp.where(there < count // 2, 2 * there, 2 * (count - 1 - there) + 1)


def pairs_kernel(me_ref, *rest):
    count = len(rest) - 3
    blocks, out_a, out_b, sems = rest[:count], rest[-3], rest[-2], rest[-1]
    core = lax.rem(me_ref[0], 2)
    rows = blocks[0].shape[0] // 2
    copies = []
    for number in range(count):
        steps = number if number <= count // 2 else number - count // 2
        ahead = core if number <= count // 2 else 1 - core
        back = jnp.where(ahead == 1, lax.rem(count - steps, count), steps)
        place = pl.ds(pl.multiple_of(group_at(me_ref, back, count) * rows, rows), rows)
        first, second = (out_a, out_b) if number <= count // 2 else (out_b, out_a)
        for part, out in enumerate((first, second)):
            copies.append(
                pltpu.make_async_copy(
                    blocks[number].at[pl.ds(part * rows, rows), :],
                    out.at[place, :],
                    sems.at[number, part],
                )
            )
    for copy in copies:
        copy.start()
    for copy in copies:
        copy.wait()


def small_kernel(me_ref, vec1, vec2, bup_a, bup_b, own_ref, oth_ref):
    own_ref[...] = jnp.zeros_like(own_ref)
    oth_ref[...] = jnp.zeros_like(oth_ref)
    for low, vec in ((0, vec1), (3, vec2)):
        total = jnp.sum(vec[...], axis=0)
        own_ref[low : low + 3, :] = total
        oth_ref[low : low + 3, :] = total
    own_ref[6:7, :] = jnp.sum(bup_a[...], axis=0)
    oth_ref[6:7, :] = jnp.sum(bup_b[...], axis=0)


def as_halves(value):
    high = value.astype(BF).astype(F32)
    return jnp.concatenate([high, value - high], 0).astype(BF)


def from_halves(both):
    both = both.astype(F32)
    return both[:8] + both[8:]


def whole(array):
    shape = array.shape
    return pl.BlockSpec(shape, lambda i, s: (0,) * len(shape))


def held(array):
    return pl.BlockSpec(memory_space=pltpu.VMEM)


def by_row(array, first=0):
    shape = array.shape
    rest = (0,) * (len(shape) - 1)
    return pl.BlockSpec((1,) + shape[1:], lambda i, s: (first + i,) + rest)


def on_row(row, rowed, skip, kernel):
    def inner(*refs):
        kernel(*[
            ref.at[pl.ds(row, 1)] if number in rowed else ref
            for number, ref in enumerate(refs)
            if number not in skip
        ])

    return inner


def call(kernel, grid, ins, outs, out_specs, scratch, name, micros, alias=None, room=32):
    flops = int(micros * 10)
    return pl.pallas_call(
        kernel,
        out_shape=outs,
        grid_spec=pltpu.PrefetchScalarGridSpec(
            num_scalar_prefetch=1,
            grid=grid,
            in_specs=[spec for _, spec in ins[1:]],
            out_specs=out_specs,
            scratch_shapes=scratch,
        ),
        input_output_aliases=alias or {},
        compiler_params=pltpu.CompilerParams(vmem_limit_bytes=room << 20),
        cost_estimate=pl.CostEstimate(flops=flops, bytes_accessed=1, transcendentals=0),
        name=name,
    )(*[a for a, _ in ins])


def body(
    tokens, cotangent, prev_logits, segment_ids, w_qkv, b_qv, w_out, w_up, b_up, w_down,
    biases, gains, shifts,
):
    rows, slots, width = tokens.shape
    full = width * lax.axis_size("tensor")
    groups = lax.axis_size("dp")
    near_dp = groups == 8
    heads = prev_logits.shape[1]
    half = slots // 2
    units = w_up.shape[1]
    me = lax.axis_index("tensor").astype(jnp.int32)
    dp = lax.axis_index("dp").astype(jnp.int32)
    me_ref = jnp.stack([me, dp, lax.rem(dp, 2), lax.rem(dp // 2, 2), dp // 4])
    core = lax.rem(me, 2)
    sds = jax.ShapeDtypeStruct

    def after(value, *others):
        return lax.optimization_barrier((value, others))[0]

    together = lax.optimization_barrier

    def pp(array, step):
        return lax.ppermute(array, "tensor", [(i, i ^ step) for i in range(4)])

    def swap(array, bit):
        return lax.ppermute(array, "dp", [(i, i ^ (1 << bit)) for i in range(groups)])

    order = list(range(0, groups, 2)) + list(range(groups - 1, 0, -2))
    onward = [(order[i], order[(i + 1) % groups]) for i in range(groups)]
    backward = [(b, a) for a, b in onward]

    ring_steps = [0]
    for step in range(1, groups // 2):
        ring_steps += [step, groups - step]
    ring_steps += [groups // 2]

    def ring_step(ahead, behind):
        return lax.ppermute(ahead, "dp", onward), lax.ppermute(behind, "dp", backward)

    def place_pairs(blocks):
        outs = [sds((full, blocks[0].shape[1]), BF)] * 2
        return call(
            pairs_kernel, (1,),
            [(me_ref, None)] + [(b, held(b)) for b in blocks], outs, [held(o) for o in outs],
            [pltpu.SemaphoreType.DMA((groups, 2))], "pairs", 2, None, 8,
        )

    both_ways = []
    for i, j in onward:
        both_ways += [(i * 4 + t, j * 4 + t) if t % 2 == 0 else (j * 4 + t, i * 4 + t) for t in range(4)]

    def pair_step(pair):
        return lax.ppermute(pair, ("dp", "tensor"), both_ways)

    tokens = jnp.swapaxes(tokens, 1, 2)
    cotangent = jnp.swapaxes(cotangent, 1, 2)
    shard_in = w_qkv.astype(BF).reshape(w_qkv.shape[0], 3 * width)
    x_y = pp(tokens, 2)
    x_c = pp(tokens, 1)
    shard_in = jnp.concatenate([shard_in, w_out.T.astype(BF)], 1)
    shard_big = jnp.concatenate([w_up.astype(BF), w_down.T.astype(BF)], 1)
    if near_dp:
        pair_big = jnp.concatenate([shard_big, pp(shard_big, 1)], 0)
        ring = [ring_step(shard_in, shard_in)]
        ring.append(ring_step(*together(ring[-1])))
        ring.append(ring_step(*together(ring[-1])))
        last = lax.ppermute(together(ring[-1])[0], "dp", onward)
        pair_big = after(pair_big, last)
        came = [pair_step(pair_big)]
        pieces_in = [shard_in, *ring[0], *ring[1], *ring[2], last]
    else:
        pieces_in = [lax.all_gather(shard_in, "dp", axis=0, tiled=True)]
        big_a = lax.all_gather(shard_big, "dp", axis=0, tiled=True)
    x_d = pp(x_y, 1)
    x_pieces = (tokens, x_c, x_y, x_d)
    cot = after(cotangent, x_y)
    dy_mine = lax.dynamic_slice_in_dim(cot, core * half, half, 2)
    dy_other = lax.dynamic_slice_in_dim(cot, (1 - core) * half, half, 2)
    dy1, dy2, dy3 = pp(dy_other, 1), pp(dy_mine, 2), pp(dy_other, 3)
    b_up_a = b_up.reshape(1, units)
    b_up_b = pp(b_up_a, 1)

    sds3 = lambda *shape_type: sds((rows,) + shape_type[:-1], shape_type[-1])

    class Stage:
        def __init__(self, kernel, fulls, parts, scratch, name, room, far=()):
            self.kernel, self.fulls, self.parts, self.scratch = kernel, fulls, parts, scratch
            self.name, self.room, self.far, self.kept = name, room, far, None

        def step(self, row, given):
            fulls, far = self.fulls, self.far
            ins = [(me_ref, None)]
            ins += [(a, held(a) if isinstance(k, str) else k) for a, k in given]
            rowed = {1 + i for i, (_, k) in enumerate(given) if isinstance(k, str) and k == "row"}
            low, alias = len(ins), {}
            if self.kept is not None:
                alias = {low + i: i for i in range(len(fulls))}
                ins += [
                    (k, pl.BlockSpec(memory_space=pl.ANY) if i in far else held(k))
                    for i, k in enumerate(self.kept)
                ]
            base = len(ins)
            outs = list(fulls) + list(self.parts)
            specs = [by_row(o, row) if i in far else held(o) for i, o in enumerate(fulls)]
            specs += [held(o) for o in self.parts]
            rowed |= {base + i for i in range(len(fulls)) if i not in far}
            result = call(
                on_row(row, rowed, set(alias), self.kernel), (1,), ins, outs, specs,
                self.scratch, self.name, 1, alias, self.room,
            )
            self.kept = result[: len(fulls)]
            return result[len(fulls) :]

    ins = [(me_ref, None)] + [(p, by_row(p)) for p in x_pieces]
    ins += [(b_qv, whole(b_qv)), (prev_logits, by_row(prev_logits))]
    ins += [(segment_ids, whole(segment_ids))] + [(b, whole(b)) for b in pieces_in]
    outs = [
        sds(prev_logits.shape, BF),
        sds(prev_logits.shape, BF),
        sds3(3, width, slots, BF),
        sds3(width, half, BF),
        sds3(width, half, BF),
        sds3(full, slots, BF),
        sds3(half, full, BF),
        sds((full, full), BF),
    ]
    raw, prob, qkv, o_own, o_oth, xt, xh, w_in = call(
        functools.partial(attend_kernel, heads, ring_steps if near_dp else [0]), (rows,), ins,
        outs, [by_row(o) for o in outs[:-1]] + [held(outs[-1])],
        [pltpu.VMEM((width, slots), BF)], "attend", 1, None, 48,
    )
    o1, o2, o3 = pp(o_oth, 1), pp(o_own, 2), pp(o_oth, 3)
    wo0 = w_in[:, 3 * width :]
    wo2 = pp(wo0, 2)
    wo1, wo3 = pp(wo0, 1), pp(wo2, 1)
    if near_dp:
        came.append(pair_step(after(came[0], o_own, dy1, dy2, dy3)))
        came.append(pair_step(after(came[1], o2)))
        came.append(pair_step(after(came[2], o1, o3)))
        big_a, big_b = place_pairs(
            [pair_big, *came[:3], after(came[3], wo2), *[pp(b, 1) for b in came[:3]]]
        )
    else:
        big_a = after(big_a, o_own)
        big_b = pp(big_a, 1)

    one = (1, half, full)
    up = Stage(
        up_kernel,
        [
            sds3(half, full, F32), sds3(half, 128, F32), sds3(half, full, BF),
            sds3(half, units, BF), sds3(half, units, BF), sds3(half, units, BF), sds3(half, units, BF),
        ],
        [sds(one, BF)], [], "up", 16,
    )
    part, part_y = [], []
    for row in range(rows):
        given = [(o, "row") for o in (o_own, o1, o2, o3)]
        given += [(w, "all") for w in (wo0, wo1, wo2, wo3, big_a, big_b)] + [(xh, "row")]
        given += [(w, "all") for w in (biases, gains, shifts, b_up_a, b_up_b)]
        part += up.step(row, given)
        part_y.append(pp(part[row], 2))
    n1, r1, x1, ga, gb, gpa, gpb = up.kept
    gc, x1_c = pp(gb, 1), pp(x1, 1)

    down = Stage(
        down_kernel,
        [
            sds3(width, half, BF), sds3(width, half, BF), sds3(half, full, F32),
            sds3(half, full, BF), sds3(half, units, BF), sds3(half, units, BF),
            sds3(3, full, F32), sds3(1, units, F32), sds3(1, units, F32),
        ],
        [sds(one, BF)], [pltpu.VMEM((full, half), F32)], "down", 16,
    )
    part2, part2_y = [], []
    for row in range(rows):
        got = after(part_y[row], part2_y[0]) if row == 2 else part_y[row]
        given = [(n1, "row"), (part[row], "all"), (got, "all")]
        given += [(d, "row") for d in (dy_mine, dy1, dy2, dy3)]
        given += [(w, "all") for w in (biases, gains, shifts, big_a, big_b)]
        given += [(gpa, "row"), (gpb, "row")]
        part2 += down.step(row, given)
        part2_y.append(pp(part2[row], 2))
    act_own, act_oth, ds2, ds2b, da, db, vec2, bup_a, bup_b = down.kept
    ds2b_c, dc = pp(ds2b, 1), pp(db, 1)

    def ffn_grad(lefts, rights, bit):
        block = 256
        def part(a):
            return pl.BlockSpec(a.shape[:2] + (block,), lambda i, s: (0, 0, i))
        ins = [(me_ref, None)] + [(a, whole(a)) for a in lefts] + [(a, part(a)) for a in rights]
        across, down = rights[0].shape[-1], lefts[0].shape[-1]
        outs = [sds((down // 2, across), BF)] * 2
        specs = [pl.BlockSpec((down // 2, block), lambda i, s: (0, i))] * 2
        return call(
            functools.partial(ffn_grad_kernel, len(lefts), bit),
            (across // block,), ins, outs, specs, [pltpu.VMEM((down, block), F32)], "ffn_grad", 3,
        )

    def halve(bit, *pairs, tail=0):
        down, across = pairs[0][0].shape
        outs = [sds((len(pairs) * (down - tail) // 2 + tail, across), BF)] * 2
        ins = [(me_ref, None)] + [(a, whole(a)) for pair in pairs for a in pair]
        return call(
            functools.partial(halve_kernel, bit, tail), (1,), ins, outs, [whole(o) for o in outs], [],
            "halve", 1,
        )

    def added(keep, got):
        return (keep.astype(F32) + got.astype(F32)).astype(BF)

    def finish(blocks, outs, pair=False):
        return call(
            functools.partial(finish_kernel, ring_steps, pair), (1,),
            [(me_ref, None)] + [(b, whole(b)) for b in blocks],
            outs, [whole(o) for o in outs], [], "finish", 2,
        )

    def whole_of(keep, send, bit):
        low = jnp.where(lax.rem(dp >> bit, 2) == 0, keep, send)
        high = jnp.where(lax.rem(dp >> bit, 2) == 0, send, keep)
        return jnp.concatenate([low, high], 0)

    mid = Stage(
        mid_kernel, [sds3(half, full, BF), sds3(3, full, F32)],
        [sds((1, width, half), BF)] * 2 + [sds((1, 2 * width, half), F32)],
        [pltpu.VMEM((half, full), F32)], "mid", 16,
    )
    back = Stage(
        functools.partial(back_kernel, heads),
        [sds(prev_logits.shape, BF), sds3(3 * width, slots, BF)] + [sds3(width, slots, BF)] * 4,
        [sds((1, 2, width), F32)],
        [pltpu.VMEM((width, slots), BF), pltpu.VMEM((full, slots), F32), pltpu.VMEM((2, width, 128), F32)],
        "back", 32, (0,),
    )

    def mid_step(row, *earlier):
        given = [(ds2, "row"), (part2[row], "all"), (after(part2_y[row], *earlier), "all")]
        given += [(n1, "row"), (r1, "row"), (gains, "all"), (wo0, "all"), (wo1, "all")]
        own, oth, near = mid.step(row, given)
        return own, pp(oth, 1), near

    def back_step(row, held_by, *earlier):
        own, got, near = held_by
        given = [(prob, by_row(prob, row)), (qkv, by_row(qkv, row)), (own, "all")]
        given += [(after(got, *earlier), "all"), (w_in, "all"), (near, "all")]
        return back.step(row, given)[0]

    keep_d, send_d = ffn_grad((ga, gc), (ds2b, ds2b_c), 0)
    mids = [mid_step(0)]
    keep_u, send_u = ffn_grad((x1, x1_c), (da, dc), 1)
    mids.append(mid_step(1, keep_d, keep_u, mids[0][0]))
    sums = [back_step(0, mids[0], mids[1][0]), back_step(1, mids[1])]
    if near_dp:
        got_d, got_u = (swap(after(g, mids[1][0]), b) for g, b in ((send_d, 0), (send_u, 1)))
        mids.append(mid_step(2, sums[1], got_d, got_u))
        keep_d, send_d = halve(1, (keep_d, after(got_d, mids[2][0])))
        keep_u, send_u = halve(0, (keep_u, got_u))
        got_d, got_u = swap(send_d, 1), swap(send_u, 0)
        sums.append(back_step(2, mids[2], keep_d, keep_u))
    else:
        mids.append(mid_step(2, sums[1]))
        grad_down, grad_up = lax.psum((whole_of(keep_d, send_d, 0), whole_of(keep_u, send_u, 1)), "dp")
        grad_down, grad_up = grad_down.astype(F32), grad_up.astype(F32)
        sums.append(back_step(2, mids[2]))
    ds1b, vec1 = mid.kept
    ds1b_c = pp(ds1b, 1)
    ins = [(me_ref, None)] + [(a, whole(a)) for a in (vec1, vec2, bup_a, bup_b)]
    outs = [sds((8, full), F32)] * 2
    small, other = call(small_kernel, (1,), ins, outs, [whole(o) for o in outs], [], "small", 1)
    small = small + pp(other, 1)
    small_y = pp(small, 2)
    lg, dqkv, e0, e1, e2, e3 = back.kept

    ins = [(me_ref, None)] + [(a, whole(a)) for a in (xt, dqkv, o_own, ds1b, o_oth, ds1b_c)]
    ins += [(a, whole(a)) for a in (small, small_y, *sums)]
    outs = [sds((full // 2 + 16, full), BF)] * 2
    keep, send = call(
        functools.partial(qkv_grad_kernel, 1), (1,), ins, outs, [whole(o) for o in outs],
        [pltpu.VMEM((full, full), F32)], "qkv_grad", 4,
    )

    if near_dp:
        got = swap(send, 0)
        keep_du, send_du = halve(2, (keep_d, after(got_d, send)), (keep_u, got_u))
        got_du = swap(send_du, 2)
        keep, send = halve(1, (keep, got), tail=16)
        got = swap(send, 1)
        pair = added(keep_du, got_du)
        ring_u = [ring_step(pair, pair)]
        keep, send = halve(2, (keep, got), tail=16)
        got = swap(send, 2)
        ring_u.append(ring_step(*together(ring_u[-1])))
        outs = [sds((full // 8, full), BF), sds((8, full), F32)]
        total, small = call(
            last_kernel, (1,), [(me_ref, None), (keep, whole(keep)), (got, whole(got))], outs,
            [whole(o) for o in outs], [], "last", 1,
        )
        ring = [ring_step(total, total)]
        ring_u.append(ring_step(*together(ring_u[-1])))
        ring.append(ring_step(*together(ring[-1])))
        last_u = lax.ppermute(ring_u[-1][0], "dp", onward)
        ring.append(ring_step(*together(ring[-1])))
        last = lax.ppermute(ring[-1][0], "dp", onward)
        grad_down, grad_up = finish(
            [after(pair, *ring[2]), *ring_u[0], *ring_u[1], *ring_u[2], last_u],
            [sds((units, full), F32), sds((full, units), F32)], True,
        )
        grad_in, grad_out = finish(
            [total, *ring[0], *ring[1], *ring[2], last],
            [sds((3 * width, full), F32), sds((width, full), F32)],
        )
    else:
        part = full // 2
        tail = lax.psum(whole_of(keep[:part], send[:part], 0), "dp").astype(F32)
        small = lax.psum(keep[part : part + 8].astype(F32) + keep[part + 8 :].astype(F32), "dp")
        grad_in, grad_out = tail[: 3 * width], tail[3 * width :]
    grad_b_up = small[6]
    grad_b_qv = small[7, : 2 * width].reshape(2, width)

    grad_in = jnp.transpose(grad_in.reshape(3, width, full), (2, 0, 1))

    act_c = pp(act_oth, 1)
    block_out = jnp.concatenate(
        [jnp.where(core == 0, act_own, act_c), jnp.where(core == 0, act_c, act_own)], 2
    )
    near_sum = e2.astype(F32) + pp(e3, 1).astype(F32)
    far = pp(near_sum.astype(BF), 2).astype(F32)
    grad_x = (e0.astype(F32) + pp(e1, 1).astype(F32) + far).astype(BF)
    return (
        jnp.swapaxes(block_out, 1, 2),
        raw,
        jnp.swapaxes(grad_x, 1, 2),
        lg,
        grad_in,
        grad_b_qv,
        grad_out,
        grad_up,
        grad_b_up,
        grad_down,
        jnp.stack([small[2], small[5]]),
        jnp.stack([small[0], small[3]]),
        jnp.stack([small[1], small[4]]),
    )


def solution(mesh):
    placed = (
        P("dp", None, "tensor"),
        P("dp", None, "tensor"),
        P("dp", "tensor", None, None),
        P("dp", None),
        P("dp", None, "tensor"),
        P(None, "tensor"),
        P("tensor", "dp"),
        P("dp", "tensor"),
        P("tensor"),
        P("tensor", "dp"),
        P(),
        P(),
        P(),
    )
    return jax.shard_map(
        body,
        mesh=mesh,
        in_specs=placed,
        out_specs=(
            P("dp", None, "tensor"),
            P("dp", "tensor", None, None),
            P("dp", None, "tensor"),
            P("dp", "tensor", None, None),
            P(None, None, "tensor"),
            P(None, "tensor"),
            P("tensor", None),
            P(None, "tensor"),
            P("tensor"),
            P("tensor", None),
            P(),
            P(),
            P(),
        ),
        check_vma=False,
    )
```

```python
import functools

import jax
import jax.numpy as jnp
from jax import lax
from jax.experimental import pallas as pl
from jax.experimental.pallas import tpu as pltpu
from jax.sharding import PartitionSpec as P

EPS = 1e-06
NEG = -1e30
BF = jnp.bfloat16
F32 = jnp.float32


def dot(a, b):
    return lax.dot_general(a, b, (((1,), (0,)), ((), ())), preferred_element_type=F32)


def dot_nt(a, b):
    return lax.dot_general(a, b, (((1,), (1,)), ((), ())), preferred_element_type=F32)


def dot_tn(a, b):
    return lax.dot_general(a, b, (((0,), (0,)), ((), ())), preferred_element_type=F32)


def place_of(me, step):
    core, chip = lax.rem(me, 2), me // 2
    core = 1 - core if step % 2 else core
    chip = 1 - chip if step // 2 else chip
    return 2 * chip + core


def ln_stats(summed):
    row_mean = jnp.mean(summed, axis=-1, keepdims=True)
    centered = summed - row_mean
    inv_std = lax.rsqrt(jnp.mean(centered * centered, axis=-1, keepdims=True) + EPS)
    return centered * inv_std, inv_std


def ln_back(grad, normed, inv_std, gain):
    scaled = grad * gain
    inner = (
        scaled
        - jnp.mean(scaled, axis=-1, keepdims=True)
        - normed * jnp.mean(scaled * normed, axis=-1, keepdims=True)
    )
    return inner * inv_std


def attend_kernel(
    heads, steps, me_ref, x0, x1, x2, x3, b_ref, prev_ref, seg_ref, *rest
):
    count = len(steps)
    blocks = rest[:count]
    raw_ref, p_ref, qkv_ref, own_ref, oth_ref, xt_ref, xh_ref, w_ref, o_scr = rest[count:]

    @pl.when(pl.program_id(0) == 0)
    def _():
        rows = blocks[0].shape[0]
        for block, back in zip(blocks, steps):
            group = group_at(me_ref, back, count) if count > 1 else 0
            w_ref[pl.ds(pl.multiple_of(group * rows, rows), rows), :] = block[...]

    me = me_ref[0]
    core = lax.rem(me, 2)
    width, slots = x0.shape[1], x0.shape[2]
    half = slots // 2
    size = width // heads
    for step, piece in enumerate((x0, x1, x2, x3)):
        start = pl.multiple_of(place_of(me, step) * width, width)
        xt_ref[0, pl.ds(start, width), :] = piece[0]
    bias = jnp.transpose(jnp.broadcast_to(b_ref[0:1, :], (128, width)))[:, 0:1]
    bias_v = jnp.transpose(jnp.broadcast_to(b_ref[1:2, :], (128, width)))[:, 0:1]
    packed = dot_tn(w_ref[...], xt_ref[0])
    scale = 1.0 / (size**0.5)
    qkv_ref[0, 0] = ((packed[:width] + bias).astype(BF).astype(F32) * scale).astype(BF)
    qkv_ref[0, 1] = packed[width : 2 * width].astype(BF)
    qkv_ref[0, 2] = (packed[2 * width :] + bias_v).astype(BF)
    mine = pl.ds(pl.multiple_of(core * half, half), half)
    other = pl.ds(pl.multiple_of((1 - core) * half, half), half)
    xh_ref[0] = jnp.transpose(xt_ref[0, :, mine])
    row = seg_ref[pl.ds(pl.program_id(0), 1), :].astype(F32)
    column = jnp.transpose(jnp.broadcast_to(row, (128, slots)))[:, 0:1]
    for block in range(2):
        rows = slice(block * half, (block + 1) * half)
        allowed = column[rows] == row
        for h in range(heads):
            feats = slice(h * size, (h + 1) * size)
            scores = dot_tn(qkv_ref[0, 0, feats, rows], qkv_ref[0, 1, feats, :])
            scores = scores + prev_ref[0, h, rows, :].astype(F32)
            raw_ref[0, h, rows, :] = scores.astype(BF)
            masked = jnp.where(allowed, scores, NEG)
            expanded = jnp.exp(masked - jnp.max(masked, axis=-1, keepdims=True))
            prob = expanded * (1.0 / jnp.sum(expanded, axis=-1, keepdims=True))
            prob = prob.astype(BF)
            p_ref[0, h, rows, :] = prob
            heads_out = dot_nt(prob, qkv_ref[0, 2, feats, :])
            o_scr[feats, rows] = jnp.transpose(heads_out).astype(BF)
    own_ref[0] = o_scr[:, mine]
    oth_ref[0] = o_scr[:, other]


def up_kernel(
    me_ref, o0, o1, o2, o3, wo0, wo1, wo2, wo3, big_a, big_b, xh_ref, bias_ref, gain_ref, shift_ref,
    b_up_a, b_up_b,
    n1_ref, r1_ref, x1_ref, ga_ref, gb_ref, gpa_ref, gpb_ref, part_ref,
):
    units = b_up_a.shape[1]
    w1a, w1b = big_a.at[:, :units], big_b.at[:, :units]
    w2a, w2b = big_a.at[:, units : 2 * units], big_b.at[:, units : 2 * units]
    total = xh_ref[0].astype(F32) + bias_ref[0:1, :]
    for left, right in ((o0, wo0), (o1, wo1), (o2, wo2), (o3, wo3)):
        total = total + dot_nt(jnp.transpose(left[0]), right[...])
    normed, inv_std = ln_stats(total)
    n1_ref[0] = normed
    r1_ref[0] = jnp.broadcast_to(inv_std, r1_ref.shape[1:])
    x1_ref[0] = (normed * gain_ref[0:1, :] + shift_ref[0:1, :]).astype(BF)
    block = 256

    def one_block(step, carry):
        lanes = pl.ds(pl.multiple_of(step * block, block), block)
        sides = ((w1a, b_up_a, ga_ref, gpa_ref), (w1b, b_up_b, gb_ref, gpb_ref))
        for w1, b_up, g_ref, gp_ref in sides:
            hidden = dot(x1_ref[0], w1[:, lanes]) + b_up[:, lanes]
            cdf = 0.5 * (1.0 + lax.erf(hidden * (0.5**0.5)))
            pdf = jnp.exp(-0.5 * hidden * hidden) * 0.3989422804014327
            g_ref[0, :, lanes] = (hidden * cdf).astype(BF)
            gp_ref[0, :, lanes] = (cdf + hidden * pdf).astype(BF)
        return carry

    lax.fori_loop(0, units // block, one_block, 0)
    part_ref[0] = (dot_nt(ga_ref[0], w2a[...]) + dot_nt(gb_ref[0], w2b[...])).astype(BF)


def down_kernel(
    me_ref, n1_ref, pa_ref, pb_ref, dy0, dy1, dy2, dy3, bias_ref, gain_ref, shift_ref,
    big_a, big_b, gpa_ref, gpb_ref,
    act_own_ref, act_oth_ref, ds_ref, dsb_ref, da_ref, db_ref, vec_ref, bup_a_ref, bup_b_ref, part_ref,
    scr,
):
    me = me_ref[0]
    width = dy0.shape[1]
    units = gpa_ref.shape[2]
    w1a, w1b = big_a.at[:, :units], big_b.at[:, :units]
    w2a, w2b = big_a.at[:, units : 2 * units], big_b.at[:, units : 2 * units]
    branch = pa_ref[0].astype(F32) + pb_ref[0].astype(F32)
    first_out = n1_ref[0] * gain_ref[0:1, :] + shift_ref[0:1, :]
    normed, inv_std = ln_stats(first_out + branch + bias_ref[1:2, :])
    gain = gain_ref[1:2, :]
    scr[...] = jnp.transpose(normed * gain + shift_ref[1:2, :])
    for step, out in ((0, act_own_ref), (1, act_oth_ref)):
        start = pl.multiple_of(place_of(me, step) * width, width)
        out[0] = scr[pl.ds(start, width), :].astype(BF)
    for step, piece in enumerate((dy0, dy1, dy2, dy3)):
        start = pl.multiple_of(place_of(me, step) * width, width)
        scr[pl.ds(start, width), :] = piece[0].astype(F32)
    grad = jnp.transpose(scr[...])
    inner = ln_back(grad, normed, inv_std, gain)
    ds_ref[0] = inner
    vec_ref[0, 0:1, :] = jnp.sum(grad * normed, axis=0, keepdims=True)
    vec_ref[0, 1:2, :] = jnp.sum(grad, axis=0, keepdims=True)
    vec_ref[0, 2:3, :] = jnp.sum(inner, axis=0, keepdims=True)
    dsb_ref[0] = inner.astype(BF)
    block = 256

    def one_block(step, carry):
        lanes = pl.ds(pl.multiple_of(step * block, block), block)
        sides = ((w2a, da_ref, gpa_ref, bup_a_ref), (w2b, db_ref, gpb_ref, bup_b_ref))
        for w2, dh_ref, gp_ref, bup_ref in sides:
            grad_hidden = dot(dsb_ref[0], w2[:, lanes]) * gp_ref[0, :, lanes].astype(F32)
            bup_ref[0, 0:1, lanes] = jnp.sum(grad_hidden, axis=0, keepdims=True)
            dh_ref[0, :, lanes] = grad_hidden.astype(BF)
        return carry

    lax.fori_loop(0, units // block, one_block, 0)
    part_ref[0] = (dot_nt(da_ref[0], w1a[...]) + dot_nt(db_ref[0], w1b[...])).astype(BF)


def mid_kernel(
    me_ref, ds_ref, pa_ref, pb_ref, n1_ref, r1_ref, gain_ref, wo0, wo1,
    dsb_ref, vec_ref, do_own_ref, do_oth_ref, near_ref, scr,
):
    chip = me_ref[0] // 2
    width = do_own_ref.shape[1]
    grad = ds_ref[0] + (pa_ref[0].astype(F32) + pb_ref[0].astype(F32))
    normed = n1_ref[0]
    inner = ln_back(grad, normed, r1_ref[0, :, 0:1], gain_ref[0:1, :])
    vec_ref[0, 0:1, :] = jnp.sum(grad * normed, axis=0, keepdims=True)
    vec_ref[0, 1:2, :] = jnp.sum(grad, axis=0, keepdims=True)
    vec_ref[0, 2:3, :] = jnp.sum(inner, axis=0, keepdims=True)
    dsb = inner.astype(BF)
    dsb_ref[0] = dsb
    scr[...] = inner
    chip_lanes = pl.ds(pl.multiple_of(chip * 2 * width, 128), 2 * width)
    near_ref[0] = jnp.transpose(scr[:, chip_lanes])
    do_own_ref[0] = jnp.transpose(dot(dsb, wo0[...])).astype(BF)
    do_oth_ref[0] = jnp.transpose(dot(dsb, wo1[...])).astype(BF)


def back_kernel(
    heads, me_ref, p_ref, qkv_ref, do_own_ref, do_oth_ref, w_ref, near_ref,
    lg_ref, dqkv_ref, e0, e1, e2, e3, vec_ref, do_scr, dx_scr, sum_scr,
):
    me = me_ref[0]
    core, chip = lax.rem(me, 2), me // 2
    width, slots = qkv_ref.shape[2], qkv_ref.shape[3]
    half = slots // 2
    size = width // heads
    mine = pl.ds(pl.multiple_of(core * half, half), half)
    other = pl.ds(pl.multiple_of((1 - core) * half, half), half)
    do_scr[:, mine] = do_own_ref[0]
    do_scr[:, other] = do_oth_ref[0]
    scale = 1.0 / (size**0.5)
    def one_head(h, carry):
        feats = pl.ds(pl.multiple_of(h * size, size), size)
        query, key, value = (qkv_ref[0, part, feats, :] for part in range(3))
        out_grad = do_scr[feats, :]
        for block in range(2):
            rows = slice(block * half, (block + 1) * half)
            prob = p_ref[0, h, rows, :].astype(F32)
            grad_prob = dot_tn(do_scr[feats, rows], value)
            weighted = grad_prob * prob
            inner = jnp.sum(weighted, axis=-1, keepdims=True)
            lg_ref[0, h, rows, :] = (weighted - prob * inner).astype(BF)
        grad_query = jnp.transpose(dot_nt(lg_ref[0, h], key)) * scale
        grad_key = dot(query, lg_ref[0, h])
        grad_value = dot(out_grad, p_ref[0, h])
        for number, grad in ((0, grad_query), (1, grad_value)):
            line = jnp.sum(grad, axis=1, keepdims=True)
            sum_scr[number, feats, :] = jnp.broadcast_to(line, (size, 128))
        dqkv_ref[0, feats, :] = grad_query.astype(BF)
        dqkv_ref[0, pl.ds(pl.multiple_of(width + h * size, size), size), :] = grad_key.astype(BF)
        dqkv_ref[0, pl.ds(pl.multiple_of(2 * width + h * size, size), size), :] = grad_value.astype(BF)
        return carry

    lax.fori_loop(0, heads, one_head, 0)
    for number in range(2):
        vec_ref[0, number : number + 1, :] = jnp.transpose(sum_scr[number])[0:1, :]
    dx_scr[...] = dot(w_ref[...], dqkv_ref[0])
    near = pl.ds(pl.multiple_of(chip * 2 * width, width), 2 * width)
    dx_scr[near, mine] = dx_scr[near, mine] + near_ref[0]
    for step, out in enumerate((e0, e1, e2, e3)):
        start = pl.multiple_of(place_of(me, step) * width, width)
        out[0] = dx_scr[pl.ds(start, width), :].astype(BF)


def ffn_grad_kernel(count, bit, me_ref, *rest):
    lefts, rights = rest[:count], rest[count : 2 * count]
    keep_ref, send_ref, scr = rest[2 * count :]
    side = me_ref[2 + bit]
    total = None
    for left, right in zip(lefts, rights):
        a = left[...].reshape(-1, left.shape[-1])
        b = right[...].reshape(-1, right.shape[-1])
        product = dot_tn(a, b)
        total = product if total is None else total + product
    part = keep_ref.shape[0]
    scr[...] = total
    keep_ref[...] = scr[pl.ds(pl.multiple_of(side * part, part), part), :].astype(BF)
    send_ref[...] = scr[pl.ds(pl.multiple_of((1 - side) * part, part), part), :].astype(BF)


def qkv_grad_kernel(count, me_ref, *rest):
    groups = [rest[i * count : (i + 1) * count] for i in range(6)]
    small_ref, came_ref, *bqv, keep_ref, send_ref, scr = rest[6 * count :]
    side = me_ref[2]
    width = bqv[0].shape[2]
    line = lax.broadcasted_iota(jnp.int32, small_ref.shape, 0)
    small = small_ref[...]
    scr[:8, :] = jnp.where(line < 6, (small + came_ref[...]) * 0.5, small)
    total = functools.reduce(jnp.add, [b[0] for b in bqv])
    scr[7:8, :width] = total[0:1, :]
    scr[7:8, width : 2 * width] = total[1:2, :]
    halves = as_halves(scr[:8, :])
    total = None
    for x, grad in zip(groups[0], groups[1]):
        for index in range(grad.shape[0]):
            product = dot_nt(grad[index], x[index])
            total = product if total is None else total + product
    used = total.shape[0]
    scr[:used, :] = total
    total = None
    for lefts, rights in ((groups[2], groups[3]), (groups[4], groups[5])):
        for left, right in zip(lefts, rights):
            for index in range(left.shape[0]):
                product = dot(left[index], right[index])
                total = product if total is None else total + product
    scr[used:, :] = total
    part = scr.shape[0] // 2
    for out, half in ((keep_ref, side), (send_ref, 1 - side)):
        place = pl.ds(pl.multiple_of(half * part, part), part)
        out[:part, :] = scr[place, :].astype(BF)
        out[part:, :] = halves


def halve_kernel(bit, tail, me_ref, *rest):
    count = (len(rest) - 2) // 2
    keep_ref, send_ref = rest[-2:]
    side = me_ref[2 + bit]
    rows = (rest[0].shape[0] - tail) // 2
    for number in range(count):
        kept, came = rest[2 * number], rest[2 * number + 1]
        for out, half in ((keep_ref, side), (send_ref, 1 - side)):
            place = pl.ds(pl.multiple_of(half * rows, rows), rows)
            total = kept[place, :].astype(F32) + came[place, :].astype(F32)
            out[number * rows : (number + 1) * rows, :] = total.astype(BF)
    if tail:
        both = as_halves(from_halves(kept[2 * rows :, :]) + from_halves(came[2 * rows :, :]))
        keep_ref[rows:, :] = both
        send_ref[rows:, :] = both


def last_kernel(me_ref, kept, came, out_ref, small_ref):
    rows = out_ref.shape[0]
    out_ref[...] = (kept[:rows, :].astype(F32) + came[:rows, :].astype(F32)).astype(BF)
    small_ref[...] = from_halves(kept[rows:, :]) + from_halves(came[rows:, :])


def finish_kernel(steps, pair, me_ref, *rest):
    count = len(steps)
    blocks, outs = rest[:count], rest[count:]
    rows = blocks[0].shape[0]
    for number, back in enumerate(steps):
        group = group_at(me_ref, back, count)
        bits = lax.rem(group, 2), lax.rem(group // 2, 2), group // 4
        index = bits[0] * 4 + bits[1] * 2 + bits[2]
        if pair:
            part = rows // 2
            other = bits[1] * 4 + bits[0] * 2 + bits[2]
            for out, place, low in ((outs[0], index, 0), (outs[1], other, part)):
                place = pl.ds(pl.multiple_of(place * part, part), part)
                out[place, :] = blocks[number][low : low + part, :].astype(F32)
            continue
        block = blocks[number][...].astype(F32)
        before = 0
        for out in outs:
            held = out.shape[0] // rows

            @pl.when((index >= before) & (index < before + held))
            def _():
                out[pl.ds(pl.multiple_of((index - before) * rows, rows), rows), :] = block

            before += held


def ring_place(group, groups):
    return jnp.where(lax.rem(group, 2) == 0, group // 2, groups - 1 - group // 2)


def group_at(me_ref, back, count):
    there = lax.rem(ring_place(me_ref[1], count) + count - back, count)
    return jnp.where(there < count // 2, 2 * there, 2 * (count - 1 - there) + 1)


def shard_kernel(me_ref, *rest):
    out_ref = rest[-1]
    low = 0
    for block in rest[:-1]:
        parts = [block[i] for i in range(block.shape[0])] if len(block.shape) == 3 else [block[...]]
        for part in parts:
            out_ref[:, low : low + part.shape[1]] = part.astype(BF)
            low += part.shape[1]


def stack_kernel(me_ref, first, second, out_ref):
    rows = first.shape[0]
    out_ref[:rows, :] = first[...]
    out_ref[rows:, :] = second[...]


def lanes_kernel(me_ref, whole_ref, mine_ref, other_ref):
    core = lax.rem(me_ref[0], 2)
    half = mine_ref.shape[2]
    for out, place in ((mine_ref, core), (other_ref, 1 - core)):
        lanes = pl.ds(pl.multiple_of(place * half, half), half)
        for row in range(out.shape[0]):
            out[row] = whole_ref[row, :, lanes]


def pairs_kernel(me_ref, *rest):
    blocks, outs = rest[:-6], rest[-6:]
    count = len(blocks)
    core = lax.rem(me_ref[0], 2)
    rows = blocks[0].shape[0] // 2
    for number in range(count):
        steps = number if number <= count // 2 else number - count // 2
        ahead = core if number <= count // 2 else 1 - core
        back = jnp.where(ahead == 1, lax.rem(count - steps, count), steps)
        place = pl.ds(pl.multiple_of(group_at(me_ref, back, count) * rows, rows), rows)
        first, second = (outs[:3], outs[3:]) if number <= count // 2 else (outs[3:], outs[:3])
        for part, three in enumerate((first, second)):
            low = 0
            for out in three:
                high = low + out.shape[1]
                out[place, :] = blocks[number][part * rows : (part + 1) * rows, low:high]
                low = high


def small_kernel(me_ref, vec1, vec2, bup_a, bup_b, own_ref, oth_ref):
    own_ref[...] = jnp.zeros_like(own_ref)
    oth_ref[...] = jnp.zeros_like(oth_ref)
    for low, vec in ((0, vec1), (3, vec2)):
        total = jnp.sum(vec[...], axis=0)
        own_ref[low : low + 3, :] = total
        oth_ref[low : low + 3, :] = total
    own_ref[6:7, :] = jnp.sum(bup_a[...], axis=0)
    oth_ref[6:7, :] = jnp.sum(bup_b[...], axis=0)


def as_halves(value):
    high = value.astype(BF).astype(F32)
    return jnp.concatenate([high, value - high], 0).astype(BF)


def from_halves(both):
    both = both.astype(F32)
    return both[:8] + both[8:]


def whole(array):
    shape = array.shape
    return pl.BlockSpec(shape, lambda i, s: (0,) * len(shape))


def held(array):
    return pl.BlockSpec(memory_space=pltpu.VMEM)


def by_row(array, first=0):
    shape = array.shape
    rest = (0,) * (len(shape) - 1)
    return pl.BlockSpec((1,) + shape[1:], lambda i, s: (first + i,) + rest)


def on_row(row, rowed, skip, kernel):
    def inner(*refs):
        kernel(*[
            ref.at[pl.ds(row, 1)] if number in rowed else ref
            for number, ref in enumerate(refs)
            if number not in skip
        ])

    return inner


def call(kernel, grid, ins, outs, out_specs, scratch, name, micros, alias=None, room=32):
    flops = int(micros * 10)
    return pl.pallas_call(
        kernel,
        out_shape=outs,
        grid_spec=pltpu.PrefetchScalarGridSpec(
            num_scalar_prefetch=1,
            grid=grid,
            in_specs=[spec for _, spec in ins[1:]],
            out_specs=out_specs,
            scratch_shapes=scratch,
        ),
        input_output_aliases=alias or {},
        compiler_params=pltpu.CompilerParams(vmem_limit_bytes=room << 20),
        cost_estimate=pl.CostEstimate(flops=flops, bytes_accessed=1, transcendentals=0),
        name=name,
    )(*[a for a, _ in ins])


def body(
    tokens, cotangent, prev_logits, segment_ids, w_qkv, b_qv, w_out, w_up, b_up, w_down,
    biases, gains, shifts,
):
    rows, slots, width = tokens.shape
    full = width * lax.axis_size("tensor")
    groups = lax.axis_size("dp")
    near_dp = groups == 8
    heads = prev_logits.shape[1]
    half = slots // 2
    units = w_up.shape[1]
    me = lax.axis_index("tensor").astype(jnp.int32)
    dp = lax.axis_index("dp").astype(jnp.int32)
    me_ref = jnp.stack([me, dp, lax.rem(dp, 2), lax.rem(dp // 2, 2), dp // 4])
    core = lax.rem(me, 2)
    sds = jax.ShapeDtypeStruct

    def after(value, *others):
        return lax.optimization_barrier((value, others))[0]

    together = lax.optimization_barrier

    def pp(array, step):
        return lax.ppermute(array, "tensor", [(i, i ^ step) for i in range(4)])

    def swap(array, bit):
        return lax.ppermute(array, "dp", [(i, i ^ (1 << bit)) for i in range(groups)])

    order = list(range(0, groups, 2)) + list(range(groups - 1, 0, -2))
    onward = [(order[i], order[(i + 1) % groups]) for i in range(groups)]
    backward = [(b, a) for a, b in onward]

    ring_steps = [0]
    for step in range(1, groups // 2):
        ring_steps += [step, groups - step]
    ring_steps += [groups // 2]

    def ring_step(ahead, behind):
        return lax.ppermute(ahead, "dp", onward), lax.ppermute(behind, "dp", backward)

    def place_pairs(blocks):
        outs = [sds((full, wide), BF) for wide in (2 * units, width, width)] * 2
        return call(
            pairs_kernel, (1,), [(me_ref, None)] + [(b, held(b)) for b in blocks], outs,
            [held(o) for o in outs], [], "pairs", 2, None, 8,
        )

    both_ways = []
    for i, j in onward:
        both_ways += [(i * 4 + t, j * 4 + t) if t % 2 == 0 else (j * 4 + t, i * 4 + t) for t in range(4)]

    def pair_step(pair):
        return lax.ppermute(pair, ("dp", "tensor"), both_ways)

    tokens = jnp.swapaxes(tokens, 1, 2)
    cotangent = jnp.swapaxes(cotangent, 1, 2)
    def joined(kernel, outs, *arrays):
        ins = [(me_ref, None)] + [(a, whole(a)) for a in arrays]
        return call(kernel, (1,), ins, outs, [whole(o) for o in outs], [], "joined", 1, None, 8)

    shard_out = w_out.T.astype(BF)
    if near_dp:
        own = w_up.shape[0]
        shard_in = joined(
            shard_kernel, [sds((own, 3 * width), BF)], jnp.transpose(w_qkv, (1, 0, 2))
        )[0]
        out_y = pp(shard_out, 2)
        x_y = pp(after(tokens, out_y), 2)
        x_c = pp(tokens, 1)
        ring = [ring_step(shard_in, shard_in)]
        ring.append(ring_step(*together(ring[-1])))
        shard_big = joined(
            shard_kernel, [sds((own, 2 * units + 2 * width), BF)], w_up, w_down.T, shard_out, out_y
        )[0]
        ring.append(ring_step(*together(ring[-1])))
        last = lax.ppermute(together(ring[-1])[0], "dp", onward)
        pair_big = joined(
            stack_kernel, [sds((2 * own, 2 * units + 2 * width), BF)], shard_big, pp(shard_big, 1)
        )[0]
        came = [pair_step(after(pair_big, last))]
        pieces_in = [shard_in, *ring[0], *ring[1], *ring[2], last]
        dy_mine, dy_other = joined(
            lanes_kernel, [sds((rows, width, half), BF)] * 2, after(cotangent, x_y)
        )
    else:
        x_y = pp(tokens, 2)
        x_c = pp(tokens, 1)
        shard_in = w_qkv.astype(BF).reshape(w_qkv.shape[0], 3 * width)
        shard_big = jnp.concatenate(
            [w_up.astype(BF), w_down.T.astype(BF), shard_out, pp(shard_out, 2)], 1
        )
        pieces_in = [lax.all_gather(shard_in, "dp", axis=0, tiled=True)]
        big_a = lax.all_gather(shard_big, "dp", axis=0, tiled=True)
        cot = after(cotangent, x_y)
        dy_mine = lax.dynamic_slice_in_dim(cot, core * half, half, 2)
        dy_other = lax.dynamic_slice_in_dim(cot, (1 - core) * half, half, 2)
    x_d = pp(x_y, 1)
    x_pieces = (tokens, x_c, x_y, x_d)
    dy1, dy2, dy3 = pp(dy_other, 1), pp(dy_mine, 2), pp(dy_other, 3)
    b_up_a = b_up.reshape(1, units)
    b_up_b = pp(b_up_a, 1)

    sds3 = lambda *shape_type: sds((rows,) + shape_type[:-1], shape_type[-1])

    class Stage:
        def __init__(self, kernel, fulls, parts, scratch, name, room, far=()):
            self.kernel, self.fulls, self.parts, self.scratch = kernel, fulls, parts, scratch
            self.name, self.room, self.far, self.kept = name, room, far, None

        def step(self, row, given):
            fulls, far = self.fulls, self.far
            ins = [(me_ref, None)]
            ins += [(a, held(a) if isinstance(k, str) else k) for a, k in given]
            rowed = {1 + i for i, (_, k) in enumerate(given) if isinstance(k, str) and k == "row"}
            low, alias = len(ins), {}
            if self.kept is not None:
                alias = {low + i: i for i in range(len(fulls))}
                ins += [
                    (k, pl.BlockSpec(memory_space=pl.ANY) if i in far else held(k))
                    for i, k in enumerate(self.kept)
                ]
            base = len(ins)
            outs = list(fulls) + list(self.parts)
            specs = [by_row(o, row) if i in far else held(o) for i, o in enumerate(fulls)]
            specs += [held(o) for o in self.parts]
            rowed |= {base + i for i in range(len(fulls)) if i not in far}
            result = call(
                on_row(row, rowed, set(alias), self.kernel), (1,), ins, outs, specs,
                self.scratch, self.name, 1, alias, self.room,
            )
            self.kept = result[: len(fulls)]
            return result[len(fulls) :]

    ins = [(me_ref, None)] + [(p, by_row(p)) for p in x_pieces]
    ins += [(b_qv, whole(b_qv)), (prev_logits, by_row(prev_logits))]
    ins += [(segment_ids, whole(segment_ids))] + [(b, held(b)) for b in pieces_in]
    outs = [
        sds(prev_logits.shape, BF),
        sds(prev_logits.shape, BF),
        sds3(3, width, slots, BF),
        sds3(width, half, BF),
        sds3(width, half, BF),
        sds3(full, slots, BF),
        sds3(half, full, BF),
        sds((full, 3 * width), BF),
    ]
    raw, prob, qkv, o_own, o_oth, xt, xh, w_in = call(
        functools.partial(attend_kernel, heads, ring_steps if near_dp else [0]), (rows,), ins,
        outs, [by_row(o) for o in outs[:-1]] + [held(outs[-1])],
        [pltpu.VMEM((width, slots), BF)], "attend", 1, None, 48,
    )
    o1, o2, o3 = pp(o_oth, 1), pp(o_own, 2), pp(o_oth, 3)
    if near_dp:
        came.append(pair_step(after(came[0], o_own, dy1, dy2, dy3)))
        came.append(pair_step(after(came[1], o2)))
        came.append(pair_step(after(came[2], o1, o3)))
        big_a, wo0, wo2, big_b, wo1, wo3 = place_pairs(
            [pair_big, *came, *[pp(b, 1) for b in came[:3]]]
        )
    else:
        big_a = after(big_a, o_own)
        big_b = pp(big_a, 1)
        wo0, wo1 = (b[:, 2 * units : 2 * units + width] for b in (big_a, big_b))
        wo2, wo3 = (b[:, 2 * units + width :] for b in (big_a, big_b))
        big_a, big_b = big_a[:, : 2 * units], big_b[:, : 2 * units]

    one = (1, half, full)
    up = Stage(
        up_kernel,
        [
            sds3(half, full, F32), sds3(half, 128, F32), sds3(half, full, BF),
            sds3(half, units, BF), sds3(half, units, BF), sds3(half, units, BF), sds3(half, units, BF),
        ],
        [sds(one, BF)], [], "up", 16,
    )
    part, part_y = [], []
    for row in range(rows):
        given = [(o, "row") for o in (o_own, o1, o2, o3)]
        given += [(w, "all") for w in (wo0, wo1, wo2, wo3, big_a, big_b)] + [(xh, "row")]
        given += [(w, "all") for w in (biases, gains, shifts, b_up_a, b_up_b)]
        part += up.step(row, given)
        part_y.append(pp(part[row], 2))
    n1, r1, x1, ga, gb, gpa, gpb = up.kept
    gc, x1_c = pp(gb, 1), pp(x1, 1)

    down = Stage(
        down_kernel,
        [
            sds3(width, half, BF), sds3(width, half, BF), sds3(half, full, F32),
            sds3(half, full, BF), sds3(half, units, BF), sds3(half, units, BF),
            sds3(3, full, F32), sds3(1, units, F32), sds3(1, units, F32),
        ],
        [sds(one, BF)], [pltpu.VMEM((full, half), F32)], "down", 16,
    )
    part2, part2_y = [], []
    for row in range(rows):
        got = after(part_y[row], part2_y[0]) if row == 2 else part_y[row]
        given = [(n1, "row"), (part[row], "all"), (got, "all")]
        given += [(d, "row") for d in (dy_mine, dy1, dy2, dy3)]
        given += [(w, "all") for w in (biases, gains, shifts, big_a, big_b)]
        given += [(gpa, "row"), (gpb, "row")]
        part2 += down.step(row, given)
        part2_y.append(pp(part2[row], 2))
    act_own, act_oth, ds2, ds2b, da, db, vec2, bup_a, bup_b = down.kept
    ds2b_c, dc = pp(ds2b, 1), pp(db, 1)

    def ffn_grad(lefts, rights, bit):
        block = 256
        def part(a):
            return pl.BlockSpec(a.shape[:2] + (block,), lambda i, s: (0, 0, i))
        ins = [(me_ref, None)] + [(a, whole(a)) for a in lefts] + [(a, part(a)) for a in rights]
        across, down = rights[0].shape[-1], lefts[0].shape[-1]
        outs = [sds((down // 2, across), BF)] * 2
        specs = [pl.BlockSpec((down // 2, block), lambda i, s: (0, i))] * 2
        return call(
            functools.partial(ffn_grad_kernel, len(lefts), bit),
            (across // block,), ins, outs, specs, [pltpu.VMEM((down, block), F32)], "ffn_grad", 3,
        )

    def halve(bit, *pairs, tail=0):
        down, across = pairs[0][0].shape
        outs = [sds((len(pairs) * (down - tail) // 2 + tail, across), BF)] * 2
        ins = [(me_ref, None)] + [(a, whole(a)) for pair in pairs for a in pair]
        return call(
            functools.partial(halve_kernel, bit, tail), (1,), ins, outs, [whole(o) for o in outs], [],
            "halve", 1,
        )

    def added(keep, got):
        return (keep.astype(F32) + got.astype(F32)).astype(BF)

    def finish(blocks, outs, pair=False):
        return call(
            functools.partial(finish_kernel, ring_steps, pair), (1,),
            [(me_ref, None)] + [(b, whole(b)) for b in blocks],
            outs, [whole(o) for o in outs], [], "finish", 2,
        )

    def whole_of(keep, send, bit):
        low = jnp.where(lax.rem(dp >> bit, 2) == 0, keep, send)
        high = jnp.where(lax.rem(dp >> bit, 2) == 0, send, keep)
        return jnp.concatenate([low, high], 0)

    mid = Stage(
        mid_kernel, [sds3(half, full, BF), sds3(3, full, F32)],
        [sds((1, width, half), BF)] * 2 + [sds((1, 2 * width, half), F32)],
        [pltpu.VMEM((half, full), F32)], "mid", 16,
    )
    back = Stage(
        functools.partial(back_kernel, heads),
        [sds(prev_logits.shape, BF), sds3(3 * width, slots, BF)] + [sds3(width, slots, BF)] * 4,
        [sds((1, 2, width), F32)],
        [pltpu.VMEM((width, slots), BF), pltpu.VMEM((full, slots), F32), pltpu.VMEM((2, width, 128), F32)],
        "back", 32, (0,),
    )

    def mid_step(row, *earlier):
        given = [(ds2, "row"), (part2[row], "all"), (after(part2_y[row], *earlier), "all")]
        given += [(n1, "row"), (r1, "row"), (gains, "all"), (wo0, "all"), (wo1, "all")]
        own, oth, near = mid.step(row, given)
        return own, pp(oth, 1), near

    def back_step(row, held_by, *earlier):
        own, got, near = held_by
        given = [(prob, by_row(prob, row)), (qkv, by_row(qkv, row)), (own, "all")]
        given += [(after(got, *earlier), "all"), (w_in, "all"), (near, "all")]
        return back.step(row, given)[0]

    keep_d, send_d = ffn_grad((ga, gc), (ds2b, ds2b_c), 0)
    mids = [mid_step(0)]
    keep_u, send_u = ffn_grad((x1, x1_c), (da, dc), 1)
    mids.append(mid_step(1, keep_d, keep_u, mids[0][0]))
    sums = [back_step(0, mids[0], mids[1][0]), back_step(1, mids[1])]
    if near_dp:
        got_d, got_u = (swap(after(g, mids[1][0]), b) for g, b in ((send_d, 0), (send_u, 1)))
        mids.append(mid_step(2, sums[1], got_d, got_u))
        keep_d, send_d = halve(1, (keep_d, after(got_d, mids[2][0])))
        keep_u, send_u = halve(0, (keep_u, got_u))
        got_d, got_u = swap(send_d, 1), swap(send_u, 0)
        sums.append(back_step(2, mids[2], keep_d, keep_u))
    else:
        mids.append(mid_step(2, sums[1]))
        grad_down, grad_up = lax.psum((whole_of(keep_d, send_d, 0), whole_of(keep_u, send_u, 1)), "dp")
        grad_down, grad_up = grad_down.astype(F32), grad_up.astype(F32)
        sums.append(back_step(2, mids[2]))
    ds1b, vec1 = mid.kept
    ds1b_c = pp(ds1b, 1)
    ins = [(me_ref, None)] + [(a, whole(a)) for a in (vec1, vec2, bup_a, bup_b)]
    outs = [sds((8, full), F32)] * 2
    small, other = call(small_kernel, (1,), ins, outs, [whole(o) for o in outs], [], "small", 1)
    small = small + pp(other, 1)
    small_y = pp(small, 2)
    lg, dqkv, e0, e1, e2, e3 = back.kept

    ins = [(me_ref, None)] + [(a, whole(a)) for a in (xt, dqkv, o_own, ds1b, o_oth, ds1b_c)]
    ins += [(a, whole(a)) for a in (small, small_y, *sums)]
    outs = [sds((full // 2 + 16, full), BF)] * 2
    keep, send = call(
        functools.partial(qkv_grad_kernel, 1), (1,), ins, outs, [whole(o) for o in outs],
        [pltpu.VMEM((full, full), F32)], "qkv_grad", 4,
    )

    if near_dp:
        got = swap(send, 0)
        keep_du, send_du = halve(2, (keep_d, after(got_d, send)), (keep_u, got_u))
        got_du = swap(send_du, 2)
        keep, send = halve(1, (keep, got), tail=16)
        got = swap(send, 1)
        pair = added(keep_du, got_du)
        ring_u = [ring_step(pair, pair)]
        keep, send = halve(2, (keep, got), tail=16)
        got = swap(send, 2)
        ring_u.append(ring_step(*together(ring_u[-1])))
        outs = [sds((full // 8, full), BF), sds((8, full), F32)]
        total, small = call(
            last_kernel, (1,), [(me_ref, None), (keep, whole(keep)), (got, whole(got))], outs,
            [whole(o) for o in outs], [], "last", 1,
        )
        ring = [ring_step(total, total)]
        ring_u.append(ring_step(*together(ring_u[-1])))
        ring.append(ring_step(*together(ring[-1])))
        last_u = lax.ppermute(ring_u[-1][0], "dp", onward)
        ring.append(ring_step(*together(ring[-1])))
        last = lax.ppermute(ring[-1][0], "dp", onward)
        grad_down, grad_up = finish(
            [after(pair, *ring[2]), *ring_u[0], *ring_u[1], *ring_u[2], last_u],
            [sds((units, full), F32), sds((full, units), F32)], True,
        )
        grad_in, grad_out = finish(
            [total, *ring[0], *ring[1], *ring[2], last],
            [sds((3 * width, full), F32), sds((width, full), F32)],
        )
    else:
        part = full // 2
        tail = lax.psum(whole_of(keep[:part], send[:part], 0), "dp").astype(F32)
        small = lax.psum(keep[part : part + 8].astype(F32) + keep[part + 8 :].astype(F32), "dp")
        grad_in, grad_out = tail[: 3 * width], tail[3 * width :]
    grad_b_up = small[6]
    grad_b_qv = small[7, : 2 * width].reshape(2, width)

    grad_in = jnp.transpose(grad_in.reshape(3, width, full), (2, 0, 1))

    act_c = pp(act_oth, 1)
    block_out = jnp.concatenate(
        [jnp.where(core == 0, act_own, act_c), jnp.where(core == 0, act_c, act_own)], 2
    )
    near_sum = e2.astype(F32) + pp(e3, 1).astype(F32)
    far = pp(near_sum.astype(BF), 2).astype(F32)
    grad_x = (e0.astype(F32) + pp(e1, 1).astype(F32) + far).astype(BF)
    return (
        jnp.swapaxes(block_out, 1, 2),
        raw,
        jnp.swapaxes(grad_x, 1, 2),
        lg,
        grad_in,
        grad_b_qv,
        grad_out,
        grad_up,
        grad_b_up,
        grad_down,
        jnp.stack([small[2], small[5]]),
        jnp.stack([small[0], small[3]]),
        jnp.stack([small[1], small[4]]),
    )


def solution(mesh):
    placed = (
        P("dp", None, "tensor"),
        P("dp", None, "tensor"),
        P("dp", "tensor", None, None),
        P("dp", None),
        P("dp", None, "tensor"),
        P(None, "tensor"),
        P("tensor", "dp"),
        P("dp", "tensor"),
        P("tensor"),
        P("tensor", "dp"),
        P(),
        P(),
        P(),
    )
    return jax.shard_map(
        body,
        mesh=mesh,
        in_specs=placed,
        out_specs=(
            P("dp", None, "tensor"),
            P("dp", "tensor", None, None),
            P("dp", None, "tensor"),
            P("dp", "tensor", None, None),
            P(None, None, "tensor"),
            P(None, "tensor"),
            P("tensor", None),
            P(None, "tensor"),
            P("tensor"),
            P("tensor", None),
            P(),
            P(),
            P(),
        ),
        check_vma=False,
    )
```

```python
import functools

import jax
import jax.numpy as jnp
from jax import lax
from jax.experimental import pallas as pl
from jax.experimental.pallas import tpu as pltpu
from jax.sharding import PartitionSpec as P

EPS = 1e-06
NEG = -1e30
BF = jnp.bfloat16
F32 = jnp.float32


def dot(a, b):
    return lax.dot_general(a, b, (((1,), (0,)), ((), ())), preferred_element_type=F32)


def dot_nt(a, b):
    return lax.dot_general(a, b, (((1,), (1,)), ((), ())), preferred_element_type=F32)


def dot_tn(a, b):
    return lax.dot_general(a, b, (((0,), (0,)), ((), ())), preferred_element_type=F32)


def place_of(me, step):
    core, chip = lax.rem(me, 2), me // 2
    core = 1 - core if step % 2 else core
    chip = 1 - chip if step // 2 else chip
    return 2 * chip + core


def ln_stats(summed):
    row_mean = jnp.mean(summed, axis=-1, keepdims=True)
    centered = summed - row_mean
    inv_std = lax.rsqrt(jnp.mean(centered * centered, axis=-1, keepdims=True) + EPS)
    return centered * inv_std, inv_std


def ln_back(grad, normed, inv_std, gain):
    scaled = grad * gain
    inner = (
        scaled
        - jnp.mean(scaled, axis=-1, keepdims=True)
        - normed * jnp.mean(scaled * normed, axis=-1, keepdims=True)
    )
    return inner * inv_std


def attend_kernel(
    heads, steps, me_ref, x0, x1, x2, x3, b_ref, prev_ref, seg_ref, *rest
):
    count = len(steps)
    blocks = rest[:count]
    raw_ref, p_ref, qkv_ref, own_ref, oth_ref, xt_ref, xh_ref, w_ref, o_scr = rest[count:]

    @pl.when(pl.program_id(0) == 0)
    def _():
        rows = blocks[0].shape[0]
        for block, back in zip(blocks, steps):
            group = group_at(me_ref, back, count) if count > 1 else 0
            w_ref[pl.ds(pl.multiple_of(group * rows, rows), rows), :] = block[...]

    me = me_ref[0]
    core = lax.rem(me, 2)
    width, slots = x0.shape[1], x0.shape[2]
    half = slots // 2
    size = width // heads
    for step, piece in enumerate((x0, x1, x2, x3)):
        start = pl.multiple_of(place_of(me, step) * width, width)
        xt_ref[0, pl.ds(start, width), :] = piece[0]
    bias = jnp.transpose(jnp.broadcast_to(b_ref[0:1, :], (128, width)))[:, 0:1]
    bias_v = jnp.transpose(jnp.broadcast_to(b_ref[1:2, :], (128, width)))[:, 0:1]
    packed = dot_tn(w_ref[...], xt_ref[0])
    scale = 1.0 / (size**0.5)
    qkv_ref[0, 0] = ((packed[:width] + bias).astype(BF).astype(F32) * scale).astype(BF)
    qkv_ref[0, 1] = packed[width : 2 * width].astype(BF)
    qkv_ref[0, 2] = (packed[2 * width :] + bias_v).astype(BF)
    mine = pl.ds(pl.multiple_of(core * half, half), half)
    other = pl.ds(pl.multiple_of((1 - core) * half, half), half)
    xh_ref[0] = jnp.transpose(xt_ref[0, :, mine])
    row = seg_ref[pl.ds(pl.program_id(0), 1), :].astype(F32)
    column = jnp.transpose(jnp.broadcast_to(row, (128, slots)))[:, 0:1]
    for block in range(2):
        rows = slice(block * half, (block + 1) * half)
        allowed = column[rows] == row
        for h in range(heads):
            feats = slice(h * size, (h + 1) * size)
            scores = dot_tn(qkv_ref[0, 0, feats, rows], qkv_ref[0, 1, feats, :])
            scores = scores + prev_ref[0, h, rows, :].astype(F32)
            raw_ref[0, h, rows, :] = scores.astype(BF)
            masked = jnp.where(allowed, scores, NEG)
            expanded = jnp.exp(masked - jnp.max(masked, axis=-1, keepdims=True))
            prob = expanded * (1.0 / jnp.sum(expanded, axis=-1, keepdims=True))
            prob = prob.astype(BF)
            p_ref[0, h, rows, :] = prob
            heads_out = dot_nt(prob, qkv_ref[0, 2, feats, :])
            o_scr[feats, rows] = jnp.transpose(heads_out).astype(BF)
    own_ref[0] = o_scr[:, mine]
    oth_ref[0] = o_scr[:, other]


def up_kernel(
    me_ref, o0, o1, o2, o3, wo0, wo1, wo2, wo3, big_a, big_b, xh_ref, bias_ref, gain_ref, shift_ref,
    b_up_a, b_up_b,
    n1_ref, r1_ref, x1_ref, ga_ref, gb_ref, gpa_ref, gpb_ref, part_ref,
):
    units = b_up_a.shape[1]
    w1a, w1b = big_a.at[:, :units], big_b.at[:, :units]
    w2a, w2b = big_a.at[:, units : 2 * units], big_b.at[:, units : 2 * units]
    total = xh_ref[0].astype(F32) + bias_ref[0:1, :]
    for left, right in ((o0, wo0), (o1, wo1), (o2, wo2), (o3, wo3)):
        total = total + dot_nt(jnp.transpose(left[0]), right[...])
    normed, inv_std = ln_stats(total)
    n1_ref[0] = normed
    r1_ref[0] = jnp.broadcast_to(inv_std, r1_ref.shape[1:])
    x1_ref[0] = (normed * gain_ref[0:1, :] + shift_ref[0:1, :]).astype(BF)
    block = 256

    def one_block(step, carry):
        lanes = pl.ds(pl.multiple_of(step * block, block), block)
        sides = ((w1a, b_up_a, ga_ref, gpa_ref), (w1b, b_up_b, gb_ref, gpb_ref))
        for w1, b_up, g_ref, gp_ref in sides:
            hidden = dot(x1_ref[0], w1[:, lanes]) + b_up[:, lanes]
            cdf = 0.5 * (1.0 + lax.erf(hidden * (0.5**0.5)))
            pdf = jnp.exp(-0.5 * hidden * hidden) * 0.3989422804014327
            g_ref[0, :, lanes] = (hidden * cdf).astype(BF)
            gp_ref[0, :, lanes] = (cdf + hidden * pdf).astype(BF)
        return carry

    lax.fori_loop(0, units // block, one_block, 0)
    part_ref[0] = (dot_nt(ga_ref[0], w2a[...]) + dot_nt(gb_ref[0], w2b[...])).astype(BF)


def down_kernel(
    me_ref, n1_ref, pa_ref, pb_ref, dy0, dy1, dy2, dy3, bias_ref, gain_ref, shift_ref,
    big_a, big_b, gpa_ref, gpb_ref,
    act_own_ref, act_oth_ref, ds_ref, dsb_ref, da_ref, db_ref, vec_ref, bup_a_ref, bup_b_ref, part_ref,
    scr,
):
    me = me_ref[0]
    width = dy0.shape[1]
    units = gpa_ref.shape[2]
    w1a, w1b = big_a.at[:, :units], big_b.at[:, :units]
    w2a, w2b = big_a.at[:, units : 2 * units], big_b.at[:, units : 2 * units]
    branch = pa_ref[0].astype(F32) + pb_ref[0].astype(F32)
    first_out = n1_ref[0] * gain_ref[0:1, :] + shift_ref[0:1, :]
    normed, inv_std = ln_stats(first_out + branch + bias_ref[1:2, :])
    gain = gain_ref[1:2, :]
    scr[...] = jnp.transpose(normed * gain + shift_ref[1:2, :])
    for step, out in ((0, act_own_ref), (1, act_oth_ref)):
        start = pl.multiple_of(place_of(me, step) * width, width)
        out[0] = scr[pl.ds(start, width), :].astype(BF)
    for step, piece in enumerate((dy0, dy1, dy2, dy3)):
        start = pl.multiple_of(place_of(me, step) * width, width)
        scr[pl.ds(start, width), :] = piece[0].astype(F32)
    grad = jnp.transpose(scr[...])
    inner = ln_back(grad, normed, inv_std, gain)
    ds_ref[0] = inner
    vec_ref[0, 0:1, :] = jnp.sum(grad * normed, axis=0, keepdims=True)
    vec_ref[0, 1:2, :] = jnp.sum(grad, axis=0, keepdims=True)
    vec_ref[0, 2:3, :] = jnp.sum(inner, axis=0, keepdims=True)
    dsb_ref[0] = inner.astype(BF)
    block = 256

    def one_block(step, carry):
        lanes = pl.ds(pl.multiple_of(step * block, block), block)
        sides = ((w2a, da_ref, gpa_ref, bup_a_ref), (w2b, db_ref, gpb_ref, bup_b_ref))
        for w2, dh_ref, gp_ref, bup_ref in sides:
            grad_hidden = dot(dsb_ref[0], w2[:, lanes]) * gp_ref[0, :, lanes].astype(F32)
            bup_ref[0, 0:1, lanes] = jnp.sum(grad_hidden, axis=0, keepdims=True)
            dh_ref[0, :, lanes] = grad_hidden.astype(BF)
        return carry

    lax.fori_loop(0, units // block, one_block, 0)
    part_ref[0] = (dot_nt(da_ref[0], w1a[...]) + dot_nt(db_ref[0], w1b[...])).astype(BF)


def mid_kernel(
    me_ref, ds_ref, pa_ref, pb_ref, n1_ref, r1_ref, gain_ref, wo0, wo1,
    dsb_ref, vec_ref, do_own_ref, do_oth_ref, near_ref, scr,
):
    chip = me_ref[0] // 2
    width = do_own_ref.shape[1]
    grad = ds_ref[0] + (pa_ref[0].astype(F32) + pb_ref[0].astype(F32))
    normed = n1_ref[0]
    inner = ln_back(grad, normed, r1_ref[0, :, 0:1], gain_ref[0:1, :])
    vec_ref[0, 0:1, :] = jnp.sum(grad * normed, axis=0, keepdims=True)
    vec_ref[0, 1:2, :] = jnp.sum(grad, axis=0, keepdims=True)
    vec_ref[0, 2:3, :] = jnp.sum(inner, axis=0, keepdims=True)
    dsb = inner.astype(BF)
    dsb_ref[0] = dsb
    scr[...] = inner
    chip_lanes = pl.ds(pl.multiple_of(chip * 2 * width, 128), 2 * width)
    near_ref[0] = jnp.transpose(scr[:, chip_lanes])
    do_own_ref[0] = jnp.transpose(dot(dsb, wo0[...])).astype(BF)
    do_oth_ref[0] = jnp.transpose(dot(dsb, wo1[...])).astype(BF)


def back_kernel(
    heads, me_ref, p_ref, qkv_ref, do_own_ref, do_oth_ref, w_ref, near_ref,
    lg_ref, dqkv_ref, e0, e1, e2, e3, vec_ref, do_scr, dx_scr, sum_scr,
):
    me = me_ref[0]
    core, chip = lax.rem(me, 2), me // 2
    width, slots = qkv_ref.shape[2], qkv_ref.shape[3]
    half = slots // 2
    size = width // heads
    mine = pl.ds(pl.multiple_of(core * half, half), half)
    other = pl.ds(pl.multiple_of((1 - core) * half, half), half)
    do_scr[:, mine] = do_own_ref[0]
    do_scr[:, other] = do_oth_ref[0]
    scale = 1.0 / (size**0.5)
    def one_head(h, carry):
        feats = pl.ds(pl.multiple_of(h * size, size), size)
        query, key, value = (qkv_ref[0, part, feats, :] for part in range(3))
        out_grad = do_scr[feats, :]
        for block in range(2):
            rows = slice(block * half, (block + 1) * half)
            prob = p_ref[0, h, rows, :].astype(F32)
            grad_prob = dot_tn(do_scr[feats, rows], value)
            weighted = grad_prob * prob
            inner = jnp.sum(weighted, axis=-1, keepdims=True)
            lg_ref[0, h, rows, :] = (weighted - prob * inner).astype(BF)
        grad_query = jnp.transpose(dot_nt(lg_ref[0, h], key)) * scale
        grad_key = dot(query, lg_ref[0, h])
        grad_value = dot(out_grad, p_ref[0, h])
        for number, grad in ((0, grad_query), (1, grad_value)):
            line = jnp.sum(grad, axis=1, keepdims=True)
            sum_scr[number, feats, :] = jnp.broadcast_to(line, (size, 128))
        dqkv_ref[0, feats, :] = grad_query.astype(BF)
        dqkv_ref[0, pl.ds(pl.multiple_of(width + h * size, size), size), :] = grad_key.astype(BF)
        dqkv_ref[0, pl.ds(pl.multiple_of(2 * width + h * size, size), size), :] = grad_value.astype(BF)
        return carry

    lax.fori_loop(0, heads, one_head, 0)
    for number in range(2):
        vec_ref[0, number : number + 1, :] = jnp.transpose(sum_scr[number])[0:1, :]
    dx_scr[...] = dot(w_ref[...], dqkv_ref[0])
    near = pl.ds(pl.multiple_of(chip * 2 * width, width), 2 * width)
    dx_scr[near, mine] = dx_scr[near, mine] + near_ref[0]
    for step, out in enumerate((e0, e1, e2, e3)):
        start = pl.multiple_of(place_of(me, step) * width, width)
        out[0] = dx_scr[pl.ds(start, width), :].astype(BF)


def ffn_grad_kernel(count, bit, me_ref, *rest):
    lefts, rights = rest[:count], rest[count : 2 * count]
    keep_ref, send_ref, scr = rest[2 * count :]
    side = me_ref[2 + bit]
    total = None
    for left, right in zip(lefts, rights):
        a = left[...].reshape(-1, left.shape[-1])
        b = right[...].reshape(-1, right.shape[-1])
        product = dot_tn(a, b)
        total = product if total is None else total + product
    part = keep_ref.shape[0]
    scr[...] = total
    keep_ref[...] = scr[pl.ds(pl.multiple_of(side * part, part), part), :].astype(BF)
    send_ref[...] = scr[pl.ds(pl.multiple_of((1 - side) * part, part), part), :].astype(BF)


def qkv_grad_kernel(count, me_ref, *rest):
    groups = [rest[i * count : (i + 1) * count] for i in range(6)]
    small_ref, came_ref, *bqv, keep_ref, send_ref, scr = rest[6 * count :]
    side = me_ref[2]
    width = bqv[0].shape[2]
    line = lax.broadcasted_iota(jnp.int32, small_ref.shape, 0)
    small = small_ref[...]
    scr[:8, :] = jnp.where(line < 6, (small + came_ref[...]) * 0.5, small)
    total = functools.reduce(jnp.add, [b[0] for b in bqv])
    scr[7:8, :width] = total[0:1, :]
    scr[7:8, width : 2 * width] = total[1:2, :]
    halves = as_halves(scr[:8, :])
    total = None
    for x, grad in zip(groups[0], groups[1]):
        for index in range(grad.shape[0]):
            product = dot_nt(grad[index], x[index])
            total = product if total is None else total + product
    used = total.shape[0]
    scr[:used, :] = total
    total = None
    for lefts, rights in ((groups[2], groups[3]), (groups[4], groups[5])):
        for left, right in zip(lefts, rights):
            for index in range(left.shape[0]):
                product = dot(left[index], right[index])
                total = product if total is None else total + product
    scr[used:, :] = total
    part = scr.shape[0] // 2
    for out, half in ((keep_ref, side), (send_ref, 1 - side)):
        place = pl.ds(pl.multiple_of(half * part, part), part)
        out[:part, :] = scr[place, :].astype(BF)
        out[part:, :] = halves


def halve_kernel(bit, tail, me_ref, *rest):
    count = (len(rest) - 2) // 2
    keep_ref, send_ref = rest[-2:]
    side = me_ref[2 + bit]
    rows = (rest[0].shape[0] - tail) // 2
    for number in range(count):
        kept, came = rest[2 * number], rest[2 * number + 1]
        for out, half in ((keep_ref, side), (send_ref, 1 - side)):
            place = pl.ds(pl.multiple_of(half * rows, rows), rows)
            total = kept[place, :].astype(F32) + came[place, :].astype(F32)
            out[number * rows : (number + 1) * rows, :] = total.astype(BF)
    if tail:
        both = as_halves(from_halves(kept[2 * rows :, :]) + from_halves(came[2 * rows :, :]))
        keep_ref[rows:, :] = both
        send_ref[rows:, :] = both


def halve_two_kernel(bits, me_ref, *rest):
    for number, bit in enumerate(bits):
        halve_kernel(bit, 0, me_ref, *rest[2 * number : 2 * number + 2], *rest[4 + 2 * number : 6 + 2 * number])


def last_kernel(me_ref, kept, came, out_ref, small_ref):
    rows = out_ref.shape[0]
    out_ref[...] = (kept[:rows, :].astype(F32) + came[:rows, :].astype(F32)).astype(BF)
    small_ref[...] = from_halves(kept[rows:, :]) + from_halves(came[rows:, :])


def finish_kernel(steps, count, pair, me_ref, *rest):
    blocks, outs = rest[: len(steps)], rest[len(steps) :]
    rows = blocks[0].shape[0]
    for number, back in enumerate(steps):
        group = group_at(me_ref, back, count)
        bits = lax.rem(group, 2), lax.rem(group // 2, 2), group // 4
        index = bits[0] * 4 + bits[1] * 2 + bits[2]
        if pair:
            part = rows // 2
            other = bits[1] * 4 + bits[0] * 2 + bits[2]
            for out, place, low in ((outs[0], index, 0), (outs[1], other, part)):
                place = pl.ds(pl.multiple_of(place * part, part), part)
                out[place, :] = blocks[number][low : low + part, :].astype(F32)
            continue
        block = blocks[number][...].astype(F32)
        before = 0
        for out in outs:
            held = out.shape[0] // rows

            @pl.when((index >= before) & (index < before + held))
            def _():
                out[pl.ds(pl.multiple_of((index - before) * rows, rows), rows), :] = block

            before += held


def late_kernel(pair, me_ref, block_ref, *rest):
    half = (len(rest) - 2) // 2
    outs, scr, sems = rest[half : 2 * half], rest[-2], rest[-1]
    group = group_at(me_ref, 4, 8)
    bits = lax.rem(group, 2), lax.rem(group // 2, 2), group // 4
    index = bits[0] * 4 + bits[1] * 2 + bits[2]
    rows = block_ref.shape[0]
    scr[...] = block_ref[...].astype(F32)
    if pair:
        part = rows // 2
        other = bits[1] * 4 + bits[0] * 2 + bits[2]
        copies = []
        for number, place in enumerate((index, other)):
            place = pl.ds(pl.multiple_of(place * part, part), part)
            source = scr.at[pl.ds(number * part, part), :]
            copies.append(pltpu.make_async_copy(source, outs[number].at[place, :], sems.at[number]))
        for copy in copies:
            copy.start()
        for copy in copies:
            copy.wait()
        return
    before = 0
    for number, out in enumerate(outs):
        held = out.shape[0] // rows

        @pl.when((index >= before) & (index < before + held))
        def _():
            place = pl.ds(pl.multiple_of((index - before) * rows, rows), rows)
            copy = pltpu.make_async_copy(scr, out.at[place, :], sems.at[number])
            copy.start()
            copy.wait()

        before += held


def ring_place(group, groups):
    return jnp.where(lax.rem(group, 2) == 0, group // 2, groups - 1 - group // 2)


def group_at(me_ref, back, count):
    there = lax.rem(ring_place(me_ref[1], count) + count - back, count)
    return jnp.where(there < count // 2, 2 * there, 2 * (count - 1 - there) + 1)


def shard_kernel(me_ref, *rest):
    out_ref = rest[-1]
    low = 0
    for block in rest[:-1]:
        parts = [block[i] for i in range(block.shape[0])] if len(block.shape) == 3 else [block[...]]
        for part in parts:
            out_ref[:, low : low + part.shape[1]] = part.astype(BF)
            low += part.shape[1]


def stack_kernel(me_ref, first, second, out_ref):
    rows = first.shape[0]
    out_ref[:rows, :] = first[...]
    out_ref[rows:, :] = second[...]


def lanes_kernel(me_ref, whole_ref, mine_ref, other_ref):
    core = lax.rem(me_ref[0], 2)
    half = mine_ref.shape[2]
    for out, place in ((mine_ref, core), (other_ref, 1 - core)):
        lanes = pl.ds(pl.multiple_of(place * half, half), half)
        for row in range(out.shape[0]):
            out[row] = whole_ref[row, :, lanes]


def pairs_kernel(me_ref, *rest):
    blocks, outs = rest[:-6], rest[-6:]
    count = len(blocks)
    core = lax.rem(me_ref[0], 2)
    rows = blocks[0].shape[0] // 2
    for number in range(count):
        steps = number if number <= count // 2 else number - count // 2
        ahead = core if number <= count // 2 else 1 - core
        back = jnp.where(ahead == 1, lax.rem(count - steps, count), steps)
        place = pl.ds(pl.multiple_of(group_at(me_ref, back, count) * rows, rows), rows)
        first, second = (outs[:3], outs[3:]) if number <= count // 2 else (outs[3:], outs[:3])
        for part, three in enumerate((first, second)):
            low = 0
            for out in three:
                high = low + out.shape[1]
                out[place, :] = blocks[number][part * rows : (part + 1) * rows, low:high]
                low = high


def small_kernel(me_ref, vec1, vec2, bup_a, bup_b, own_ref, oth_ref):
    own_ref[...] = jnp.zeros_like(own_ref)
    oth_ref[...] = jnp.zeros_like(oth_ref)
    for low, vec in ((0, vec1), (3, vec2)):
        total = jnp.sum(vec[...], axis=0)
        own_ref[low : low + 3, :] = total
        oth_ref[low : low + 3, :] = total
    own_ref[6:7, :] = jnp.sum(bup_a[...], axis=0)
    oth_ref[6:7, :] = jnp.sum(bup_b[...], axis=0)


def as_halves(value):
    high = value.astype(BF).astype(F32)
    return jnp.concatenate([high, value - high], 0).astype(BF)


def from_halves(both):
    both = both.astype(F32)
    return both[:8] + both[8:]


def whole(array):
    shape = array.shape
    return pl.BlockSpec(shape, lambda i, s: (0,) * len(shape))


def held(array):
    return pl.BlockSpec(memory_space=pltpu.VMEM)


def by_row(array, first=0):
    shape = array.shape
    rest = (0,) * (len(shape) - 1)
    return pl.BlockSpec((1,) + shape[1:], lambda i, s: (first + i,) + rest)


def on_row(row, rowed, skip, kernel):
    def inner(*refs):
        kernel(*[
            ref.at[pl.ds(row, 1)] if number in rowed else ref
            for number, ref in enumerate(refs)
            if number not in skip
        ])

    return inner


def call(kernel, grid, ins, outs, out_specs, scratch, name, micros, alias=None, room=32):
    flops = int(micros * 10)
    return pl.pallas_call(
        kernel,
        out_shape=outs,
        grid_spec=pltpu.PrefetchScalarGridSpec(
            num_scalar_prefetch=1,
            grid=grid,
            in_specs=[spec for _, spec in ins[1:]],
            out_specs=out_specs,
            scratch_shapes=scratch,
        ),
        input_output_aliases=alias or {},
        compiler_params=pltpu.CompilerParams(vmem_limit_bytes=room << 20),
        cost_estimate=pl.CostEstimate(flops=flops, bytes_accessed=1, transcendentals=0),
        name=name,
    )(*[a for a, _ in ins])


def body(
    tokens, cotangent, prev_logits, segment_ids, w_qkv, b_qv, w_out, w_up, b_up, w_down,
    biases, gains, shifts,
):
    rows, slots, width = tokens.shape
    full = width * lax.axis_size("tensor")
    groups = lax.axis_size("dp")
    near_dp = groups == 8
    heads = prev_logits.shape[1]
    half = slots // 2
    units = w_up.shape[1]
    me = lax.axis_index("tensor").astype(jnp.int32)
    dp = lax.axis_index("dp").astype(jnp.int32)
    me_ref = jnp.stack([me, dp, lax.rem(dp, 2), lax.rem(dp // 2, 2), dp // 4])
    core = lax.rem(me, 2)
    sds = jax.ShapeDtypeStruct

    def after(value, *others):
        return lax.optimization_barrier((value, others))[0]

    together = lax.optimization_barrier

    def pp(array, step):
        return lax.ppermute(array, "tensor", [(i, i ^ step) for i in range(4)])

    def swap(array, bit):
        return lax.ppermute(array, "dp", [(i, i ^ (1 << bit)) for i in range(groups)])

    order = list(range(0, groups, 2)) + list(range(groups - 1, 0, -2))
    onward = [(order[i], order[(i + 1) % groups]) for i in range(groups)]
    backward = [(b, a) for a, b in onward]

    ring_steps = [0]
    for step in range(1, groups // 2):
        ring_steps += [step, groups - step]
    ring_steps += [groups // 2]

    def ring_step(ahead, behind):
        return lax.ppermute(ahead, "dp", onward), lax.ppermute(behind, "dp", backward)

    def place_pairs(blocks):
        outs = [sds((full, wide), BF) for wide in (2 * units, width, width)] * 2
        return call(
            pairs_kernel, (1,), [(me_ref, None)] + [(b, held(b)) for b in blocks], outs,
            [held(o) for o in outs], [], "pairs", 2, None, 8,
        )

    both_ways = []
    for i, j in onward:
        both_ways += [(i * 4 + t, j * 4 + t) if t % 2 == 0 else (j * 4 + t, i * 4 + t) for t in range(4)]

    def pair_step(pair):
        return lax.ppermute(pair, ("dp", "tensor"), both_ways)

    tokens = jnp.swapaxes(tokens, 1, 2)
    cotangent = jnp.swapaxes(cotangent, 1, 2)
    def joined(kernel, outs, *arrays):
        ins = [(me_ref, None)] + [(a, whole(a)) for a in arrays]
        return call(kernel, (1,), ins, outs, [whole(o) for o in outs], [], "joined", 1, None, 8)

    shard_out = w_out.T.astype(BF)
    if near_dp:
        own = w_up.shape[0]
        shard_in = joined(
            shard_kernel, [sds((own, 3 * width), BF)], jnp.transpose(w_qkv, (1, 0, 2))
        )[0]
        out_y = pp(shard_out, 2)
        x_y = pp(after(tokens, out_y), 2)
        x_c = pp(tokens, 1)
        ring = [ring_step(shard_in, shard_in)]
        ring.append(ring_step(*together(ring[-1])))
        shard_big = joined(
            shard_kernel, [sds((own, 2 * units + 2 * width), BF)], w_up, w_down.T, shard_out, out_y
        )[0]
        ring.append(ring_step(*together(ring[-1])))
        last = lax.ppermute(together(ring[-1])[0], "dp", onward)
        pair_big = joined(
            stack_kernel, [sds((2 * own, 2 * units + 2 * width), BF)], shard_big, pp(shard_big, 1)
        )[0]
        came = [pair_step(after(pair_big, last))]
        pieces_in = [shard_in, *ring[0], *ring[1], *ring[2], last]
        dy_mine, dy_other = joined(
            lanes_kernel, [sds((rows, width, half), BF)] * 2, after(cotangent, x_y)
        )
    else:
        x_y = pp(tokens, 2)
        x_c = pp(tokens, 1)
        shard_in = w_qkv.astype(BF).reshape(w_qkv.shape[0], 3 * width)
        shard_big = jnp.concatenate(
            [w_up.astype(BF), w_down.T.astype(BF), shard_out, pp(shard_out, 2)], 1
        )
        pieces_in = [lax.all_gather(shard_in, "dp", axis=0, tiled=True)]
        big_a = lax.all_gather(shard_big, "dp", axis=0, tiled=True)
        cot = after(cotangent, x_y)
        dy_mine = lax.dynamic_slice_in_dim(cot, core * half, half, 2)
        dy_other = lax.dynamic_slice_in_dim(cot, (1 - core) * half, half, 2)
    x_d = pp(x_y, 1)
    x_pieces = (tokens, x_c, x_y, x_d)
    dy1, dy2, dy3 = pp(dy_other, 1), pp(dy_mine, 2), pp(dy_other, 3)
    b_up_a = b_up.reshape(1, units)
    b_up_b = pp(b_up_a, 1)

    sds3 = lambda *shape_type: sds((rows,) + shape_type[:-1], shape_type[-1])

    class Stage:
        def __init__(self, kernel, fulls, parts, scratch, name, room, far=()):
            self.kernel, self.fulls, self.parts, self.scratch = kernel, fulls, parts, scratch
            self.name, self.room, self.far, self.kept = name, room, far, None

        def step(self, row, given):
            fulls, far = self.fulls, self.far
            ins = [(me_ref, None)]
            ins += [(a, held(a) if isinstance(k, str) else k) for a, k in given]
            rowed = {1 + i for i, (_, k) in enumerate(given) if isinstance(k, str) and k == "row"}
            low, alias = len(ins), {}
            if self.kept is not None:
                alias = {low + i: i for i in range(len(fulls))}
                ins += [
                    (k, pl.BlockSpec(memory_space=pl.ANY) if i in far else held(k))
                    for i, k in enumerate(self.kept)
                ]
            base = len(ins)
            outs = list(fulls) + list(self.parts)
            specs = [by_row(o, row) if i in far else held(o) for i, o in enumerate(fulls)]
            specs += [held(o) for o in self.parts]
            rowed |= {base + i for i in range(len(fulls)) if i not in far}
            result = call(
                on_row(row, rowed, set(alias), self.kernel), (1,), ins, outs, specs,
                self.scratch, self.name, 1, alias, self.room,
            )
            self.kept = result[: len(fulls)]
            return result[len(fulls) :]

    ins = [(me_ref, None)] + [(p, by_row(p)) for p in x_pieces]
    ins += [(b_qv, whole(b_qv)), (prev_logits, by_row(prev_logits))]
    ins += [(segment_ids, whole(segment_ids))] + [(b, held(b)) for b in pieces_in]
    outs = [
        sds(prev_logits.shape, BF),
        sds(prev_logits.shape, BF),
        sds3(3, width, slots, BF),
        sds3(width, half, BF),
        sds3(width, half, BF),
        sds3(full, slots, BF),
        sds3(half, full, BF),
        sds((full, 3 * width), BF),
    ]
    raw, prob, qkv, o_own, o_oth, xt, xh, w_in = call(
        functools.partial(attend_kernel, heads, ring_steps if near_dp else [0]), (rows,), ins,
        outs, [by_row(o) for o in outs[:-1]] + [held(outs[-1])],
        [pltpu.VMEM((width, slots), BF)], "attend", 1, None, 48,
    )
    o1, o2, o3 = pp(o_oth, 1), pp(o_own, 2), pp(o_oth, 3)
    if near_dp:
        came.append(pair_step(after(came[0], o_own, dy1, dy2, dy3)))
        came.append(pair_step(after(came[1], o2)))
        came.append(pair_step(after(came[2], o1, o3)))
        big_a, wo0, wo2, big_b, wo1, wo3 = place_pairs(
            [pair_big, *came, *[pp(b, 1) for b in came[:3]]]
        )
    else:
        big_a = after(big_a, o_own)
        big_b = pp(big_a, 1)
        wo0, wo1 = (b[:, 2 * units : 2 * units + width] for b in (big_a, big_b))
        wo2, wo3 = (b[:, 2 * units + width :] for b in (big_a, big_b))
        big_a, big_b = big_a[:, : 2 * units], big_b[:, : 2 * units]

    one = (1, half, full)
    up = Stage(
        up_kernel,
        [
            sds3(half, full, F32), sds3(half, 128, F32), sds3(half, full, BF),
            sds3(half, units, BF), sds3(half, units, BF), sds3(half, units, BF), sds3(half, units, BF),
        ],
        [sds(one, BF)], [], "up", 16,
    )
    part, part_y = [], []
    for row in range(rows):
        given = [(o, "row") for o in (o_own, o1, o2, o3)]
        given += [(w, "all") for w in (wo0, wo1, wo2, wo3, big_a, big_b)] + [(xh, "row")]
        given += [(w, "all") for w in (biases, gains, shifts, b_up_a, b_up_b)]
        part += up.step(row, given)
        part_y.append(pp(part[row], 2))
    n1, r1, x1, ga, gb, gpa, gpb = up.kept
    gc, x1_c = pp(gb, 1), pp(x1, 1)

    down = Stage(
        down_kernel,
        [
            sds3(width, half, BF), sds3(width, half, BF), sds3(half, full, F32),
            sds3(half, full, BF), sds3(half, units, BF), sds3(half, units, BF),
            sds3(3, full, F32), sds3(1, units, F32), sds3(1, units, F32),
        ],
        [sds(one, BF)], [pltpu.VMEM((full, half), F32)], "down", 16,
    )
    part2, part2_y = [], []
    for row in range(rows):
        got = after(part_y[row], part2_y[0]) if row == 2 else part_y[row]
        given = [(n1, "row"), (part[row], "all"), (got, "all")]
        given += [(d, "row") for d in (dy_mine, dy1, dy2, dy3)]
        given += [(w, "all") for w in (biases, gains, shifts, big_a, big_b)]
        given += [(gpa, "row"), (gpb, "row")]
        part2 += down.step(row, given)
        part2_y.append(pp(part2[row], 2))
    act_own, act_oth, ds2, ds2b, da, db, vec2, bup_a, bup_b = down.kept
    ds2b_c, dc = pp(ds2b, 1), pp(db, 1)

    def ffn_grad(lefts, rights, bit):
        block = 256
        def part(a):
            return pl.BlockSpec(a.shape[:2] + (block,), lambda i, s: (0, 0, i))
        ins = [(me_ref, None)] + [(a, whole(a)) for a in lefts] + [(a, part(a)) for a in rights]
        across, down = rights[0].shape[-1], lefts[0].shape[-1]
        outs = [sds((down // 2, across), BF)] * 2
        specs = [pl.BlockSpec((down // 2, block), lambda i, s: (0, i))] * 2
        return call(
            functools.partial(ffn_grad_kernel, len(lefts), bit),
            (across // block,), ins, outs, specs, [pltpu.VMEM((down, block), F32)], "ffn_grad", 3,
        )

    def halve(bit, *pairs, tail=0):
        down, across = pairs[0][0].shape
        outs = [sds((len(pairs) * (down - tail) // 2 + tail, across), BF)] * 2
        ins = [(me_ref, None)] + [(a, whole(a)) for pair in pairs for a in pair]
        return call(
            functools.partial(halve_kernel, bit, tail), (1,), ins, outs, [whole(o) for o in outs], [],
            "halve", 1,
        )

    def added(keep, got):
        return (keep.astype(F32) + got.astype(F32)).astype(BF)

    def finish(blocks, outs, pair=False, split=False):
        early = blocks[:-1] if split else blocks
        placed = call(
            functools.partial(finish_kernel, ring_steps[: len(early)], groups, pair), (1,),
            [(me_ref, None)] + [(b, whole(b)) for b in early],
            outs, [whole(o) for o in outs], [], "finish", 2,
        )
        return (blocks[-1], outs, pair, placed) if split else placed

    def finish_late(late, outs, pair, placed):
        anywhere = pl.BlockSpec(memory_space=pl.ANY)
        return call(
            functools.partial(late_kernel, pair), (1,),
            [(me_ref, None), (late, whole(late))] + [(p, anywhere) for p in placed],
            outs, [anywhere] * len(outs),
            [pltpu.VMEM(late.shape, F32), pltpu.SemaphoreType.DMA((len(outs),))], "late", 1,
            {2 + i: i for i in range(len(outs))}, 8,
        )

    def whole_of(keep, send, bit):
        low = jnp.where(lax.rem(dp >> bit, 2) == 0, keep, send)
        high = jnp.where(lax.rem(dp >> bit, 2) == 0, send, keep)
        return jnp.concatenate([low, high], 0)

    mid = Stage(
        mid_kernel, [sds3(half, full, BF), sds3(3, full, F32)],
        [sds((1, width, half), BF)] * 2 + [sds((1, 2 * width, half), F32)],
        [pltpu.VMEM((half, full), F32)], "mid", 16,
    )
    back = Stage(
        functools.partial(back_kernel, heads),
        [sds(prev_logits.shape, BF), sds3(3 * width, slots, BF)] + [sds3(width, slots, BF)] * 4,
        [sds((1, 2, width), F32)],
        [pltpu.VMEM((width, slots), BF), pltpu.VMEM((full, slots), F32), pltpu.VMEM((2, width, 128), F32)],
        "back", 32, (0,),
    )

    def mid_step(row, *earlier):
        given = [(ds2, "row"), (part2[row], "all"), (after(part2_y[row], *earlier), "all")]
        given += [(n1, "row"), (r1, "row"), (gains, "all"), (wo0, "all"), (wo1, "all")]
        own, oth, near = mid.step(row, given)
        return own, pp(oth, 1), near

    def back_step(row, held_by, *earlier):
        own, got, near = held_by
        given = [(prob, by_row(prob, row)), (qkv, by_row(qkv, row)), (own, "all")]
        given += [(after(got, *earlier), "all"), (w_in, "all"), (near, "all")]
        return back.step(row, given)[0]

    keep_d, send_d = ffn_grad((ga, gc), (ds2b, ds2b_c), 0)
    mids = [mid_step(0)]
    keep_u, send_u = ffn_grad((x1, x1_c), (da, dc), 1)
    mids.append(mid_step(1, keep_d, keep_u, mids[0][0]))
    sums = [back_step(0, mids[0], mids[1][0]), back_step(1, mids[1])]
    if near_dp:
        got_d, got_u = (swap(after(g, mids[1][0]), b) for g, b in ((send_d, 0), (send_u, 1)))
        mids.append(mid_step(2, sums[1], got_d, got_u))
        ins = (keep_d, after(got_d, mids[2][0]), keep_u, got_u)
        outs = [sds((full // 4, full), BF)] * 4
        keep_d, send_d, keep_u, send_u = call(
            functools.partial(halve_two_kernel, (1, 0)), (1,),
            [(me_ref, None)] + [(a, whole(a)) for a in ins], outs, [whole(o) for o in outs], [],
            "halve", 1,
        )
        got_d, got_u = swap(send_d, 1), swap(send_u, 0)
        sums.append(back_step(2, mids[2], keep_d, keep_u))
    else:
        mids.append(mid_step(2, sums[1]))
        grad_down, grad_up = lax.psum((whole_of(keep_d, send_d, 0), whole_of(keep_u, send_u, 1)), "dp")
        grad_down, grad_up = grad_down.astype(F32), grad_up.astype(F32)
        sums.append(back_step(2, mids[2]))
    ds1b, vec1 = mid.kept
    ds1b_c = pp(ds1b, 1)
    ins = [(me_ref, None)] + [(a, whole(a)) for a in (vec1, vec2, bup_a, bup_b)]
    outs = [sds((8, full), F32)] * 2
    small, other = call(small_kernel, (1,), ins, outs, [whole(o) for o in outs], [], "small", 1)
    small = small + pp(other, 1)
    small_y = pp(small, 2)
    lg, dqkv, e0, e1, e2, e3 = back.kept

    ins = [(me_ref, None)] + [(a, whole(a)) for a in (xt, dqkv, o_own, ds1b, o_oth, ds1b_c)]
    ins += [(a, whole(a)) for a in (small, small_y, *sums)]
    outs = [sds((full // 2 + 16, full), BF)] * 2
    keep, send = call(
        functools.partial(qkv_grad_kernel, 1), (1,), ins, outs, [whole(o) for o in outs],
        [pltpu.VMEM((full, full), F32)], "qkv_grad", 4,
    )

    act_c = pp(act_oth, 1)
    block_out = jnp.concatenate(
        [jnp.where(core == 0, act_own, act_c), jnp.where(core == 0, act_c, act_own)], 2
    )
    near_sum = e2.astype(F32) + pp(e3, 1).astype(F32)
    far = pp(near_sum.astype(BF), 2).astype(F32)
    grad_x = (e0.astype(F32) + pp(e1, 1).astype(F32) + far).astype(BF)
    if near_dp:
        got = swap(send, 0)
        keep_du, send_du = halve(2, (keep_d, after(got_d, send)), (keep_u, got_u))
        got_du = swap(send_du, 2)
        keep, send = halve(1, (keep, got), tail=16)
        got = swap(send, 1)
        pair = after(added(keep_du, got_du), block_out, near_sum)
        ring_u = [ring_step(pair, pair)]
        keep, send = halve(2, (keep, got), tail=16)
        got = swap(send, 2)
        ring_u.append(ring_step(*together(ring_u[-1])))
        outs = [sds((full // 8, full), BF), sds((8, full), F32)]
        total, small = call(
            last_kernel, (1,), [(me_ref, None), (keep, whole(keep)), (got, whole(got))], outs,
            [whole(o) for o in outs], [], "last", 1,
        )
        ring = [ring_step(total, total)]
        ring_u.append(ring_step(*together(ring_u[-1])))
        ring.append(ring_step(*together(ring[-1])))
        last_u = lax.ppermute(ring_u[-1][0], "dp", onward)
        most = finish(
            [after(pair, *ring[1]), *ring_u[0], *ring_u[1], *ring_u[2], last_u],
            [sds((units, full), F32), sds((full, units), F32)], True, True,
        )
        ring.append(ring_step(*together(ring[-1])))
        last = lax.ppermute(after(ring[-1], *most[3])[0], "dp", onward)
        grad_down, grad_up = finish_late(*most)
        grad_in, grad_out = finish(
            [total, *ring[0], *ring[1], *ring[2], last],
            [sds((3 * width, full), F32), sds((width, full), F32)],
        )
    else:
        part = full // 2
        tail = lax.psum(whole_of(keep[:part], send[:part], 0), "dp").astype(F32)
        small = lax.psum(keep[part : part + 8].astype(F32) + keep[part + 8 :].astype(F32), "dp")
        grad_in, grad_out = tail[: 3 * width], tail[3 * width :]
    grad_b_up = small[6]
    grad_b_qv = small[7, : 2 * width].reshape(2, width)

    grad_in = jnp.transpose(grad_in.reshape(3, width, full), (2, 0, 1))

    return (
        jnp.swapaxes(block_out, 1, 2),
        raw,
        jnp.swapaxes(grad_x, 1, 2),
        lg,
        grad_in,
        grad_b_qv,
        grad_out,
        grad_up,
        grad_b_up,
        grad_down,
        jnp.stack([small[2], small[5]]),
        jnp.stack([small[0], small[3]]),
        jnp.stack([small[1], small[4]]),
    )


def solution(mesh):
    placed = (
        P("dp", None, "tensor"),
        P("dp", None, "tensor"),
        P("dp", "tensor", None, None),
        P("dp", None),
        P("dp", None, "tensor"),
        P(None, "tensor"),
        P("tensor", "dp"),
        P("dp", "tensor"),
        P("tensor"),
        P("tensor", "dp"),
        P(),
        P(),
        P(),
    )
    return jax.shard_map(
        body,
        mesh=mesh,
        in_specs=placed,
        out_specs=(
            P("dp", None, "tensor"),
            P("dp", "tensor", None, None),
            P("dp", None, "tensor"),
            P("dp", "tensor", None, None),
            P(None, None, "tensor"),
            P(None, "tensor"),
            P("tensor", None),
            P(None, "tensor"),
            P("tensor"),
            P("tensor", None),
            P(),
            P(),
            P(),
        ),
        check_vma=False,
    )
```

```python
import functools

import jax
import jax.numpy as jnp
from jax import lax
from jax.experimental import pallas as pl
from jax.experimental.pallas import tpu as pltpu
from jax.sharding import PartitionSpec as P

EPS = 1e-06
NEG = -1e30
BF = jnp.bfloat16
F32 = jnp.float32


def dot(a, b):
    return lax.dot_general(a, b, (((1,), (0,)), ((), ())), preferred_element_type=F32)


def dot_nt(a, b):
    return lax.dot_general(a, b, (((1,), (1,)), ((), ())), preferred_element_type=F32)


def dot_tn(a, b):
    return lax.dot_general(a, b, (((0,), (0,)), ((), ())), preferred_element_type=F32)


def place_of(me, step):
    core, chip = lax.rem(me, 2), me // 2
    core = 1 - core if step % 2 else core
    chip = 1 - chip if step // 2 else chip
    return 2 * chip + core


def ln_stats(summed):
    row_mean = jnp.mean(summed, axis=-1, keepdims=True)
    centered = summed - row_mean
    inv_std = lax.rsqrt(jnp.mean(centered * centered, axis=-1, keepdims=True) + EPS)
    return centered * inv_std, inv_std


def ln_back(grad, normed, inv_std, gain):
    scaled = grad * gain
    inner = (
        scaled
        - jnp.mean(scaled, axis=-1, keepdims=True)
        - normed * jnp.mean(scaled * normed, axis=-1, keepdims=True)
    )
    return inner * inv_std


def attend_kernel(
    heads, steps, me_ref, x0, x1, x2, x3, b_ref, prev_ref, seg_ref, *rest
):
    count = len(steps)
    blocks = rest[:count]
    raw_ref, p_ref, qkv_ref, own_ref, oth_ref, xt_ref, xh_ref, w_ref, o_scr = rest[count:]

    @pl.when(pl.program_id(0) == 0)
    def _():
        rows = blocks[0].shape[0]
        for block, back in zip(blocks, steps):
            group = group_at(me_ref, back, count) if count > 1 else 0
            w_ref[pl.ds(pl.multiple_of(group * rows, rows), rows), :] = block[...]

    me = me_ref[0]
    core = lax.rem(me, 2)
    width, slots = x0.shape[1], x0.shape[2]
    half = slots // 2
    size = width // heads
    for step, piece in enumerate((x0, x1, x2, x3)):
        start = pl.multiple_of(place_of(me, step) * width, width)
        xt_ref[0, pl.ds(start, width), :] = piece[0]
    bias = jnp.transpose(jnp.broadcast_to(b_ref[0:1, :], (128, width)))[:, 0:1]
    bias_v = jnp.transpose(jnp.broadcast_to(b_ref[1:2, :], (128, width)))[:, 0:1]
    packed = dot_tn(w_ref[...], xt_ref[0])
    scale = 1.0 / (size**0.5)
    qkv_ref[0, 0] = ((packed[:width] + bias).astype(BF).astype(F32) * scale).astype(BF)
    qkv_ref[0, 1] = packed[width : 2 * width].astype(BF)
    qkv_ref[0, 2] = (packed[2 * width :] + bias_v).astype(BF)
    mine = pl.ds(pl.multiple_of(core * half, half), half)
    other = pl.ds(pl.multiple_of((1 - core) * half, half), half)
    xh_ref[0] = jnp.transpose(xt_ref[0, :, mine])
    row = seg_ref[pl.ds(pl.program_id(0), 1), :].astype(F32)
    column = jnp.transpose(jnp.broadcast_to(row, (128, slots)))[:, 0:1]
    for block in range(2):
        rows = slice(block * half, (block + 1) * half)
        allowed = column[rows] == row
        for h in range(heads):
            feats = slice(h * size, (h + 1) * size)
            scores = dot_tn(qkv_ref[0, 0, feats, rows], qkv_ref[0, 1, feats, :])
            scores = scores + prev_ref[0, h, rows, :].astype(F32)
            raw_ref[0, h, rows, :] = scores.astype(BF)
            masked = jnp.where(allowed, scores, NEG)
            expanded = jnp.exp(masked - jnp.max(masked, axis=-1, keepdims=True))
            prob = expanded * (1.0 / jnp.sum(expanded, axis=-1, keepdims=True))
            prob = prob.astype(BF)
            p_ref[0, h, rows, :] = prob
            heads_out = dot_nt(prob, qkv_ref[0, 2, feats, :])
            o_scr[feats, rows] = jnp.transpose(heads_out).astype(BF)
    own_ref[0] = o_scr[:, mine]
    oth_ref[0] = o_scr[:, other]


def up_kernel(
    me_ref, o0, o1, o2, o3, wo0, wo1, wo2, wo3, big_a, big_b, xh_ref, bias_ref, gain_ref, shift_ref,
    b_up_a, b_up_b,
    n1_ref, r1_ref, x1_ref, ga_ref, gb_ref, gpa_ref, gpb_ref, part_ref,
):
    units = b_up_a.shape[1]
    w1a, w1b = big_a.at[:, :units], big_b.at[:, :units]
    w2a, w2b = big_a.at[:, units : 2 * units], big_b.at[:, units : 2 * units]
    total = xh_ref[0].astype(F32) + bias_ref[0:1, :]
    for left, right in ((o0, wo0), (o1, wo1), (o2, wo2), (o3, wo3)):
        total = total + dot_nt(jnp.transpose(left[0]), right[...])
    normed, inv_std = ln_stats(total)
    n1_ref[0] = normed
    r1_ref[0] = jnp.broadcast_to(inv_std, r1_ref.shape[1:])
    x1_ref[0] = (normed * gain_ref[0:1, :] + shift_ref[0:1, :]).astype(BF)
    block = 256

    def one_block(step, carry):
        lanes = pl.ds(pl.multiple_of(step * block, block), block)
        sides = ((w1a, b_up_a, ga_ref, gpa_ref), (w1b, b_up_b, gb_ref, gpb_ref))
        for w1, b_up, g_ref, gp_ref in sides:
            hidden = dot(x1_ref[0], w1[:, lanes]) + b_up[:, lanes]
            cdf = 0.5 * (1.0 + lax.erf(hidden * (0.5**0.5)))
            pdf = jnp.exp(-0.5 * hidden * hidden) * 0.3989422804014327
            g_ref[0, :, lanes] = (hidden * cdf).astype(BF)
            gp_ref[0, :, lanes] = (cdf + hidden * pdf).astype(BF)
        return carry

    lax.fori_loop(0, units // block, one_block, 0)
    part_ref[0] = (dot_nt(ga_ref[0], w2a[...]) + dot_nt(gb_ref[0], w2b[...])).astype(BF)


def down_kernel(
    me_ref, n1_ref, pa_ref, pb_ref, dy0, dy1, dy2, dy3, bias_ref, gain_ref, shift_ref,
    big_a, big_b, gpa_ref, gpb_ref,
    act_own_ref, act_oth_ref, ds_ref, dsb_ref, da_ref, db_ref, vec_ref, bup_a_ref, bup_b_ref, part_ref,
    scr,
):
    me = me_ref[0]
    width = dy0.shape[1]
    units = gpa_ref.shape[2]
    w1a, w1b = big_a.at[:, :units], big_b.at[:, :units]
    w2a, w2b = big_a.at[:, units : 2 * units], big_b.at[:, units : 2 * units]
    branch = pa_ref[0].astype(F32) + pb_ref[0].astype(F32)
    first_out = n1_ref[0] * gain_ref[0:1, :] + shift_ref[0:1, :]
    normed, inv_std = ln_stats(first_out + branch + bias_ref[1:2, :])
    gain = gain_ref[1:2, :]
    scr[...] = jnp.transpose(normed * gain + shift_ref[1:2, :])
    for step, out in ((0, act_own_ref), (1, act_oth_ref)):
        start = pl.multiple_of(place_of(me, step) * width, width)
        out[0] = scr[pl.ds(start, width), :].astype(BF)
    for step, piece in enumerate((dy0, dy1, dy2, dy3)):
        start = pl.multiple_of(place_of(me, step) * width, width)
        scr[pl.ds(start, width), :] = piece[0].astype(F32)
    grad = jnp.transpose(scr[...])
    inner = ln_back(grad, normed, inv_std, gain)
    ds_ref[0] = inner
    vec_ref[0, 0:1, :] = jnp.sum(grad * normed, axis=0, keepdims=True)
    vec_ref[0, 1:2, :] = jnp.sum(grad, axis=0, keepdims=True)
    vec_ref[0, 2:3, :] = jnp.sum(inner, axis=0, keepdims=True)
    dsb_ref[0] = inner.astype(BF)
    block = 256

    def one_block(step, carry):
        lanes = pl.ds(pl.multiple_of(step * block, block), block)
        sides = ((w2a, da_ref, gpa_ref, bup_a_ref), (w2b, db_ref, gpb_ref, bup_b_ref))
        for w2, dh_ref, gp_ref, bup_ref in sides:
            grad_hidden = dot(dsb_ref[0], w2[:, lanes]) * gp_ref[0, :, lanes].astype(F32)
            bup_ref[0, 0:1, lanes] = jnp.sum(grad_hidden, axis=0, keepdims=True)
            dh_ref[0, :, lanes] = grad_hidden.astype(BF)
        return carry

    lax.fori_loop(0, units // block, one_block, 0)
    part_ref[0] = (dot_nt(da_ref[0], w1a[...]) + dot_nt(db_ref[0], w1b[...])).astype(BF)


def mid_kernel(
    me_ref, ds_ref, pa_ref, pb_ref, n1_ref, r1_ref, gain_ref, wo0, wo1,
    dsb_ref, vec_ref, do_own_ref, do_oth_ref, near_ref, scr,
):
    chip = me_ref[0] // 2
    width = do_own_ref.shape[1]
    grad = ds_ref[0] + (pa_ref[0].astype(F32) + pb_ref[0].astype(F32))
    normed = n1_ref[0]
    inner = ln_back(grad, normed, r1_ref[0, :, 0:1], gain_ref[0:1, :])
    vec_ref[0, 0:1, :] = jnp.sum(grad * normed, axis=0, keepdims=True)
    vec_ref[0, 1:2, :] = jnp.sum(grad, axis=0, keepdims=True)
    vec_ref[0, 2:3, :] = jnp.sum(inner, axis=0, keepdims=True)
    dsb = inner.astype(BF)
    dsb_ref[0] = dsb
    scr[...] = inner
    chip_lanes = pl.ds(pl.multiple_of(chip * 2 * width, 128), 2 * width)
    near_ref[0] = jnp.transpose(scr[:, chip_lanes])
    do_own_ref[0] = jnp.transpose(dot(dsb, wo0[...])).astype(BF)
    do_oth_ref[0] = jnp.transpose(dot(dsb, wo1[...])).astype(BF)


def back_kernel(
    heads, unroll, me_ref, p_ref, qkv_ref, do_own_ref, do_oth_ref, w_ref, near_ref,
    lg_ref, dqkv_ref, e0, e1, e2, e3, vec_ref, do_scr, dx_scr, sum_scr,
):
    me = me_ref[0]
    core, chip = lax.rem(me, 2), me // 2
    width, slots = qkv_ref.shape[2], qkv_ref.shape[3]
    half = slots // 2
    size = width // heads
    mine = pl.ds(pl.multiple_of(core * half, half), half)
    other = pl.ds(pl.multiple_of((1 - core) * half, half), half)
    do_scr[:, mine] = do_own_ref[0]
    do_scr[:, other] = do_oth_ref[0]
    scale = 1.0 / (size**0.5)
    def one_head(h, carry):
        feats = pl.ds(pl.multiple_of(h * size, size), size)
        query, key, value = (qkv_ref[0, part, feats, :] for part in range(3))
        out_grad = do_scr[feats, :]
        for block in range(2):
            rows = slice(block * half, (block + 1) * half)
            prob = p_ref[0, h, rows, :].astype(F32)
            grad_prob = dot_tn(do_scr[feats, rows], value)
            weighted = grad_prob * prob
            inner = jnp.sum(weighted, axis=-1, keepdims=True)
            lg_ref[0, h, rows, :] = (weighted - prob * inner).astype(BF)
        grad_query = jnp.transpose(dot_nt(lg_ref[0, h], key)) * scale
        grad_key = dot(query, lg_ref[0, h])
        grad_value = dot(out_grad, p_ref[0, h])
        for number, grad in ((0, grad_query), (1, grad_value)):
            line = jnp.sum(grad, axis=1, keepdims=True)
            sum_scr[number, feats, :] = jnp.broadcast_to(line, (size, 128))
        dqkv_ref[0, feats, :] = grad_query.astype(BF)
        dqkv_ref[0, pl.ds(pl.multiple_of(width + h * size, size), size), :] = grad_key.astype(BF)
        dqkv_ref[0, pl.ds(pl.multiple_of(2 * width + h * size, size), size), :] = grad_value.astype(BF)
        return carry

    lax.fori_loop(0, heads, one_head, 0, unroll=unroll)
    for number in range(2):
        vec_ref[0, number : number + 1, :] = jnp.transpose(sum_scr[number])[0:1, :]
    dx_scr[...] = dot(w_ref[...], dqkv_ref[0])
    near = pl.ds(pl.multiple_of(chip * 2 * width, width), 2 * width)
    dx_scr[near, mine] = dx_scr[near, mine] + near_ref[0]
    for step, out in enumerate((e0, e1, e2, e3)):
        start = pl.multiple_of(place_of(me, step) * width, width)
        out[0] = dx_scr[pl.ds(start, width), :].astype(BF)


def ffn_grad_kernel(count, bit, me_ref, *rest):
    lefts, rights = rest[:count], rest[count : 2 * count]
    keep_ref, send_ref, scr = rest[2 * count :]
    side = me_ref[2 + bit]
    total = None
    for left, right in zip(lefts, rights):
        a = left[...].reshape(-1, left.shape[-1])
        b = right[...].reshape(-1, right.shape[-1])
        product = dot_tn(a, b)
        total = product if total is None else total + product
    part = keep_ref.shape[0]
    scr[...] = total
    keep_ref[...] = scr[pl.ds(pl.multiple_of(side * part, part), part), :].astype(BF)
    send_ref[...] = scr[pl.ds(pl.multiple_of((1 - side) * part, part), part), :].astype(BF)


def qkv_grad_kernel(count, me_ref, *rest):
    groups = [rest[i * count : (i + 1) * count] for i in range(6)]
    small_ref, came_ref, *bqv, keep_ref, send_ref, scr = rest[6 * count :]
    side = me_ref[2]
    width = bqv[0].shape[2]
    line = lax.broadcasted_iota(jnp.int32, small_ref.shape, 0)
    small = small_ref[...]
    scr[:8, :] = jnp.where(line < 6, (small + came_ref[...]) * 0.5, small)
    total = functools.reduce(jnp.add, [b[0] for b in bqv])
    scr[7:8, :width] = total[0:1, :]
    scr[7:8, width : 2 * width] = total[1:2, :]
    halves = as_halves(scr[:8, :])
    total = None
    for x, grad in zip(groups[0], groups[1]):
        for index in range(grad.shape[0]):
            product = dot_nt(grad[index], x[index])
            total = product if total is None else total + product
    used = total.shape[0]
    scr[:used, :] = total
    total = None
    for lefts, rights in ((groups[2], groups[3]), (groups[4], groups[5])):
        for left, right in zip(lefts, rights):
            for index in range(left.shape[0]):
                product = dot(left[index], right[index])
                total = product if total is None else total + product
    scr[used:, :] = total
    part = scr.shape[0] // 2
    for out, half in ((keep_ref, side), (send_ref, 1 - side)):
        place = pl.ds(pl.multiple_of(half * part, part), part)
        out[:part, :] = scr[place, :].astype(BF)
        out[part:, :] = halves


def halve_kernel(bit, tail, me_ref, *rest):
    count = (len(rest) - 2) // 2
    keep_ref, send_ref = rest[-2:]
    side = me_ref[2 + bit]
    rows = (rest[0].shape[0] - tail) // 2
    for number in range(count):
        kept, came = rest[2 * number], rest[2 * number + 1]
        for out, half in ((keep_ref, side), (send_ref, 1 - side)):
            place = pl.ds(pl.multiple_of(half * rows, rows), rows)
            total = kept[place, :].astype(F32) + came[place, :].astype(F32)
            out[number * rows : (number + 1) * rows, :] = total.astype(BF)
    if tail:
        both = as_halves(from_halves(kept[2 * rows :, :]) + from_halves(came[2 * rows :, :]))
        keep_ref[rows:, :] = both
        send_ref[rows:, :] = both


def halve_two_kernel(bits, me_ref, *rest):
    for number, bit in enumerate(bits):
        halve_kernel(bit, 0, me_ref, *rest[2 * number : 2 * number + 2], *rest[4 + 2 * number : 6 + 2 * number])


def last_kernel(me_ref, kept, came, out_ref, small_ref):
    rows = out_ref.shape[0]
    out_ref[...] = (kept[:rows, :].astype(F32) + came[:rows, :].astype(F32)).astype(BF)
    small_ref[...] = from_halves(kept[rows:, :]) + from_halves(came[rows:, :])


def finish_kernel(steps, count, pair, me_ref, *rest):
    blocks, outs = rest[: len(steps)], rest[len(steps) :]
    rows = blocks[0].shape[0]
    for number, back in enumerate(steps):
        group = group_at(me_ref, back, count)
        bits = lax.rem(group, 2), lax.rem(group // 2, 2), group // 4
        index = bits[0] * 4 + bits[1] * 2 + bits[2]
        if pair:
            part = rows // 2
            other = bits[1] * 4 + bits[0] * 2 + bits[2]
            for out, place, low in ((outs[0], index, 0), (outs[1], other, part)):
                place = pl.ds(pl.multiple_of(place * part, part), part)
                out[place, :] = blocks[number][low : low + part, :].astype(F32)
            continue
        block = blocks[number][...].astype(F32)
        before = 0
        for out in outs:
            held = out.shape[0] // rows

            @pl.when((index >= before) & (index < before + held))
            def _():
                out[pl.ds(pl.multiple_of((index - before) * rows, rows), rows), :] = block

            before += held


def late_kernel(pair, me_ref, block_ref, *rest):
    half = (len(rest) - 2) // 2
    outs, scr, sems = rest[half : 2 * half], rest[-2], rest[-1]
    group = group_at(me_ref, 4, 8)
    bits = lax.rem(group, 2), lax.rem(group // 2, 2), group // 4
    index = bits[0] * 4 + bits[1] * 2 + bits[2]
    rows = block_ref.shape[0]
    scr[...] = block_ref[...].astype(F32)
    if pair:
        part = rows // 2
        other = bits[1] * 4 + bits[0] * 2 + bits[2]
        copies = []
        for number, place in enumerate((index, other)):
            place = pl.ds(pl.multiple_of(place * part, part), part)
            source = scr.at[pl.ds(number * part, part), :]
            copies.append(pltpu.make_async_copy(source, outs[number].at[place, :], sems.at[number]))
        for copy in copies:
            copy.start()
        for copy in copies:
            copy.wait()
        return
    before = 0
    for number, out in enumerate(outs):
        held = out.shape[0] // rows

        @pl.when((index >= before) & (index < before + held))
        def _():
            place = pl.ds(pl.multiple_of((index - before) * rows, rows), rows)
            copy = pltpu.make_async_copy(scr, out.at[place, :], sems.at[number])
            copy.start()
            copy.wait()

        before += held


def ring_place(group, groups):
    return jnp.where(lax.rem(group, 2) == 0, group // 2, groups - 1 - group // 2)


def group_at(me_ref, back, count):
    there = lax.rem(ring_place(me_ref[1], count) + count - back, count)
    return jnp.where(there < count // 2, 2 * there, 2 * (count - 1 - there) + 1)


def shard_kernel(me_ref, *rest):
    out_ref = rest[-1]
    low = 0
    for block in rest[:-1]:
        parts = [block[i] for i in range(block.shape[0])] if len(block.shape) == 3 else [block[...]]
        for part in parts:
            out_ref[:, low : low + part.shape[1]] = part.astype(BF)
            low += part.shape[1]


def stack_kernel(me_ref, first, second, out_ref):
    rows = first.shape[0]
    out_ref[:rows, :] = first[...]
    out_ref[rows:, :] = second[...]


def lanes_kernel(me_ref, whole_ref, mine_ref, other_ref):
    core = lax.rem(me_ref[0], 2)
    half = mine_ref.shape[2]
    for out, place in ((mine_ref, core), (other_ref, 1 - core)):
        lanes = pl.ds(pl.multiple_of(place * half, half), half)
        for row in range(out.shape[0]):
            out[row] = whole_ref[row, :, lanes]


def pairs_kernel(me_ref, *rest):
    blocks, outs = rest[:-6], rest[-6:]
    count = len(blocks)
    core = lax.rem(me_ref[0], 2)
    rows = blocks[0].shape[0] // 2
    for number in range(count):
        steps = number if number <= count // 2 else number - count // 2
        ahead = core if number <= count // 2 else 1 - core
        back = jnp.where(ahead == 1, lax.rem(count - steps, count), steps)
        place = pl.ds(pl.multiple_of(group_at(me_ref, back, count) * rows, rows), rows)
        first, second = (outs[:3], outs[3:]) if number <= count // 2 else (outs[3:], outs[:3])
        for part, three in enumerate((first, second)):
            low = 0
            for out in three:
                high = low + out.shape[1]
                out[place, :] = blocks[number][part * rows : (part + 1) * rows, low:high]
                low = high


def small_kernel(me_ref, vec1, vec2, bup_a, bup_b, own_ref, oth_ref):
    own_ref[...] = jnp.zeros_like(own_ref)
    oth_ref[...] = jnp.zeros_like(oth_ref)
    for low, vec in ((0, vec1), (3, vec2)):
        total = jnp.sum(vec[...], axis=0)
        own_ref[low : low + 3, :] = total
        oth_ref[low : low + 3, :] = total
    own_ref[6:7, :] = jnp.sum(bup_a[...], axis=0)
    oth_ref[6:7, :] = jnp.sum(bup_b[...], axis=0)


def as_halves(value):
    high = value.astype(BF).astype(F32)
    return jnp.concatenate([high, value - high], 0).astype(BF)


def from_halves(both):
    both = both.astype(F32)
    return both[:8] + both[8:]


def whole(array):
    shape = array.shape
    return pl.BlockSpec(shape, lambda i, s: (0,) * len(shape))


def held(array):
    return pl.BlockSpec(memory_space=pltpu.VMEM)


def by_row(array, first=0):
    shape = array.shape
    rest = (0,) * (len(shape) - 1)
    return pl.BlockSpec((1,) + shape[1:], lambda i, s: (first + i,) + rest)


def on_row(row, rowed, skip, kernel):
    def inner(*refs):
        kernel(*[
            ref.at[pl.ds(row, 1)] if number in rowed else ref
            for number, ref in enumerate(refs)
            if number not in skip
        ])

    return inner


def call(kernel, grid, ins, outs, out_specs, scratch, name, micros, alias=None, room=32):
    flops = int(micros * 10)
    return pl.pallas_call(
        kernel,
        out_shape=outs,
        grid_spec=pltpu.PrefetchScalarGridSpec(
            num_scalar_prefetch=1,
            grid=grid,
            in_specs=[spec for _, spec in ins[1:]],
            out_specs=out_specs,
            scratch_shapes=scratch,
        ),
        input_output_aliases=alias or {},
        compiler_params=pltpu.CompilerParams(vmem_limit_bytes=room << 20),
        cost_estimate=pl.CostEstimate(flops=flops, bytes_accessed=1, transcendentals=0),
        name=name,
    )(*[a for a, _ in ins])


def body(
    tokens, cotangent, prev_logits, segment_ids, w_qkv, b_qv, w_out, w_up, b_up, w_down,
    biases, gains, shifts,
):
    rows, slots, width = tokens.shape
    full = width * lax.axis_size("tensor")
    groups = lax.axis_size("dp")
    near_dp = groups == 8
    heads = prev_logits.shape[1]
    half = slots // 2
    units = w_up.shape[1]
    me = lax.axis_index("tensor").astype(jnp.int32)
    dp = lax.axis_index("dp").astype(jnp.int32)
    me_ref = jnp.stack([me, dp, lax.rem(dp, 2), lax.rem(dp // 2, 2), dp // 4])
    core = lax.rem(me, 2)
    sds = jax.ShapeDtypeStruct

    def after(value, *others):
        return lax.optimization_barrier((value, others))[0]

    together = lax.optimization_barrier

    def pp(array, step):
        return lax.ppermute(array, "tensor", [(i, i ^ step) for i in range(4)])

    def swap(array, bit):
        return lax.ppermute(array, "dp", [(i, i ^ (1 << bit)) for i in range(groups)])

    order = list(range(0, groups, 2)) + list(range(groups - 1, 0, -2))
    onward = [(order[i], order[(i + 1) % groups]) for i in range(groups)]
    backward = [(b, a) for a, b in onward]

    ring_steps = [0]
    for step in range(1, groups // 2):
        ring_steps += [step, groups - step]
    ring_steps += [groups // 2]

    def ring_step(ahead, behind):
        return lax.ppermute(ahead, "dp", onward), lax.ppermute(behind, "dp", backward)

    def place_pairs(blocks):
        outs = [sds((full, wide), BF) for wide in (2 * units, width, width)] * 2
        return call(
            pairs_kernel, (1,), [(me_ref, None)] + [(b, held(b)) for b in blocks], outs,
            [held(o) for o in outs], [], "pairs", 2, None, 8,
        )

    both_ways = []
    for i, j in onward:
        both_ways += [(i * 4 + t, j * 4 + t) if t % 2 == 0 else (j * 4 + t, i * 4 + t) for t in range(4)]

    def pair_step(pair):
        return lax.ppermute(pair, ("dp", "tensor"), both_ways)

    tokens = jnp.swapaxes(tokens, 1, 2)
    cotangent = jnp.swapaxes(cotangent, 1, 2)
    def joined(kernel, outs, *arrays):
        ins = [(me_ref, None)] + [(a, whole(a)) for a in arrays]
        return call(kernel, (1,), ins, outs, [whole(o) for o in outs], [], "joined", 1, None, 8)

    shard_out = w_out.T.astype(BF)
    if near_dp:
        own = w_up.shape[0]
        shard_in = joined(
            shard_kernel, [sds((own, 3 * width), BF)], jnp.transpose(w_qkv, (1, 0, 2))
        )[0]
        out_y = pp(shard_out, 2)
        x_y = pp(after(tokens, out_y), 2)
        x_c = pp(tokens, 1)
        ring = [ring_step(shard_in, shard_in)]
        ring.append(ring_step(*together(ring[-1])))
        shard_big = joined(
            shard_kernel, [sds((own, 2 * units + 2 * width), BF)], w_up, w_down.T, shard_out, out_y
        )[0]
        ring.append(ring_step(*together(ring[-1])))
        last = lax.ppermute(together(ring[-1])[0], "dp", onward)
        pair_big = joined(
            stack_kernel, [sds((2 * own, 2 * units + 2 * width), BF)], shard_big, pp(shard_big, 1)
        )[0]
        came = [pair_step(after(pair_big, last))]
        pieces_in = [shard_in, *ring[0], *ring[1], *ring[2], last]
        dy_mine, dy_other = joined(
            lanes_kernel, [sds((rows, width, half), BF)] * 2, after(cotangent, x_y)
        )
    else:
        x_y = pp(tokens, 2)
        x_c = pp(tokens, 1)
        shard_in = w_qkv.astype(BF).reshape(w_qkv.shape[0], 3 * width)
        shard_big = jnp.concatenate(
            [w_up.astype(BF), w_down.T.astype(BF), shard_out, pp(shard_out, 2)], 1
        )
        pieces_in = [lax.all_gather(shard_in, "dp", axis=0, tiled=True)]
        big_a = lax.all_gather(shard_big, "dp", axis=0, tiled=True)
        cot = after(cotangent, x_y)
        dy_mine = lax.dynamic_slice_in_dim(cot, core * half, half, 2)
        dy_other = lax.dynamic_slice_in_dim(cot, (1 - core) * half, half, 2)
    x_d = pp(x_y, 1)
    x_pieces = (tokens, x_c, x_y, x_d)
    dy1, dy2, dy3 = pp(dy_other, 1), pp(dy_mine, 2), pp(dy_other, 3)
    b_up_a = b_up.reshape(1, units)
    b_up_b = pp(b_up_a, 1)

    sds3 = lambda *shape_type: sds((rows,) + shape_type[:-1], shape_type[-1])

    class Stage:
        def __init__(self, kernel, fulls, parts, scratch, name, room, far=()):
            self.kernel, self.fulls, self.parts, self.scratch = kernel, fulls, parts, scratch
            self.name, self.room, self.far, self.kept = name, room, far, None

        def step(self, row, given):
            fulls, far = self.fulls, self.far
            ins = [(me_ref, None)]
            ins += [(a, held(a) if isinstance(k, str) else k) for a, k in given]
            rowed = {1 + i for i, (_, k) in enumerate(given) if isinstance(k, str) and k == "row"}
            low, alias = len(ins), {}
            if self.kept is not None:
                alias = {low + i: i for i in range(len(fulls))}
                ins += [
                    (k, pl.BlockSpec(memory_space=pl.ANY) if i in far else held(k))
                    for i, k in enumerate(self.kept)
                ]
            base = len(ins)
            outs = list(fulls) + list(self.parts)
            specs = [by_row(o, row) if i in far else held(o) for i, o in enumerate(fulls)]
            specs += [held(o) for o in self.parts]
            rowed |= {base + i for i in range(len(fulls)) if i not in far}
            result = call(
                on_row(row, rowed, set(alias), self.kernel), (1,), ins, outs, specs,
                self.scratch, self.name, 1, alias, self.room,
            )
            self.kept = result[: len(fulls)]
            return result[len(fulls) :]

    ins = [(me_ref, None)] + [(p, by_row(p)) for p in x_pieces]
    ins += [(b_qv, whole(b_qv)), (prev_logits, by_row(prev_logits))]
    ins += [(segment_ids, whole(segment_ids))] + [(b, held(b)) for b in pieces_in]
    outs = [
        sds(prev_logits.shape, BF),
        sds(prev_logits.shape, BF),
        sds3(3, width, slots, BF),
        sds3(width, half, BF),
        sds3(width, half, BF),
        sds3(full, slots, BF),
        sds3(half, full, BF),
        sds((full, 3 * width), BF),
    ]
    raw, prob, qkv, o_own, o_oth, xt, xh, w_in = call(
        functools.partial(attend_kernel, heads, ring_steps if near_dp else [0]), (rows,), ins,
        outs, [by_row(o) for o in outs[:-1]] + [held(outs[-1])],
        [pltpu.VMEM((width, slots), BF)], "attend", 1, None, 48,
    )
    o1, o2, o3 = pp(o_oth, 1), pp(o_own, 2), pp(o_oth, 3)
    if near_dp:
        came.append(pair_step(after(came[0], o_own, dy1, dy2, dy3)))
        came.append(pair_step(after(came[1], o2)))
        came.append(pair_step(after(came[2], o1, o3)))
        big_a, wo0, wo2, big_b, wo1, wo3 = place_pairs(
            [pair_big, *came, *[pp(b, 1) for b in came[:3]]]
        )
    else:
        big_a = after(big_a, o_own)
        big_b = pp(big_a, 1)
        wo0, wo1 = (b[:, 2 * units : 2 * units + width] for b in (big_a, big_b))
        wo2, wo3 = (b[:, 2 * units + width :] for b in (big_a, big_b))
        big_a, big_b = big_a[:, : 2 * units], big_b[:, : 2 * units]

    one = (1, half, full)
    up = Stage(
        up_kernel,
        [
            sds3(half, full, F32), sds3(half, 128, F32), sds3(half, full, BF),
            sds3(half, units, BF), sds3(half, units, BF), sds3(half, units, BF), sds3(half, units, BF),
        ],
        [sds(one, BF)], [], "up", 16,
    )
    part, part_y = [], []
    for row in range(rows):
        given = [(o, "row") for o in (o_own, o1, o2, o3)]
        given += [(w, "all") for w in (wo0, wo1, wo2, wo3, big_a, big_b)] + [(xh, "row")]
        given += [(w, "all") for w in (biases, gains, shifts, b_up_a, b_up_b)]
        part += up.step(row, given)
        part_y.append(pp(part[row], 2))
    n1, r1, x1, ga, gb, gpa, gpb = up.kept
    gc, x1_c = pp(gb, 1), pp(x1, 1)

    down = Stage(
        down_kernel,
        [
            sds3(width, half, BF), sds3(width, half, BF), sds3(half, full, F32),
            sds3(half, full, BF), sds3(half, units, BF), sds3(half, units, BF),
            sds3(3, full, F32), sds3(1, units, F32), sds3(1, units, F32),
        ],
        [sds(one, BF)], [pltpu.VMEM((full, half), F32)], "down", 16,
    )
    part2, part2_y = [], []
    for row in range(rows):
        got = after(part_y[row], part2_y[0]) if row == 2 else part_y[row]
        given = [(n1, "row"), (part[row], "all"), (got, "all")]
        given += [(d, "row") for d in (dy_mine, dy1, dy2, dy3)]
        given += [(w, "all") for w in (biases, gains, shifts, big_a, big_b)]
        given += [(gpa, "row"), (gpb, "row")]
        part2 += down.step(row, given)
        part2_y.append(pp(part2[row], 2))
    act_own, act_oth, ds2, ds2b, da, db, vec2, bup_a, bup_b = down.kept
    ds2b_c, dc = pp(ds2b, 1), pp(db, 1)

    def ffn_grad(lefts, rights, bit):
        block = 256
        def part(a):
            return pl.BlockSpec(a.shape[:2] + (block,), lambda i, s: (0, 0, i))
        ins = [(me_ref, None)] + [(a, whole(a)) for a in lefts] + [(a, part(a)) for a in rights]
        across, down = rights[0].shape[-1], lefts[0].shape[-1]
        outs = [sds((down // 2, across), BF)] * 2
        specs = [pl.BlockSpec((down // 2, block), lambda i, s: (0, i))] * 2
        return call(
            functools.partial(ffn_grad_kernel, len(lefts), bit),
            (across // block,), ins, outs, specs, [pltpu.VMEM((down, block), F32)], "ffn_grad", 3,
        )

    def halve(bit, *pairs, tail=0):
        down, across = pairs[0][0].shape
        outs = [sds((len(pairs) * (down - tail) // 2 + tail, across), BF)] * 2
        ins = [(me_ref, None)] + [(a, whole(a)) for pair in pairs for a in pair]
        return call(
            functools.partial(halve_kernel, bit, tail), (1,), ins, outs, [whole(o) for o in outs], [],
            "halve", 1,
        )

    def added(keep, got):
        return (keep.astype(F32) + got.astype(F32)).astype(BF)

    def finish(blocks, outs, pair=False, split=False):
        early = blocks[:-1] if split else blocks
        placed = call(
            functools.partial(finish_kernel, ring_steps[: len(early)], groups, pair), (1,),
            [(me_ref, None)] + [(b, whole(b)) for b in early],
            outs, [whole(o) for o in outs], [], "finish", 2,
        )
        return (blocks[-1], outs, pair, placed) if split else placed

    def finish_late(late, outs, pair, placed):
        anywhere = pl.BlockSpec(memory_space=pl.ANY)
        return call(
            functools.partial(late_kernel, pair), (1,),
            [(me_ref, None), (late, whole(late))] + [(p, anywhere) for p in placed],
            outs, [anywhere] * len(outs),
            [pltpu.VMEM(late.shape, F32), pltpu.SemaphoreType.DMA((len(outs),))], "late", 1,
            {2 + i: i for i in range(len(outs))}, 8,
        )

    def whole_of(keep, send, bit):
        low = jnp.where(lax.rem(dp >> bit, 2) == 0, keep, send)
        high = jnp.where(lax.rem(dp >> bit, 2) == 0, send, keep)
        return jnp.concatenate([low, high], 0)

    mid = Stage(
        mid_kernel, [sds3(half, full, BF), sds3(3, full, F32)],
        [sds((1, width, half), BF)] * 2 + [sds((1, 2 * width, half), F32)],
        [pltpu.VMEM((half, full), F32)], "mid", 16,
    )
    back = Stage(
        functools.partial(back_kernel, heads, False),
        [sds(prev_logits.shape, BF), sds3(3 * width, slots, BF)] + [sds3(width, slots, BF)] * 4,
        [sds((1, 2, width), F32)],
        [pltpu.VMEM((width, slots), BF), pltpu.VMEM((full, slots), F32), pltpu.VMEM((2, width, 128), F32)],
        "back", 32, (0,),
    )

    def mid_step(row, *earlier):
        given = [(ds2, "row"), (part2[row], "all"), (after(part2_y[row], *earlier), "all")]
        given += [(n1, "row"), (r1, "row"), (gains, "all"), (wo0, "all"), (wo1, "all")]
        own, oth, near = mid.step(row, given)
        return own, pp(oth, 1), near

    def back_step(row, held_by, *earlier):
        own, got, near = held_by
        given = [(prob, by_row(prob, row)), (qkv, by_row(qkv, row)), (own, "all")]
        given += [(after(got, *earlier), "all"), (w_in, "all"), (near, "all")]
        return back.step(row, given)[0]

    keep_d, send_d = ffn_grad((ga, gc), (ds2b, ds2b_c), 0)
    mids = [mid_step(0)]
    keep_u, send_u = ffn_grad((x1, x1_c), (da, dc), 1)
    mids.append(mid_step(1, keep_d, keep_u, mids[0][0]))
    sums = [back_step(0, mids[0], mids[1][0]), back_step(1, mids[1])]
    if near_dp:
        got_d, got_u = (swap(after(g, mids[1][0]), b) for g, b in ((send_d, 0), (send_u, 1)))
        mids.append(mid_step(2, sums[1], got_d, got_u))
        ins = (keep_d, after(got_d, mids[2][0]), keep_u, got_u)
        outs = [sds((full // 4, full), BF)] * 4
        keep_d, send_d, keep_u, send_u = call(
            functools.partial(halve_two_kernel, (1, 0)), (1,),
            [(me_ref, None)] + [(a, whole(a)) for a in ins], outs, [whole(o) for o in outs], [],
            "halve", 1,
        )
        got_d, got_u = swap(send_d, 1), swap(send_u, 0)
        back.kernel = functools.partial(back_kernel, heads, True)
        sums.append(back_step(2, mids[2], keep_d, keep_u))
    else:
        mids.append(mid_step(2, sums[1]))
        grad_down, grad_up = lax.psum((whole_of(keep_d, send_d, 0), whole_of(keep_u, send_u, 1)), "dp")
        grad_down, grad_up = grad_down.astype(F32), grad_up.astype(F32)
        sums.append(back_step(2, mids[2]))
    ds1b, vec1 = mid.kept
    ds1b_c = pp(ds1b, 1)
    ins = [(me_ref, None)] + [(a, whole(a)) for a in (vec1, vec2, bup_a, bup_b)]
    outs = [sds((8, full), F32)] * 2
    small, other = call(small_kernel, (1,), ins, outs, [whole(o) for o in outs], [], "small", 1)
    small = small + pp(other, 1)
    small_y = pp(small, 2)
    lg, dqkv, e0, e1, e2, e3 = back.kept

    ins = [(me_ref, None)] + [(a, whole(a)) for a in (xt, dqkv, o_own, ds1b, o_oth, ds1b_c)]
    ins += [(a, whole(a)) for a in (small, small_y, *sums)]
    outs = [sds((full // 2 + 16, full), BF)] * 2
    keep, send = call(
        functools.partial(qkv_grad_kernel, 1), (1,), ins, outs, [whole(o) for o in outs],
        [pltpu.VMEM((full, full), F32)], "qkv_grad", 4,
    )

    act_c = pp(act_oth, 1)
    block_out = jnp.concatenate(
        [jnp.where(core == 0, act_own, act_c), jnp.where(core == 0, act_c, act_own)], 2
    )
    near_sum = e2.astype(F32) + pp(e3, 1).astype(F32)
    far = pp(near_sum.astype(BF), 2).astype(F32)
    grad_x = (e0.astype(F32) + pp(e1, 1).astype(F32) + far).astype(BF)
    if near_dp:
        got = swap(send, 0)
        keep_du, send_du = halve(2, (keep_d, after(got_d, send)), (keep_u, got_u))
        got_du = swap(send_du, 2)
        keep, send = halve(1, (keep, got), tail=16)
        got = swap(send, 1)
        pair = after(added(keep_du, got_du), block_out, near_sum)
        ring_u = [ring_step(pair, pair)]
        keep, send = halve(2, (keep, got), tail=16)
        got = swap(send, 2)
        ring_u.append(ring_step(*together(ring_u[-1])))
        outs = [sds((full // 8, full), BF), sds((8, full), F32)]
        total, small = call(
            last_kernel, (1,), [(me_ref, None), (keep, whole(keep)), (got, whole(got))], outs,
            [whole(o) for o in outs], [], "last", 1,
        )
        ring = [ring_step(total, total)]
        ring_u.append(ring_step(*together(ring_u[-1])))
        ring.append(ring_step(*ring[-1]))
        last_u = lax.ppermute(ring_u[-1][0], "dp", onward)
        most = finish(
            [after(pair, *ring[1]), *ring_u[0], *ring_u[1], *ring_u[2], last_u],
            [sds((units, full), F32), sds((full, units), F32)], True, True,
        )
        ring.append(ring_step(*ring[-1]))
        last = lax.ppermute(after(ring[-1], *most[3])[0], "dp", onward)
        grad_down, grad_up = finish_late(*most)
        grad_in, grad_out = finish(
            [total, *ring[0], *ring[1], *ring[2], last],
            [sds((3 * width, full), F32), sds((width, full), F32)],
        )
    else:
        part = full // 2
        tail = lax.psum(whole_of(keep[:part], send[:part], 0), "dp").astype(F32)
        small = lax.psum(keep[part : part + 8].astype(F32) + keep[part + 8 :].astype(F32), "dp")
        grad_in, grad_out = tail[: 3 * width], tail[3 * width :]
    grad_b_up = small[6]
    grad_b_qv = small[7, : 2 * width].reshape(2, width)

    grad_in = jnp.transpose(grad_in.reshape(3, width, full), (2, 0, 1))

    return (
        jnp.swapaxes(block_out, 1, 2),
        raw,
        jnp.swapaxes(grad_x, 1, 2),
        lg,
        grad_in,
        grad_b_qv,
        grad_out,
        grad_up,
        grad_b_up,
        grad_down,
        jnp.stack([small[2], small[5]]),
        jnp.stack([small[0], small[3]]),
        jnp.stack([small[1], small[4]]),
    )


def solution(mesh):
    placed = (
        P("dp", None, "tensor"),
        P("dp", None, "tensor"),
        P("dp", "tensor", None, None),
        P("dp", None),
        P("dp", None, "tensor"),
        P(None, "tensor"),
        P("tensor", "dp"),
        P("dp", "tensor"),
        P("tensor"),
        P("tensor", "dp"),
        P(),
        P(),
        P(),
    )
    return jax.shard_map(
        body,
        mesh=mesh,
        in_specs=placed,
        out_specs=(
            P("dp", None, "tensor"),
            P("dp", "tensor", None, None),
            P("dp", None, "tensor"),
            P("dp", "tensor", None, None),
            P(None, None, "tensor"),
            P(None, "tensor"),
            P("tensor", None),
            P(None, "tensor"),
            P("tensor"),
            P("tensor", None),
            P(),
            P(),
            P(),
        ),
        check_vma=False,
    )
```

```python
import functools

import jax
import jax.numpy as jnp
from jax import lax
from jax.experimental import pallas as pl
from jax.experimental.pallas import tpu as pltpu
from jax.sharding import PartitionSpec as P

EPS = 1e-06
NEG = -1e30
BF = jnp.bfloat16
F32 = jnp.float32


def dot(a, b):
    return lax.dot_general(a, b, (((1,), (0,)), ((), ())), preferred_element_type=F32)


def dot_nt(a, b):
    return lax.dot_general(a, b, (((1,), (1,)), ((), ())), preferred_element_type=F32)


def dot_tn(a, b):
    return lax.dot_general(a, b, (((0,), (0,)), ((), ())), preferred_element_type=F32)


def place_of(me, step):
    core, chip = lax.rem(me, 2), me // 2
    core = 1 - core if step % 2 else core
    chip = 1 - chip if step // 2 else chip
    return 2 * chip + core


def ln_stats(summed):
    row_mean = jnp.mean(summed, axis=-1, keepdims=True)
    centered = summed - row_mean
    inv_std = lax.rsqrt(jnp.mean(centered * centered, axis=-1, keepdims=True) + EPS)
    return centered * inv_std, inv_std


def ln_back(grad, normed, inv_std, gain):
    scaled = grad * gain
    inner = (
        scaled
        - jnp.mean(scaled, axis=-1, keepdims=True)
        - normed * jnp.mean(scaled * normed, axis=-1, keepdims=True)
    )
    return inner * inv_std


def attend_kernel(
    heads, steps, me_ref, x0, x1, x2, x3, b_ref, prev_ref, seg_ref, *rest
):
    count = len(steps)
    blocks = rest[:count]
    raw_ref, p_ref, qkv_ref, own_ref, oth_ref, xt_ref, xh_ref, w_ref, o_scr = rest[count:]

    @pl.when(pl.program_id(0) == 0)
    def _():
        rows = blocks[0].shape[0]
        for block, back in zip(blocks, steps):
            group = group_at(me_ref, back, count) if count > 1 else 0
            w_ref[pl.ds(pl.multiple_of(group * rows, rows), rows), :] = block[...]

    me = me_ref[0]
    core = lax.rem(me, 2)
    width, slots = x0.shape[1], x0.shape[2]
    half = slots // 2
    size = width // heads
    for step, piece in enumerate((x0, x1, x2, x3)):
        start = pl.multiple_of(place_of(me, step) * width, width)
        xt_ref[0, pl.ds(start, width), :] = piece[0]
    bias = jnp.transpose(jnp.broadcast_to(b_ref[0:1, :], (128, width)))[:, 0:1]
    bias_v = jnp.transpose(jnp.broadcast_to(b_ref[1:2, :], (128, width)))[:, 0:1]
    packed = dot_tn(w_ref[...], xt_ref[0])
    scale = 1.0 / (size**0.5)
    qkv_ref[0, 0] = ((packed[:width] + bias).astype(BF).astype(F32) * scale).astype(BF)
    qkv_ref[0, 1] = packed[width : 2 * width].astype(BF)
    qkv_ref[0, 2] = (packed[2 * width :] + bias_v).astype(BF)
    mine = pl.ds(pl.multiple_of(core * half, half), half)
    other = pl.ds(pl.multiple_of((1 - core) * half, half), half)
    xh_ref[0] = jnp.transpose(xt_ref[0, :, mine])
    row = seg_ref[pl.ds(pl.program_id(0), 1), :].astype(F32)
    column = jnp.transpose(jnp.broadcast_to(row, (128, slots)))[:, 0:1]
    for block in range(2):
        rows = slice(block * half, (block + 1) * half)
        allowed = column[rows] == row
        for h in range(heads):
            feats = slice(h * size, (h + 1) * size)
            scores = dot_tn(qkv_ref[0, 0, feats, rows], qkv_ref[0, 1, feats, :])
            scores = scores + prev_ref[0, h, rows, :].astype(F32)
            raw_ref[0, h, rows, :] = scores.astype(BF)
            masked = jnp.where(allowed, scores, NEG)
            expanded = jnp.exp(masked - jnp.max(masked, axis=-1, keepdims=True))
            prob = expanded * (1.0 / jnp.sum(expanded, axis=-1, keepdims=True))
            prob = prob.astype(BF)
            p_ref[0, h, rows, :] = prob
            heads_out = dot_nt(prob, qkv_ref[0, 2, feats, :])
            o_scr[feats, rows] = jnp.transpose(heads_out).astype(BF)
    own_ref[0] = o_scr[:, mine]
    oth_ref[0] = o_scr[:, other]


def up_kernel(
    me_ref, o0, o1, o2, o3, wo0, wo1, wo2, wo3, big_a, big_b, xh_ref, bias_ref, gain_ref, shift_ref,
    b_up_a, b_up_b,
    n1_ref, r1_ref, x1_ref, ga_ref, gb_ref, gpa_ref, gpb_ref, part_ref,
):
    units = b_up_a.shape[1]
    w1a, w1b = big_a.at[:, :units], big_b.at[:, :units]
    w2a, w2b = big_a.at[:, units : 2 * units], big_b.at[:, units : 2 * units]
    total = xh_ref[0].astype(F32) + bias_ref[0:1, :]
    for left, right in ((o0, wo0), (o1, wo1), (o2, wo2), (o3, wo3)):
        total = total + dot_nt(jnp.transpose(left[0]), right[...])
    normed, inv_std = ln_stats(total)
    n1_ref[0] = normed
    r1_ref[0] = jnp.broadcast_to(inv_std, r1_ref.shape[1:])
    x1_ref[0] = (normed * gain_ref[0:1, :] + shift_ref[0:1, :]).astype(BF)
    block = 256

    def one_block(step, carry):
        lanes = pl.ds(pl.multiple_of(step * block, block), block)
        sides = ((w1a, b_up_a, ga_ref, gpa_ref), (w1b, b_up_b, gb_ref, gpb_ref))
        for w1, b_up, g_ref, gp_ref in sides:
            hidden = dot(x1_ref[0], w1[:, lanes]) + b_up[:, lanes]
            cdf = 0.5 * (1.0 + lax.erf(hidden * (0.5**0.5)))
            pdf = jnp.exp(-0.5 * hidden * hidden) * 0.3989422804014327
            g_ref[0, :, lanes] = (hidden * cdf).astype(BF)
            gp_ref[0, :, lanes] = (cdf + hidden * pdf).astype(BF)
        return carry

    lax.fori_loop(0, units // block, one_block, 0)
    part_ref[0] = (dot_nt(ga_ref[0], w2a[...]) + dot_nt(gb_ref[0], w2b[...])).astype(BF)


def down_kernel(
    unroll, me_ref, n1_ref, pa_ref, pb_ref, dy0, dy1, dy2, dy3, bias_ref, gain_ref, shift_ref,
    big_a, big_b, gpa_ref, gpb_ref,
    act_own_ref, act_oth_ref, ds_ref, dsb_ref, da_ref, db_ref, vec_ref, bup_a_ref, bup_b_ref, part_ref,
    scr,
):
    me = me_ref[0]
    width = dy0.shape[1]
    units = gpa_ref.shape[2]
    w1a, w1b = big_a.at[:, :units], big_b.at[:, :units]
    w2a, w2b = big_a.at[:, units : 2 * units], big_b.at[:, units : 2 * units]
    branch = pa_ref[0].astype(F32) + pb_ref[0].astype(F32)
    first_out = n1_ref[0] * gain_ref[0:1, :] + shift_ref[0:1, :]
    normed, inv_std = ln_stats(first_out + branch + bias_ref[1:2, :])
    gain = gain_ref[1:2, :]
    scr[...] = jnp.transpose(normed * gain + shift_ref[1:2, :])
    for step, out in ((0, act_own_ref), (1, act_oth_ref)):
        start = pl.multiple_of(place_of(me, step) * width, width)
        out[0] = scr[pl.ds(start, width), :].astype(BF)
    for step, piece in enumerate((dy0, dy1, dy2, dy3)):
        start = pl.multiple_of(place_of(me, step) * width, width)
        scr[pl.ds(start, width), :] = piece[0].astype(F32)
    grad = jnp.transpose(scr[...])
    inner = ln_back(grad, normed, inv_std, gain)
    ds_ref[0] = inner
    vec_ref[0, 0:1, :] = jnp.sum(grad * normed, axis=0, keepdims=True)
    vec_ref[0, 1:2, :] = jnp.sum(grad, axis=0, keepdims=True)
    vec_ref[0, 2:3, :] = jnp.sum(inner, axis=0, keepdims=True)
    dsb_ref[0] = inner.astype(BF)
    block = 256

    def one_block(step, carry):
        lanes = pl.ds(pl.multiple_of(step * block, block), block)
        sides = ((w2a, da_ref, gpa_ref, bup_a_ref), (w2b, db_ref, gpb_ref, bup_b_ref))
        for w2, dh_ref, gp_ref, bup_ref in sides:
            grad_hidden = dot(dsb_ref[0], w2[:, lanes]) * gp_ref[0, :, lanes].astype(F32)
            bup_ref[0, 0:1, lanes] = jnp.sum(grad_hidden, axis=0, keepdims=True)
            dh_ref[0, :, lanes] = grad_hidden.astype(BF)
        return carry

    lax.fori_loop(0, units // block, one_block, 0, unroll=unroll)
    part_ref[0] = (dot_nt(da_ref[0], w1a[...]) + dot_nt(db_ref[0], w1b[...])).astype(BF)


def mid_kernel(
    me_ref, ds_ref, pa_ref, pb_ref, n1_ref, r1_ref, gain_ref, wo0, wo1,
    dsb_ref, vec_ref, do_own_ref, do_oth_ref, near_ref, scr,
):
    chip = me_ref[0] // 2
    width = do_own_ref.shape[1]
    grad = ds_ref[0] + (pa_ref[0].astype(F32) + pb_ref[0].astype(F32))
    normed = n1_ref[0]
    inner = ln_back(grad, normed, r1_ref[0, :, 0:1], gain_ref[0:1, :])
    vec_ref[0, 0:1, :] = jnp.sum(grad * normed, axis=0, keepdims=True)
    vec_ref[0, 1:2, :] = jnp.sum(grad, axis=0, keepdims=True)
    vec_ref[0, 2:3, :] = jnp.sum(inner, axis=0, keepdims=True)
    dsb = inner.astype(BF)
    dsb_ref[0] = dsb
    scr[...] = inner
    chip_lanes = pl.ds(pl.multiple_of(chip * 2 * width, 128), 2 * width)
    near_ref[0] = jnp.transpose(scr[:, chip_lanes])
    do_own_ref[0] = jnp.transpose(dot(dsb, wo0[...])).astype(BF)
    do_oth_ref[0] = jnp.transpose(dot(dsb, wo1[...])).astype(BF)


def back_kernel(
    heads, unroll, me_ref, p_ref, qkv_ref, do_own_ref, do_oth_ref, w_ref, near_ref,
    lg_ref, dqkv_ref, e0, e1, e2, e3, vec_ref, do_scr, dx_scr, sum_scr,
):
    me = me_ref[0]
    core, chip = lax.rem(me, 2), me // 2
    width, slots = qkv_ref.shape[2], qkv_ref.shape[3]
    half = slots // 2
    size = width // heads
    mine = pl.ds(pl.multiple_of(core * half, half), half)
    other = pl.ds(pl.multiple_of((1 - core) * half, half), half)
    do_scr[:, mine] = do_own_ref[0]
    do_scr[:, other] = do_oth_ref[0]
    scale = 1.0 / (size**0.5)
    def one_head(h, carry):
        feats = pl.ds(pl.multiple_of(h * size, size), size)
        query, key, value = (qkv_ref[0, part, feats, :] for part in range(3))
        out_grad = do_scr[feats, :]
        for block in range(2):
            rows = slice(block * half, (block + 1) * half)
            prob = p_ref[0, h, rows, :].astype(F32)
            grad_prob = dot_tn(do_scr[feats, rows], value)
            weighted = grad_prob * prob
            inner = jnp.sum(weighted, axis=-1, keepdims=True)
            lg_ref[0, h, rows, :] = (weighted - prob * inner).astype(BF)
        grad_query = jnp.transpose(dot_nt(lg_ref[0, h], key)) * scale
        grad_key = dot(query, lg_ref[0, h])
        grad_value = dot(out_grad, p_ref[0, h])
        for number, grad in ((0, grad_query), (1, grad_value)):
            line = jnp.sum(grad, axis=1, keepdims=True)
            sum_scr[number, feats, :] = jnp.broadcast_to(line, (size, 128))
        dqkv_ref[0, feats, :] = grad_query.astype(BF)
        dqkv_ref[0, pl.ds(pl.multiple_of(width + h * size, size), size), :] = grad_key.astype(BF)
        dqkv_ref[0, pl.ds(pl.multiple_of(2 * width + h * size, size), size), :] = grad_value.astype(BF)
        return carry

    lax.fori_loop(0, heads, one_head, 0, unroll=unroll)
    for number in range(2):
        vec_ref[0, number : number + 1, :] = jnp.transpose(sum_scr[number])[0:1, :]
    dx_scr[...] = dot(w_ref[...], dqkv_ref[0])
    near = pl.ds(pl.multiple_of(chip * 2 * width, width), 2 * width)
    dx_scr[near, mine] = dx_scr[near, mine] + near_ref[0]
    for step, out in enumerate((e0, e1, e2, e3)):
        start = pl.multiple_of(place_of(me, step) * width, width)
        out[0] = dx_scr[pl.ds(start, width), :].astype(BF)


def ffn_grad_kernel(count, bit, me_ref, *rest):
    lefts, rights = rest[:count], rest[count : 2 * count]
    keep_ref, send_ref, scr = rest[2 * count :]
    side = me_ref[2 + bit]
    total = None
    for left, right in zip(lefts, rights):
        a = left[...].reshape(-1, left.shape[-1])
        b = right[...].reshape(-1, right.shape[-1])
        product = dot_tn(a, b)
        total = product if total is None else total + product
    part = keep_ref.shape[0]
    scr[...] = total
    keep_ref[...] = scr[pl.ds(pl.multiple_of(side * part, part), part), :].astype(BF)
    send_ref[...] = scr[pl.ds(pl.multiple_of((1 - side) * part, part), part), :].astype(BF)


def qkv_grad_kernel(count, me_ref, *rest):
    groups = [rest[i * count : (i + 1) * count] for i in range(6)]
    small_ref, came_ref, *bqv, keep_ref, send_ref, scr = rest[6 * count :]
    side = me_ref[2]
    width = bqv[0].shape[2]
    line = lax.broadcasted_iota(jnp.int32, small_ref.shape, 0)
    small = small_ref[...]
    scr[:8, :] = jnp.where(line < 6, (small + came_ref[...]) * 0.5, small)
    total = functools.reduce(jnp.add, [b[0] for b in bqv])
    scr[7:8, :width] = total[0:1, :]
    scr[7:8, width : 2 * width] = total[1:2, :]
    halves = as_halves(scr[:8, :])
    total = None
    for x, grad in zip(groups[0], groups[1]):
        for index in range(grad.shape[0]):
            product = dot_nt(grad[index], x[index])
            total = product if total is None else total + product
    used = total.shape[0]
    scr[:used, :] = total
    total = None
    for lefts, rights in ((groups[2], groups[3]), (groups[4], groups[5])):
        for left, right in zip(lefts, rights):
            for index in range(left.shape[0]):
                product = dot(left[index], right[index])
                total = product if total is None else total + product
    scr[used:, :] = total
    part = scr.shape[0] // 2
    for out, half in ((keep_ref, side), (send_ref, 1 - side)):
        place = pl.ds(pl.multiple_of(half * part, part), part)
        out[:part, :] = scr[place, :].astype(BF)
        out[part:, :] = halves


def halve_kernel(bit, tail, me_ref, *rest):
    count = (len(rest) - 2) // 2
    keep_ref, send_ref = rest[-2:]
    side = me_ref[2 + bit]
    rows = (rest[0].shape[0] - tail) // 2
    for number in range(count):
        kept, came = rest[2 * number], rest[2 * number + 1]
        for out, half in ((keep_ref, side), (send_ref, 1 - side)):
            place = pl.ds(pl.multiple_of(half * rows, rows), rows)
            total = kept[place, :].astype(F32) + came[place, :].astype(F32)
            out[number * rows : (number + 1) * rows, :] = total.astype(BF)
    if tail:
        both = as_halves(from_halves(kept[2 * rows :, :]) + from_halves(came[2 * rows :, :]))
        keep_ref[rows:, :] = both
        send_ref[rows:, :] = both


def halve_two_kernel(bits, me_ref, *rest):
    for number, bit in enumerate(bits):
        halve_kernel(bit, 0, me_ref, *rest[2 * number : 2 * number + 2], *rest[4 + 2 * number : 6 + 2 * number])


def last_kernel(me_ref, kept, came, out_ref, small_ref):
    rows = out_ref.shape[0]
    out_ref[...] = (kept[:rows, :].astype(F32) + came[:rows, :].astype(F32)).astype(BF)
    small_ref[...] = from_halves(kept[rows:, :]) + from_halves(came[rows:, :])


def finish_kernel(steps, count, pair, me_ref, *rest):
    blocks, outs = rest[: len(steps)], rest[len(steps) :]
    rows = blocks[0].shape[0]
    for number, back in enumerate(steps):
        group = group_at(me_ref, back, count)
        bits = lax.rem(group, 2), lax.rem(group // 2, 2), group // 4
        index = bits[0] * 4 + bits[1] * 2 + bits[2]
        if pair:
            part = rows // 2
            other = bits[1] * 4 + bits[0] * 2 + bits[2]
            for out, place, low in ((outs[0], index, 0), (outs[1], other, part)):
                place = pl.ds(pl.multiple_of(place * part, part), part)
                out[place, :] = blocks[number][low : low + part, :].astype(F32)
            continue
        block = blocks[number][...].astype(F32)
        before = 0
        for out in outs:
            held = out.shape[0] // rows

            @pl.when((index >= before) & (index < before + held))
            def _():
                out[pl.ds(pl.multiple_of((index - before) * rows, rows), rows), :] = block

            before += held


def late_kernel(pair, me_ref, block_ref, *rest):
    half = (len(rest) - 2) // 2
    outs, scr, sems = rest[half : 2 * half], rest[-2], rest[-1]
    group = group_at(me_ref, 4, 8)
    bits = lax.rem(group, 2), lax.rem(group // 2, 2), group // 4
    index = bits[0] * 4 + bits[1] * 2 + bits[2]
    rows = block_ref.shape[0]
    scr[...] = block_ref[...].astype(F32)
    if pair:
        part = rows // 2
        other = bits[1] * 4 + bits[0] * 2 + bits[2]
        copies = []
        for number, place in enumerate((index, other)):
            place = pl.ds(pl.multiple_of(place * part, part), part)
            source = scr.at[pl.ds(number * part, part), :]
            copies.append(pltpu.make_async_copy(source, outs[number].at[place, :], sems.at[number]))
        for copy in copies:
            copy.start()
        for copy in copies:
            copy.wait()
        return
    before = 0
    for number, out in enumerate(outs):
        held = out.shape[0] // rows

        @pl.when((index >= before) & (index < before + held))
        def _():
            place = pl.ds(pl.multiple_of((index - before) * rows, rows), rows)
            copy = pltpu.make_async_copy(scr, out.at[place, :], sems.at[number])
            copy.start()
            copy.wait()

        before += held


def ring_place(group, groups):
    return jnp.where(lax.rem(group, 2) == 0, group // 2, groups - 1 - group // 2)


def group_at(me_ref, back, count):
    there = lax.rem(ring_place(me_ref[1], count) + count - back, count)
    return jnp.where(there < count // 2, 2 * there, 2 * (count - 1 - there) + 1)


def shard_kernel(me_ref, *rest):
    out_ref = rest[-1]
    low = 0
    for block in rest[:-1]:
        parts = [block[i] for i in range(block.shape[0])] if len(block.shape) == 3 else [block[...]]
        for part in parts:
            out_ref[:, low : low + part.shape[1]] = part.astype(BF)
            low += part.shape[1]


def stack_kernel(me_ref, first, second, out_ref):
    rows = first.shape[0]
    out_ref[:rows, :] = first[...]
    out_ref[rows:, :] = second[...]


def lanes_kernel(me_ref, whole_ref, mine_ref, other_ref):
    core = lax.rem(me_ref[0], 2)
    half = mine_ref.shape[2]
    for out, place in ((mine_ref, core), (other_ref, 1 - core)):
        lanes = pl.ds(pl.multiple_of(place * half, half), half)
        for row in range(out.shape[0]):
            out[row] = whole_ref[row, :, lanes]


def pairs_kernel(me_ref, *rest):
    blocks, outs = rest[:-6], rest[-6:]
    count = len(blocks)
    core = lax.rem(me_ref[0], 2)
    rows = blocks[0].shape[0] // 2
    for number in range(count):
        steps = number if number <= count // 2 else number - count // 2
        ahead = core if number <= count // 2 else 1 - core
        back = jnp.where(ahead == 1, lax.rem(count - steps, count), steps)
        place = pl.ds(pl.multiple_of(group_at(me_ref, back, count) * rows, rows), rows)
        first, second = (outs[:3], outs[3:]) if number <= count // 2 else (outs[3:], outs[:3])
        for part, three in enumerate((first, second)):
            low = 0
            for out in three:
                high = low + out.shape[1]
                out[place, :] = blocks[number][part * rows : (part + 1) * rows, low:high]
                low = high


def small_kernel(me_ref, vec1, vec2, bup_a, bup_b, own_ref, oth_ref):
    own_ref[...] = jnp.zeros_like(own_ref)
    oth_ref[...] = jnp.zeros_like(oth_ref)
    for low, vec in ((0, vec1), (3, vec2)):
        total = jnp.sum(vec[...], axis=0)
        own_ref[low : low + 3, :] = total
        oth_ref[low : low + 3, :] = total
    own_ref[6:7, :] = jnp.sum(bup_a[...], axis=0)
    oth_ref[6:7, :] = jnp.sum(bup_b[...], axis=0)


def as_halves(value):
    high = value.astype(BF).astype(F32)
    return jnp.concatenate([high, value - high], 0).astype(BF)


def from_halves(both):
    both = both.astype(F32)
    return both[:8] + both[8:]


def whole(array):
    shape = array.shape
    return pl.BlockSpec(shape, lambda i, s: (0,) * len(shape))


def held(array):
    return pl.BlockSpec(memory_space=pltpu.VMEM)


def by_row(array, first=0):
    shape = array.shape
    rest = (0,) * (len(shape) - 1)
    return pl.BlockSpec((1,) + shape[1:], lambda i, s: (first + i,) + rest)


def on_row(row, rowed, skip, kernel):
    def inner(*refs):
        kernel(*[
            ref.at[pl.ds(row, 1)] if number in rowed else ref
            for number, ref in enumerate(refs)
            if number not in skip
        ])

    return inner


def call(kernel, grid, ins, outs, out_specs, scratch, name, micros, alias=None, room=32):
    flops = int(micros * 10)
    return pl.pallas_call(
        kernel,
        out_shape=outs,
        grid_spec=pltpu.PrefetchScalarGridSpec(
            num_scalar_prefetch=1,
            grid=grid,
            in_specs=[spec for _, spec in ins[1:]],
            out_specs=out_specs,
            scratch_shapes=scratch,
        ),
        input_output_aliases=alias or {},
        compiler_params=pltpu.CompilerParams(vmem_limit_bytes=room << 20),
        cost_estimate=pl.CostEstimate(flops=flops, bytes_accessed=1, transcendentals=0),
        name=name,
    )(*[a for a, _ in ins])


def body(
    tokens, cotangent, prev_logits, segment_ids, w_qkv, b_qv, w_out, w_up, b_up, w_down,
    biases, gains, shifts,
):
    rows, slots, width = tokens.shape
    full = width * lax.axis_size("tensor")
    groups = lax.axis_size("dp")
    near_dp = groups == 8
    heads = prev_logits.shape[1]
    half = slots // 2
    units = w_up.shape[1]
    me = lax.axis_index("tensor").astype(jnp.int32)
    dp = lax.axis_index("dp").astype(jnp.int32)
    me_ref = jnp.stack([me, dp, lax.rem(dp, 2), lax.rem(dp // 2, 2), dp // 4])
    core = lax.rem(me, 2)
    sds = jax.ShapeDtypeStruct

    def after(value, *others):
        return lax.optimization_barrier((value, others))[0]

    together = lax.optimization_barrier

    def pp(array, step):
        return lax.ppermute(array, "tensor", [(i, i ^ step) for i in range(4)])

    def swap(array, bit):
        return lax.ppermute(array, "dp", [(i, i ^ (1 << bit)) for i in range(groups)])

    order = list(range(0, groups, 2)) + list(range(groups - 1, 0, -2))
    onward = [(order[i], order[(i + 1) % groups]) for i in range(groups)]
    backward = [(b, a) for a, b in onward]

    ring_steps = [0]
    for step in range(1, groups // 2):
        ring_steps += [step, groups - step]
    ring_steps += [groups // 2]

    def ring_step(ahead, behind):
        return lax.ppermute(ahead, "dp", onward), lax.ppermute(behind, "dp", backward)

    def place_pairs(blocks):
        outs = [sds((full, wide), BF) for wide in (2 * units, width, width)] * 2
        return call(
            pairs_kernel, (1,), [(me_ref, None)] + [(b, held(b)) for b in blocks], outs,
            [held(o) for o in outs], [], "pairs", 2, None, 8,
        )

    both_ways = []
    for i, j in onward:
        both_ways += [(i * 4 + t, j * 4 + t) if t % 2 == 0 else (j * 4 + t, i * 4 + t) for t in range(4)]

    def pair_step(pair):
        return lax.ppermute(pair, ("dp", "tensor"), both_ways)

    tokens = jnp.swapaxes(tokens, 1, 2)
    cotangent = jnp.swapaxes(cotangent, 1, 2)
    def joined(kernel, outs, *arrays):
        ins = [(me_ref, None)] + [(a, whole(a)) for a in arrays]
        return call(kernel, (1,), ins, outs, [whole(o) for o in outs], [], "joined", 1, None, 8)

    shard_out = w_out.T.astype(BF)
    if near_dp:
        own = w_up.shape[0]
        shard_in = joined(
            shard_kernel, [sds((own, 3 * width), BF)], jnp.transpose(w_qkv, (1, 0, 2))
        )[0]
        out_y = pp(shard_out, 2)
        x_y = pp(after(tokens, out_y), 2)
        x_c = pp(tokens, 1)
        ring = [ring_step(shard_in, shard_in)]
        ring.append(ring_step(*together(ring[-1])))
        shard_big = joined(
            shard_kernel, [sds((own, 2 * units + 2 * width), BF)], w_up, w_down.T, shard_out, out_y
        )[0]
        ring.append(ring_step(*together(ring[-1])))
        last = lax.ppermute(together(ring[-1])[0], "dp", onward)
        pair_big = joined(
            stack_kernel, [sds((2 * own, 2 * units + 2 * width), BF)], shard_big, pp(shard_big, 1)
        )[0]
        came = [pair_step(after(pair_big, last))]
        pieces_in = [shard_in, *ring[0], *ring[1], *ring[2], last]
        dy_mine, dy_other = joined(
            lanes_kernel, [sds((rows, width, half), BF)] * 2, after(cotangent, x_y)
        )
    else:
        x_y = pp(tokens, 2)
        x_c = pp(tokens, 1)
        shard_in = w_qkv.astype(BF).reshape(w_qkv.shape[0], 3 * width)
        shard_big = jnp.concatenate(
            [w_up.astype(BF), w_down.T.astype(BF), shard_out, pp(shard_out, 2)], 1
        )
        pieces_in = [lax.all_gather(shard_in, "dp", axis=0, tiled=True)]
        big_a = lax.all_gather(shard_big, "dp", axis=0, tiled=True)
        cot = after(cotangent, x_y)
        dy_mine = lax.dynamic_slice_in_dim(cot, core * half, half, 2)
        dy_other = lax.dynamic_slice_in_dim(cot, (1 - core) * half, half, 2)
    x_d = pp(x_y, 1)
    x_pieces = (tokens, x_c, x_y, x_d)
    dy1, dy2, dy3 = pp(dy_other, 1), pp(dy_mine, 2), pp(dy_other, 3)
    b_up_a = b_up.reshape(1, units)
    b_up_b = pp(b_up_a, 1)

    sds3 = lambda *shape_type: sds((rows,) + shape_type[:-1], shape_type[-1])

    class Stage:
        def __init__(self, kernel, fulls, parts, scratch, name, room, far=()):
            self.kernel, self.fulls, self.parts, self.scratch = kernel, fulls, parts, scratch
            self.name, self.room, self.far, self.kept = name, room, far, None

        def step(self, row, given):
            fulls, far = self.fulls, self.far
            ins = [(me_ref, None)]
            ins += [(a, held(a) if isinstance(k, str) else k) for a, k in given]
            rowed = {1 + i for i, (_, k) in enumerate(given) if isinstance(k, str) and k == "row"}
            low, alias = len(ins), {}
            if self.kept is not None:
                alias = {low + i: i for i in range(len(fulls))}
                ins += [
                    (k, pl.BlockSpec(memory_space=pl.ANY) if i in far else held(k))
                    for i, k in enumerate(self.kept)
                ]
            base = len(ins)
            outs = list(fulls) + list(self.parts)
            specs = [by_row(o, row) if i in far else held(o) for i, o in enumerate(fulls)]
            specs += [held(o) for o in self.parts]
            rowed |= {base + i for i in range(len(fulls)) if i not in far}
            result = call(
                on_row(row, rowed, set(alias), self.kernel), (1,), ins, outs, specs,
                self.scratch, self.name, 1, alias, self.room,
            )
            self.kept = result[: len(fulls)]
            return result[len(fulls) :]

    ins = [(me_ref, None)] + [(p, by_row(p)) for p in x_pieces]
    ins += [(b_qv, whole(b_qv)), (prev_logits, by_row(prev_logits))]
    ins += [(segment_ids, whole(segment_ids))] + [(b, held(b)) for b in pieces_in]
    outs = [
        sds(prev_logits.shape, BF),
        sds(prev_logits.shape, BF),
        sds3(3, width, slots, BF),
        sds3(width, half, BF),
        sds3(width, half, BF),
        sds3(full, slots, BF),
        sds3(half, full, BF),
        sds((full, 3 * width), BF),
    ]
    raw, prob, qkv, o_own, o_oth, xt, xh, w_in = call(
        functools.partial(attend_kernel, heads, ring_steps if near_dp else [0]), (rows,), ins,
        outs, [by_row(o) for o in outs[:-1]] + [held(outs[-1])],
        [pltpu.VMEM((width, slots), BF)], "attend", 1, None, 48,
    )
    o1, o2, o3 = pp(o_oth, 1), pp(o_own, 2), pp(o_oth, 3)
    if near_dp:
        came.append(pair_step(after(came[0], o_own, dy1, dy2, dy3)))
        came.append(pair_step(after(came[1], o2)))
        came.append(pair_step(after(came[2], o1, o3)))
        big_a, wo0, wo2, big_b, wo1, wo3 = place_pairs(
            [pair_big, *came, *[pp(b, 1) for b in came[:3]]]
        )
    else:
        big_a = after(big_a, o_own)
        big_b = pp(big_a, 1)
        wo0, wo1 = (b[:, 2 * units : 2 * units + width] for b in (big_a, big_b))
        wo2, wo3 = (b[:, 2 * units + width :] for b in (big_a, big_b))
        big_a, big_b = big_a[:, : 2 * units], big_b[:, : 2 * units]

    one = (1, half, full)
    up = Stage(
        up_kernel,
        [
            sds3(half, full, F32), sds3(half, 128, F32), sds3(half, full, BF),
            sds3(half, units, BF), sds3(half, units, BF), sds3(half, units, BF), sds3(half, units, BF),
        ],
        [sds(one, BF)], [], "up", 16,
    )
    part, part_y = [], []
    for row in range(rows):
        given = [(o, "row") for o in (o_own, o1, o2, o3)]
        given += [(w, "all") for w in (wo0, wo1, wo2, wo3, big_a, big_b)] + [(xh, "row")]
        given += [(w, "all") for w in (biases, gains, shifts, b_up_a, b_up_b)]
        part += up.step(row, given)
        part_y.append(pp(part[row], 2))
    n1, r1, x1, ga, gb, gpa, gpb = up.kept
    gc, x1_c = pp(gb, 1), pp(x1, 1)

    down = Stage(
        functools.partial(down_kernel, False),
        [
            sds3(width, half, BF), sds3(width, half, BF), sds3(half, full, F32),
            sds3(half, full, BF), sds3(half, units, BF), sds3(half, units, BF),
            sds3(3, full, F32), sds3(1, units, F32), sds3(1, units, F32),
        ],
        [sds(one, BF)], [pltpu.VMEM((full, half), F32)], "down", 16,
    )
    part2, part2_y = [], []
    for row in range(rows):
        got = after(part_y[row], part2_y[0]) if row == 2 else part_y[row]
        if row == rows - 1:
            down.kernel = functools.partial(down_kernel, True)
        given = [(n1, "row"), (part[row], "all"), (got, "all")]
        given += [(d, "row") for d in (dy_mine, dy1, dy2, dy3)]
        given += [(w, "all") for w in (biases, gains, shifts, big_a, big_b)]
        given += [(gpa, "row"), (gpb, "row")]
        part2 += down.step(row, given)
        part2_y.append(pp(part2[row], 2))
    act_own, act_oth, ds2, ds2b, da, db, vec2, bup_a, bup_b = down.kept
    ds2b_c, dc = pp(ds2b, 1), pp(db, 1)

    def ffn_grad(lefts, rights, bit):
        block = 256
        def part(a):
            return pl.BlockSpec(a.shape[:2] + (block,), lambda i, s: (0, 0, i))
        ins = [(me_ref, None)] + [(a, whole(a)) for a in lefts] + [(a, part(a)) for a in rights]
        across, down = rights[0].shape[-1], lefts[0].shape[-1]
        outs = [sds((down // 2, across), BF)] * 2
        specs = [pl.BlockSpec((down // 2, block), lambda i, s: (0, i))] * 2
        return call(
            functools.partial(ffn_grad_kernel, len(lefts), bit),
            (across // block,), ins, outs, specs, [pltpu.VMEM((down, block), F32)], "ffn_grad", 3,
        )

    def halve(bit, *pairs, tail=0):
        down, across = pairs[0][0].shape
        outs = [sds((len(pairs) * (down - tail) // 2 + tail, across), BF)] * 2
        ins = [(me_ref, None)] + [(a, whole(a)) for pair in pairs for a in pair]
        return call(
            functools.partial(halve_kernel, bit, tail), (1,), ins, outs, [whole(o) for o in outs], [],
            "halve", 1,
        )

    def added(keep, got):
        return (keep.astype(F32) + got.astype(F32)).astype(BF)

    def finish(blocks, outs, pair=False, split=False):
        early = blocks[:-1] if split else blocks
        placed = call(
            functools.partial(finish_kernel, ring_steps[: len(early)], groups, pair), (1,),
            [(me_ref, None)] + [(b, whole(b)) for b in early],
            outs, [whole(o) for o in outs], [], "finish", 2,
        )
        return (blocks[-1], outs, pair, placed) if split else placed

    def finish_late(late, outs, pair, placed):
        anywhere = pl.BlockSpec(memory_space=pl.ANY)
        return call(
            functools.partial(late_kernel, pair), (1,),
            [(me_ref, None), (late, whole(late))] + [(p, anywhere) for p in placed],
            outs, [anywhere] * len(outs),
            [pltpu.VMEM(late.shape, F32), pltpu.SemaphoreType.DMA((len(outs),))], "late", 1,
            {2 + i: i for i in range(len(outs))}, 8,
        )

    def whole_of(keep, send, bit):
        low = jnp.where(lax.rem(dp >> bit, 2) == 0, keep, send)
        high = jnp.where(lax.rem(dp >> bit, 2) == 0, send, keep)
        return jnp.concatenate([low, high], 0)

    mid = Stage(
        mid_kernel, [sds3(half, full, BF), sds3(3, full, F32)],
        [sds((1, width, half), BF)] * 2 + [sds((1, 2 * width, half), F32)],
        [pltpu.VMEM((half, full), F32)], "mid", 16,
    )
    back = Stage(
        functools.partial(back_kernel, heads, False),
        [sds(prev_logits.shape, BF), sds3(3 * width, slots, BF)] + [sds3(width, slots, BF)] * 4,
        [sds((1, 2, width), F32)],
        [pltpu.VMEM((width, slots), BF), pltpu.VMEM((full, slots), F32), pltpu.VMEM((2, width, 128), F32)],
        "back", 32, (0,),
    )

    def mid_step(row, *earlier):
        given = [(ds2, "row"), (part2[row], "all"), (after(part2_y[row], *earlier), "all")]
        given += [(n1, "row"), (r1, "row"), (gains, "all"), (wo0, "all"), (wo1, "all")]
        own, oth, near = mid.step(row, given)
        return own, pp(oth, 1), near

    def back_step(row, held_by, *earlier):
        own, got, near = held_by
        given = [(prob, by_row(prob, row)), (qkv, by_row(qkv, row)), (own, "all")]
        given += [(after(got, *earlier), "all"), (w_in, "all"), (near, "all")]
        return back.step(row, given)[0]

    keep_d, send_d = ffn_grad((ga, gc), (ds2b, ds2b_c), 0)
    mids = [mid_step(0)]
    keep_u, send_u = ffn_grad((x1, x1_c), (da, dc), 1)
    mids.append(mid_step(1, keep_d, keep_u, mids[0][0]))
    sums = [back_step(0, mids[0], mids[1][0]), back_step(1, mids[1])]
    if near_dp:
        got_d, got_u = (swap(after(g, mids[1][0]), b) for g, b in ((send_d, 0), (send_u, 1)))
        mids.append(mid_step(2, sums[1], got_d, got_u))
        ins = (keep_d, after(got_d, mids[2][0]), keep_u, got_u)
        outs = [sds((full // 4, full), BF)] * 4
        keep_d, send_d, keep_u, send_u = call(
            functools.partial(halve_two_kernel, (1, 0)), (1,),
            [(me_ref, None)] + [(a, whole(a)) for a in ins], outs, [whole(o) for o in outs], [],
            "halve", 1,
        )
        got_d, got_u = swap(send_d, 1), swap(send_u, 0)
        back.kernel = functools.partial(back_kernel, heads, True)
        sums.append(back_step(2, mids[2], keep_d, keep_u))
    else:
        mids.append(mid_step(2, sums[1]))
        grad_down, grad_up = lax.psum((whole_of(keep_d, send_d, 0), whole_of(keep_u, send_u, 1)), "dp")
        grad_down, grad_up = grad_down.astype(F32), grad_up.astype(F32)
        sums.append(back_step(2, mids[2]))
    ds1b, vec1 = mid.kept
    ds1b_c = pp(ds1b, 1)
    ins = [(me_ref, None)] + [(a, whole(a)) for a in (vec1, vec2, bup_a, bup_b)]
    outs = [sds((8, full), F32)] * 2
    small, other = call(small_kernel, (1,), ins, outs, [whole(o) for o in outs], [], "small", 1)
    small = small + pp(other, 1)
    small_y = pp(small, 2)
    lg, dqkv, e0, e1, e2, e3 = back.kept

    ins = [(me_ref, None)] + [(a, whole(a)) for a in (xt, dqkv, o_own, ds1b, o_oth, ds1b_c)]
    ins += [(a, whole(a)) for a in (small, small_y, *sums)]
    outs = [sds((full // 2 + 16, full), BF)] * 2
    keep, send = call(
        functools.partial(qkv_grad_kernel, 1), (1,), ins, outs, [whole(o) for o in outs],
        [pltpu.VMEM((full, full), F32)], "qkv_grad", 4,
    )

    act_c = pp(act_oth, 1)
    block_out = jnp.concatenate(
        [jnp.where(core == 0, act_own, act_c), jnp.where(core == 0, act_c, act_own)], 2
    )
    near_sum = e2.astype(F32) + pp(e3, 1).astype(F32)
    far = pp(near_sum.astype(BF), 2).astype(F32)
    grad_x = (e0.astype(F32) + pp(e1, 1).astype(F32) + far).astype(BF)
    if near_dp:
        got = swap(send, 0)
        keep_du, send_du = halve(2, (keep_d, after(got_d, send)), (keep_u, got_u))
        got_du = swap(send_du, 2)
        keep, send = halve(1, (keep, got), tail=16)
        got = swap(send, 1)
        pair = after(added(keep_du, got_du), block_out, near_sum)
        ring_u = [ring_step(pair, pair)]
        keep, send = halve(2, (keep, got), tail=16)
        got = swap(send, 2)
        ring_u.append(ring_step(*together(ring_u[-1])))
        outs = [sds((full // 8, full), BF), sds((8, full), F32)]
        total, small = call(
            last_kernel, (1,), [(me_ref, None), (keep, whole(keep)), (got, whole(got))], outs,
            [whole(o) for o in outs], [], "last", 1,
        )
        ring = [ring_step(total, total)]
        ring_u.append(ring_step(*together(ring_u[-1])))
        ring.append(ring_step(*ring[-1]))
        last_u = lax.ppermute(ring_u[-1][0], "dp", onward)
        most = finish(
            [after(pair, *ring[1]), *ring_u[0], *ring_u[1], *ring_u[2], last_u],
            [sds((units, full), F32), sds((full, units), F32)], True, True,
        )
        ring.append(ring_step(*ring[-1]))
        last = lax.ppermute(after(ring[-1], *most[3])[0], "dp", onward)
        grad_down, grad_up = finish_late(*most)
        grad_in, grad_out = finish(
            [total, *ring[0], *ring[1], *ring[2], last],
            [sds((3 * width, full), F32), sds((width, full), F32)],
        )
    else:
        part = full // 2
        tail = lax.psum(whole_of(keep[:part], send[:part], 0), "dp").astype(F32)
        small = lax.psum(keep[part : part + 8].astype(F32) + keep[part + 8 :].astype(F32), "dp")
        grad_in, grad_out = tail[: 3 * width], tail[3 * width :]
    grad_b_up = small[6]
    grad_b_qv = small[7, : 2 * width].reshape(2, width)

    grad_in = jnp.transpose(grad_in.reshape(3, width, full), (2, 0, 1))

    return (
        jnp.swapaxes(block_out, 1, 2),
        raw,
        jnp.swapaxes(grad_x, 1, 2),
        lg,
        grad_in,
        grad_b_qv,
        grad_out,
        grad_up,
        grad_b_up,
        grad_down,
        jnp.stack([small[2], small[5]]),
        jnp.stack([small[0], small[3]]),
        jnp.stack([small[1], small[4]]),
    )


def solution(mesh):
    placed = (
        P("dp", None, "tensor"),
        P("dp", None, "tensor"),
        P("dp", "tensor", None, None),
        P("dp", None),
        P("dp", None, "tensor"),
        P(None, "tensor"),
        P("tensor", "dp"),
        P("dp", "tensor"),
        P("tensor"),
        P("tensor", "dp"),
        P(),
        P(),
        P(),
    )
    return jax.shard_map(
        body,
        mesh=mesh,
        in_specs=placed,
        out_specs=(
            P("dp", None, "tensor"),
            P("dp", "tensor", None, None),
            P("dp", None, "tensor"),
            P("dp", "tensor", None, None),
            P(None, None, "tensor"),
            P(None, "tensor"),
            P("tensor", None),
            P(None, "tensor"),
            P("tensor"),
            P("tensor", None),
            P(),
            P(),
            P(),
        ),
        check_vma=False,
    )
```
